32 devices in a mesh: fsdp: 8 (over z, x), seq: 4 (over y, core).
Axes of the slice: x: 2, y: 2, z: 4, core: 2. Of those that a mesh axis runs over, the one named last changes fastest.
Arguments:
- hidden: bfloat16 [4, 8, 1024, 768], P(None, 'fsdp', 'seq'), may hold values from -6 to 6
- cotangent: bfloat16 [4, 8, 1024, 768], P(None, 'fsdp', 'seq'), may hold values from -6 to 6
- segment_ids: int32 [4, 8, 1024], P(None, 'fsdp', 'seq'), may hold values from 0 to 2, as said below
- pad_mask: int32 [4, 8, 1024], P(None, 'fsdp', 'seq'), may hold values from 0 to 1, as said below
- query_weight: bfloat16 [768, 192], P('fsdp'), may hold values from -0.4375 to 0.4375
- key_weight: bfloat16 [768, 192], P('fsdp'), may hold values from -0.4375 to 0.4375
- value_weight: bfloat16 [768, 192], P('fsdp'), may hold values from -0.4375 to 0.4375
- query_bias: bfloat16 [768], P('fsdp'), may hold values from -1.796875 to 1.796875
- value_bias: bfloat16 [768], P('fsdp'), may hold values from -1.796875 to 1.796875
- output_weight: bfloat16 [768, 768], P('fsdp'), may hold values from -1.75 to 1.75
- output_bias: bfloat16 [768], P('fsdp'), may hold values from -1.796875 to 1.796875
- attn_gain: bfloat16 [768], P('fsdp'), may hold values from 0.5 to 1.5
- attn_shift: bfloat16 [768], P('fsdp'), may hold values from -1.796875 to 1.796875
- expand_weight: bfloat16 [3072, 192], P('fsdp'), may hold values from -0.4375 to 0.4375
- expand_bias: bfloat16 [3072], P('fsdp'), may hold values from -1.796875 to 1.796875
- reduce_weight: bfloat16 [768, 768], P('fsdp'), may hold values from -0.21875 to 0.21875
- reduce_bias: bfloat16 [768], P('fsdp'), may hold values from -1.796875 to 1.796875
- ffn_gain: bfloat16 [768], P('fsdp'), may hold values from 0.5 to 1.5
- ffn_shift: bfloat16 [768], P('fsdp'), may hold values from -1.796875 to 1.796875
Outputs:
- layer_out: bfloat16 [4, 8, 1024, 768], P(None, 'fsdp', 'seq')
- grad_hidden: float32 [4, 8, 1024, 768], P(None, 'fsdp', 'seq')
- query_weight_grad: float32 [768, 192], P(('fsdp', 'seq'))
- key_weight_grad: float32 [768, 192], P(('fsdp', 'seq'))
- value_weight_grad: float32 [768, 192], P(('fsdp', 'seq'))
- query_bias_grad: float32 [768], P(('fsdp', 'seq'))
- value_bias_grad: float32 [768], P(('fsdp', 'seq'))
- output_weight_grad: float32 [768, 768], P(('fsdp', 'seq'))
- output_bias_grad: float32 [768], P(('fsdp', 'seq'))
- attn_gain_grad: float32 [768], P(('fsdp', 'seq'))
- attn_shift_grad: float32 [768], P(('fsdp', 'seq'))
- expand_weight_grad: float32 [3072, 192], P(('fsdp', 'seq'))
- expand_bias_grad: float32 [3072], P(('fsdp', 'seq'))
- reduce_weight_grad: float32 [768, 768], P(('fsdp', 'seq'))
- reduce_bias_grad: float32 [768], P(('fsdp', 'seq'))
- ffn_gain_grad: float32 [768], P(('fsdp', 'seq'))
- ffn_shift_grad: float32 [768], P(('fsdp', 'seq'))
The draws below stay inside these ranges and needn't reach their ends.
Inputs may be any that keep to these rules, and one draw needn't show every extreme that they name: `segment_ids`: along each sequence the numbers never fall and begin at 0; each of the 3 documents holds at least 204 positions. `pad_mask`: the pads are the last positions of each sequence, one or more, all inside its last document.
All inputs are finite; a program needn't handle non-finite values.
Results may differ from the reference program's by a relative error of at most 0.012.
The reference program's roundings to bfloat16 on the way count: a program that leaves them out, or rounds other values in their place, can miss the bound.
Values may be sent and summed in bfloat16 or wider, within the bound.
No kernel may reach another device: no remote copies, remote signals or barrier semaphores. Data moves between devices by JAX's collectives and lax.ppermute only.
A program may use at most 128 MiB of HBM per device.

```python
import jax
import jax.numpy as jnp
from jax import lax

D = 768
HEADS = 12
FF = 3072
GROUPS = 4
HEAD = 64
SEQ_LEN = 1024
MICRO = 4
BATCH = 8


def document_layout(key):
    base = jax.random.fold_in(key, 17)
    first_key, second_key, third_key = jax.random.split(base, 3)
    grid_shape = (MICRO, BATCH)
    first_cut = jax.random.randint(first_key, grid_shape, SEQ_LEN // 5, 2 * SEQ_LEN // 5 + 1)
    second_cut = first_cut + jax.random.randint(second_key, grid_shape, SEQ_LEN // 5, 2 * SEQ_LEN // 5 + 1)
    pad_count = jax.random.randint(third_key, grid_shape, 1, SEQ_LEN // 8 + 1)
    positions = jnp.arange(SEQ_LEN, dtype=jnp.int32)
    segments = (positions >= first_cut[..., None]).astype(jnp.int32) + (positions >= second_cut[..., None]).astype(jnp.int32)
    living = (positions < SEQ_LEN - pad_count[..., None]).astype(jnp.int32)
    return (segments, living)


def draw_segment_ids(key, part):
    return document_layout(key)[0]


def draw_pad_mask(key, part):
    return document_layout(key)[1]


def with_spikes(array, own_key, source, target, parts, factor):
    owner, partner = [(jnp.arange(array.shape[axis_at]) // (array.shape[axis_at] // parts)).reshape([-1 if axis == axis_at else 1 for axis in range(array.ndim)]) for axis_at in (source, target)]
    chosen = jax.random.permutation(own_key, parts)[partner]
    strong = (owner == chosen) | (owner == (partner + parts // 2) % parts)
    return jnp.where(strong, factor * array, array)


def level_of(rng, shape, cuts, least, high):
    factor_of = 1.0
    for dim, blocks in cuts:
        steps = jax.random.uniform(jax.random.fold_in(jax.random.fold_in(rng, 6), dim), (blocks,), jnp.float32, least / len(cuts), high / len(cuts))
        factor_of = factor_of * jnp.repeat(jnp.exp(steps), shape[dim] // blocks).reshape((-1,) + (1,) * (len(shape) - 1 - dim))
    return factor_of


def scatter_about(own_key, extent, width, limit, shards=(), held_as=jnp.bfloat16):
    gain = level_of(own_key, extent, shards, -0.22, 0.18) if shards else 1.0
    entries = jax.random.normal(own_key, extent, jnp.float32) * width * gain
    return jnp.minimum(jnp.maximum(entries, -limit), limit).astype(held_as)


def bell_draw_with(key, dims, scale, bound, cuts, heavy, kind=jnp.bfloat16):
    entries = scale * jax.random.normal(key, dims, jnp.float32)
    if cuts:
        entries = entries * level_of(key, dims, cuts, -0.22, 0.18)
    return jnp.clip(with_spikes(entries, jax.random.fold_in(key, 3), *heavy), -bound, bound).astype(kind)


def setup_inputs(seed: int = 0) -> dict:
    streams_of = jax.random.split(jax.random.key(seed), 20)
    hidden = scatter_about(streams_of[0], (MICRO, BATCH, SEQ_LEN, D), 1.0, 6.0, ((1, 8), (2, 4)))
    cotangent = bell_draw_with(streams_of[1], (MICRO, BATCH, SEQ_LEN, D), 1.0, 6.0, ((1, 8), (2, 4)), (1, 3, 8, 2.0))
    segment_ids = draw_segment_ids(jax.random.fold_in(streams_of[19], 71), 0)
    pad_mask = draw_pad_mask(jax.random.fold_in(streams_of[19], 71), 0)
    query_weight = scatter_about(streams_of[4], (D, D // GROUPS), (D // GROUPS) ** -0.5, 0.4375, ((0, 8),))
    key_weight = scatter_about(streams_of[5], (D, D // GROUPS), (D // GROUPS) ** -0.5, 0.4375, ((0, 8),))
    value_weight = scatter_about(streams_of[6], (D, D // GROUPS), (D // GROUPS) ** -0.5, 0.4375, ((0, 8),))
    query_bias = scatter_about(streams_of[7], (D,), 0.3, 1.796875, ((0, 8),))
    value_bias = scatter_about(streams_of[8], (D,), 0.3, 1.796875, ((0, 8),))
    output_weight = scatter_about(streams_of[9], (D, D), (D // 64) ** -0.5, 1.75, ((0, 8),))
    output_bias = scatter_about(streams_of[10], (D,), 0.3, 1.796875, ((0, 8),))
    attn_gain = jnp.clip(1.0 + 0.1 * jax.random.normal(streams_of[11], (D,), jnp.float32), 0.5, 1.5).astype(jnp.bfloat16)
    attn_shift = scatter_about(streams_of[12], (D,), 0.3, 1.796875, ((0, 8),))
    expand_weight = scatter_about(streams_of[13], (FF, D // GROUPS), (D // GROUPS) ** -0.5, 0.4375, ((0, 8),))
    expand_bias = scatter_about(streams_of[14], (FF,), 0.3, 1.796875, ((0, 8),))
    reduce_weight = scatter_about(streams_of[15], (D, FF // GROUPS), (FF // GROUPS) ** -0.5, 0.21875, ((0, 8),))
    reduce_bias = scatter_about(streams_of[16], (D,), 0.3, 1.796875, ((0, 8),))
    ffn_gain = jnp.clip(1.0 + 0.1 * jax.random.normal(streams_of[17], (D,), jnp.float32), 0.5, 1.5).astype(jnp.bfloat16)
    ffn_shift = scatter_about(streams_of[18], (D,), 0.3, 1.796875, ((0, 8),))
    return {"hidden": hidden, "cotangent": cotangent, "segment_ids": segment_ids, "pad_mask": pad_mask, "query_weight": query_weight, "key_weight": key_weight, "value_weight": value_weight, "query_bias": query_bias, "value_bias": value_bias, "output_weight": output_weight, "output_bias": output_bias, "attn_gain": attn_gain, "attn_shift": attn_shift, "expand_weight": expand_weight, "expand_bias": expand_bias, "reduce_weight": reduce_weight, "reduce_bias": reduce_bias, "ffn_gain": ffn_gain, "ffn_shift": ffn_shift}


norm_eps = 1e-05
masked_fill = -1000000000.0
highest = lax.Precision.HIGHEST

@jax.custom_vjp
def low(v):
    return lax.optimization_barrier(v.astype(jnp.bfloat16)).astype(jnp.float32)

@jax.custom_vjp
def low_back(v):
    return v

def low_keep(v):
    return (low(v), None)

def low_pass(kept, grad):
    return (grad,)

def back_keep(v):
    return (v, None)

def back_low(kept, grad):
    return (low(grad),)
low.defvjp(low_keep, low_pass)
low_back.defvjp(back_keep, back_low)

def grouped(inputs, weight):
    leading = inputs.shape[:-1]
    pieces = inputs.reshape(leading + (GROUPS, inputs.shape[-1] // GROUPS))
    kernel = weight.reshape(GROUPS, weight.shape[0] // GROUPS, weight.shape[1])
    result = jnp.einsum('...gj,goj->...go', pieces, kernel, precision=highest)
    return result.reshape(leading + (weight.shape[0],))

def layer_norm(values, norm_gain, norm_shift):
    center = values - lax.optimization_barrier(jnp.mean(values, axis=-1, keepdims=True))
    spread = lax.optimization_barrier(jnp.mean(center * center, axis=-1, keepdims=True))
    return center * lax.rsqrt(spread + norm_eps) * norm_gain + norm_shift

def attend(operands):
    queries, keys_in, values_in, segments, living = operands
    length = queries.shape[0]
    score_scale = HEAD ** (-0.5)
    query_heads = queries.reshape(length, HEADS, HEAD)
    key_heads = keys_in.reshape(length, HEADS, HEAD)
    value_heads = values_in.reshape(length, HEADS, HEAD)
    scores = jnp.einsum('qhd,khd->hqk', query_heads, key_heads, precision=highest) * score_scale
    scores = low_back(scores)
    allowed = (segments[:, None] == segments[None, :]) & (living[None, :] == 1)
    masked = jnp.where(allowed[None], scores, masked_fill)
    row_max = lax.optimization_barrier(jnp.max(masked, axis=-1, keepdims=True))
    powers = jnp.exp(masked - row_max)
    attn_weights = low(powers / lax.optimization_barrier(jnp.sum(powers, axis=-1, keepdims=True)))
    mixture = jnp.einsum('hqk,khd->qhd', attn_weights, value_heads, precision=highest)
    return mixture.reshape(length, HEADS * HEAD)

def forward(params, inputs, segments, living):
    query_weight, key_weight, value_weight, query_bias, value_bias, output_weight, output_bias, attn_gain, attn_shift, expand_weight, expand_bias, reduce_weight, reduce_bias, ffn_gain, ffn_shift = params
    queries = low_back(low(grouped(inputs, query_weight) + query_bias))
    keys_all = low_back(low(grouped(inputs, key_weight)))
    values_all = low_back(low(grouped(inputs, value_weight) + value_bias))
    mixture = lax.map(jax.checkpoint(attend), (queries, keys_all, values_all, segments, living))
    mixture = low_back(low(mixture))
    projected = low_back(jnp.einsum('nli,oi->nlo', mixture, output_weight, precision=highest) + output_bias)
    residual = inputs + projected
    normed = layer_norm(residual, attn_gain, attn_shift)
    pre_act = low_back(grouped(low(normed), expand_weight) + expand_bias)
    activated = low(jax.nn.gelu(pre_act, approximate=False))
    branch = low_back(grouped(activated, reduce_weight) + reduce_bias)
    return layer_norm(normed + branch, ffn_gain, ffn_shift)

def reference(hidden, cotangent, segment_ids, pad_mask, query_weight, key_weight, value_weight, query_bias, value_bias, output_weight, output_bias, attn_gain, attn_shift, expand_weight, expand_bias, reduce_weight, reduce_bias, ffn_gain, ffn_shift):
    params = (query_weight.astype(jnp.float32), key_weight.astype(jnp.float32), value_weight.astype(jnp.float32), query_bias.astype(jnp.float32), value_bias.astype(jnp.float32), output_weight.astype(jnp.float32), output_bias.astype(jnp.float32), attn_gain.astype(jnp.float32), attn_shift.astype(jnp.float32), expand_weight.astype(jnp.float32), expand_bias.astype(jnp.float32), reduce_weight.astype(jnp.float32), reduce_bias.astype(jnp.float32), ffn_gain.astype(jnp.float32), ffn_shift.astype(jnp.float32))
    pairs = MICRO * BATCH // 2
    inputs = hidden.reshape(pairs, 2, SEQ_LEN, D)
    upstream = cotangent.reshape(pairs, 2, SEQ_LEN, D)
    segments = segment_ids.reshape(pairs, 2, SEQ_LEN)
    living = pad_mask.reshape(pairs, 2, SEQ_LEN)

    def step(totals, operands):
        pair_in, pair_ct, pair_seg, pair_live = operands
        result_out, pull = jax.vjp(lambda weights, rows: forward(weights, rows, pair_seg, pair_live), params, pair_in.astype(jnp.float32))
        weight_grads, input_grad = pull(pair_ct.astype(jnp.float32))
        totals = jax.tree.map(lambda before, update: before + update, totals, weight_grads)
        return (totals, (result_out.astype(jnp.bfloat16), input_grad))
    initial = jax.tree.map(jnp.zeros_like, params)
    totals, (outputs, input_grads) = lax.scan(step, initial, (inputs, upstream, segments, living))
    layer_out = outputs.reshape(MICRO, BATCH, SEQ_LEN, D)
    grad_hidden = input_grads.reshape(MICRO, BATCH, SEQ_LEN, D)
    return (layer_out, grad_hidden, totals[0], totals[1], totals[2], totals[3], totals[4], totals[5], totals[6], totals[7], totals[8], totals[9], totals[10], totals[11], totals[12], totals[13], totals[14])
```

```python
import functools

import jax
import jax.numpy as jnp
from jax import lax
from jax.experimental import pallas as pl
from jax.experimental.pallas import tpu as pltpu
from jax.sharding import PartitionSpec as P

GROUPS = 4
HEAD = 64
EPS = 1e-05
LOG2E = 1.4426950408889634
BIG = float(2**30)
BF = jnp.bfloat16
F32 = jnp.float32
NT = (((1,), (1,)), ((), ()))
NN = (((1,), (0,)), ((), ()))
TN = (((0,), (0,)), ((), ()))


def mm(a, b, dims):
    return lax.dot_general(a, b, dims, preferred_element_type=F32)


def split2(v):
    hi = v.astype(BF)
    return hi, (v - hi.astype(F32)).astype(BF)


def split3(v):
    hi = v.astype(BF)
    rest = v - hi.astype(F32)
    mid = rest.astype(BF)
    return hi, mid, (rest - mid.astype(F32)).astype(BF)


def lanes(shape):
    return lax.broadcasted_iota(jnp.int32, shape, 1)


def query_parts(q, low):
    scaled = q.astype(F32) * (LOG2E * HEAD**-0.5)
    hi, lo = split2(scaled)
    hi, lo = hi.astype(F32), lo.astype(F32)
    turned = pltpu.roll(lo, 64, 1)
    return (
        jnp.where(low, hi, turned).astype(BF),
        jnp.where(low, turned, hi).astype(BF),
    )


def key_parts(k, low):
    k = k.astype(F32)
    turned = pltpu.roll(k, 64, 1)
    return (
        jnp.where(low, k, turned).astype(BF),
        jnp.where(low, turned, k).astype(BF),
    )


def square(ref):
    w = ref[...]
    part = w.shape[1]
    zero = jnp.zeros((part, part), w.dtype)
    return jnp.concatenate(
        [jnp.concatenate([w[:part], zero], axis=1), jnp.concatenate([zero, w[part:]], axis=1)], axis=0
    )


def attend_kernel(count, *refs):
    slots, refs = refs[:count], refs[count:]
    wq_ref, wk_ref, wv_ref, qb_ref, vb_ref, row_ref, col_ref, *refs = refs
    x_ref, q_ref, k_ref, v_ref, mix_ref, lse_ref, qaug, kaug, vaug = refs
    length = x_ref.shape[0]
    span = length // count
    for n, slot in enumerate(slots):
        x_ref[span * n : span * n + span, :] = slot[...]
    rows = 256
    x = x_ref[...]
    alive = row_ref[:, 6:7].astype(F32)
    q_ref[...] = ((mm(x, square(wq_ref), NT) + qb_ref[...]) * alive).astype(BF)
    k_ref[...] = mm(x, square(wk_ref), NT).astype(BF)
    v_ref[...] = (mm(x, square(wv_ref), NT) + vb_ref[...]).astype(BF)
    low = lanes((length, 128)) < 64
    for pair in range(x_ref.shape[1] // 128):
        cut = slice(128 * pair, 128 * pair + 128)
        q_parts = query_parts(q_ref[:, cut], low)
        k_parts = key_parts(k_ref[:, cut], low)
        vaug[:, :128] = v_ref[:, cut]
        vaug[:, 128:] = jnp.ones((length, 128), BF)
        for head in range(2):
            qaug[head, :, :128] = q_parts[head]
            qaug[head, :, 128:] = row_ref[...]
            kaug[head, :, :128] = k_parts[head]
            kaug[head, :, 128:] = col_ref[...]

        def block(step, carry):
            at = pl.ds(pl.multiple_of(step * rows, rows), rows)
            found = []
            for head in range(2):
                scores = mm(qaug[head, at, :], kaug[head], NT)
                top = jnp.max(scores, axis=1, keepdims=True)
                powers = jnp.exp2(scores - top).astype(BF)
                both = mm(powers, vaug[...], NN)
                total = both[:, 128:]
                found.append((both[:, :128] / total, top + jnp.log2(total)))
            left = lanes((rows, 128)) < 64
            mix_ref[at, cut] = jnp.where(left, found[0][0], found[1][0]).astype(BF)
            lse_ref[at, cut] = jnp.where(left, found[0][1], found[1][1])
            return carry

        lax.fori_loop(0, length // rows, block, 0)


def attend_forward(which, slots, weights, query_bias, value_bias, row, col):
    span, half = slots[0].shape
    length = span * len(slots)
    slot = pl.BlockSpec((span, half), lambda i: (0, 0))
    weight = [pl.BlockSpec((half, half // 2), lambda i: (which, 0))] * 3
    bias = pl.BlockSpec((1, half), lambda i: (0, which))
    info = pl.BlockSpec((length, 128), lambda i: (0, 0))
    out = pl.BlockSpec((length, half), lambda i: (0, 0))
    return pl.pallas_call(
        functools.partial(attend_kernel, len(slots)),
        grid=(1,),
        in_specs=[*[slot] * len(slots), *weight, bias, bias, info, info],
        out_specs=[out] * 6,
        out_shape=[jax.ShapeDtypeStruct((length, half), BF)] * 5
        + [jax.ShapeDtypeStruct((length, half), F32)],
        scratch_shapes=[
            pltpu.VMEM((2, length, 256), BF),
            pltpu.VMEM((2, length, 256), BF),
            pltpu.VMEM((length, 256), BF),
        ],
        compiler_params=pltpu.CompilerParams(vmem_limit_bytes=56 << 20),
        name="attend_forward",
    )(*slots, *weights, query_bias, value_bias, row, col)


def mean(v):
    return jnp.sum(v, axis=1, keepdims=True) * (1.0 / v.shape[1])


def total(v):
    return jnp.sum(v, axis=0, keepdims=True)


def gelu_parts(x):
    flat = jnp.abs(x) * 0.7071067811865476
    t = 1.0 / (1.0 + 0.3275911 * flat)
    power = jnp.exp(x * x * -0.5)
    poly = t * (0.127414796 + t * (-0.142248368 + t * (0.7107068705 + t * (-0.7265760135 + t * 0.5307027145))))
    tail = poly * power
    return jnp.where(x >= 0, 1.0 - tail, tail), power * 0.3989422804014327


def middle_kernel(
    packed, xa_ref, xb_ref, mixa_ref, mixb_ref, cot0, cot1, cot2, cot3,
    wo_ref, we_ref, wr_ref, bo_ref, g1_ref, s1_ref, be_ref, br_ref, g2_ref, s2_ref,
    out_ref, gres_ref, gmix_ref, dwo_out, dwe_out, dwr_out,
    dbo_ref, dg1_ref, ds1_ref, dbe_ref, dbr_ref, dg2_ref, ds2_ref, slope, dwe_acc, dwo_ref, dwr_ref, cots, sems,
):
    step = pl.program_id(0)
    width = wo_ref.shape[1]
    part = width // GROUPS
    deep = we_ref.shape[0] // GROUPS

    @pl.when(step == 0)
    def _():
        for ref in (dwo_ref, dwr_ref, dbo_ref, dg1_ref, ds1_ref, dbe_ref, dbr_ref, dg2_ref, ds2_ref, dwe_acc):
            ref[...] = jnp.zeros_like(ref)
        for n, ref in enumerate((cot0, cot1, cot2, cot3)):
            pltpu.make_async_copy(ref, cots.at[n], sems.at[n]).start()

    pltpu.make_async_copy(cot0, cots.at[step], sems.at[step]).wait()
    mixed = jnp.concatenate([mixa_ref[...], mixb_ref[...]], axis=1)
    rows_in = jnp.concatenate([xa_ref[...], xb_ref[...]], axis=1)
    residual = rows_in.astype(F32) + mm(mixed, wo_ref[...], NT) + bo_ref[...]
    centred = residual - mean(residual)
    rate1 = lax.rsqrt(mean(centred * centred) + EPS)
    hat1 = centred * rate1
    normed = hat1 * g1_ref[...] + s1_ref[...]
    normed_low = normed.astype(BF)
    acts, branches = [], []
    for g in range(GROUPS):
        piece = normed_low[:, part * g : part * g + part]
        tall = slice(deep * g, deep * g + deep)
        pre = mm(piece, we_ref[tall, :], NT) + be_ref[:, tall]
        upper, density = gelu_parts(pre)
        acts.append((pre * upper).astype(BF))
        slope[:, tall] = upper + pre * density
        branches.append(mm(acts[g], wr_ref[part * g : part * g + part, :], NT))
    second = normed + jnp.concatenate(branches, axis=1) + br_ref[...]
    centred = second - mean(second)
    rate2 = lax.rsqrt(mean(centred * centred) + EPS)
    hat2 = centred * rate2
    out_ref[...] = (hat2 * g2_ref[...] + s2_ref[...]).astype(BF)
    cot = cots[step].astype(F32)
    dg2_ref[...] += total(cot * hat2)
    ds2_ref[...] += total(cot)
    e = cot * g2_ref[...]
    grad_second = rate2 * (e - mean(e) - hat2 * mean(e * hat2))
    grad_branch = grad_second.astype(BF)
    dbr_ref[...] += total(grad_branch.astype(F32))
    backs = []
    for g in range(GROUPS):
        narrow = slice(part * g, part * g + part)
        tall = slice(deep * g, deep * g + deep)
        piece = grad_branch[:, narrow]
        dwr_ref[narrow, :] += mm(piece, acts[g], TN)
        grad_pre = mm(piece, wr_ref[narrow, :], NN) * slope[:, tall]
        grad_pre_low = grad_pre.astype(BF)
        dbe_ref[:, tall] += total(grad_pre_low.astype(F32))
        dwe_acc[g] += mm(normed_low[:, narrow], grad_pre_low, TN)
        backs.append(mm(grad_pre_low, we_ref[tall, :], NN))
    grad_normed = grad_second + jnp.concatenate(backs, axis=1)
    dg1_ref[...] += total(grad_normed * hat1)
    ds1_ref[...] += total(grad_normed)
    e = grad_normed * g1_ref[...]
    grad_residual = rate1 * (e - mean(e) - hat1 * mean(e * hat1))
    gres_ref[...] = grad_residual
    grad_projected = grad_residual.astype(BF)
    dbo_ref[...] += total(grad_projected.astype(F32))
    dwo_ref[...] += mm(grad_projected, mixed, TN)
    gmix_ref[...] = mm(grad_projected, wo_ref[...], NN).astype(BF)

    @pl.when(step == pl.num_programs(0) - 1)
    def _():
        if not packed:
            dwo_out[...] = dwo_ref[...]
            dwr_out[...] = dwr_ref[...]
        for g in range(GROUPS):
            tall = dwe_acc[g].T
            if not packed:
                dwe_out[deep * g : deep * g + deep, :] = tall
                continue
            for n in range(8):
                owner = 8 * g + n
                f, y, c = owner // 4, owner // 2 % 2, owner % 2
                few = slice(24 * owner, 24 * owner + 24)
                dwo_out[c, f, y] = dwo_ref[few, :].astype(BF)
                dwr_out[c, f, y] = dwr_ref[few, :].astype(BF)
                dwe_out[c, f, y] = jnp.concatenate(
                    [tall[96 * n : 96 * n + 48], tall[96 * n + 48 : 96 * n + 96]], axis=1
                ).astype(BF)


def middle(packed, halves, mixed, cots, wo, we, wr, bo, g1, s1, be, br, g2, s2):
    rows, width = cots[0].shape
    length = rows * len(cots)
    deep = we.shape[0]
    tokens = pl.BlockSpec((rows, width), lambda i: (i, 0))
    half = pl.BlockSpec((rows, width // 2), lambda i: (i, 0))

    def fixed(a):
        return pl.BlockSpec(a.shape, lambda i: (0,) * len(a.shape))

    if packed:
        sums = [jax.ShapeDtypeStruct((2, 8, 2, *s), BF) for s in ((24, width), (48, width // 2), (24, width))]
    else:
        sums = [jax.ShapeDtypeStruct(s, F32) for s in (wo.shape, we.shape, wr.shape)]
    sums += [jax.ShapeDtypeStruct((1, n), F32) for n in (width, width, width, deep, width, width, width)]
    return pl.pallas_call(
        functools.partial(middle_kernel, packed),
        grid=(length // rows,),
        in_specs=[half] * 4
        + [pl.BlockSpec(memory_space=pl.ANY)] * 4
        + [fixed(a) for a in (wo, we, wr, bo, g1, s1, be, br, g2, s2)],
        out_specs=[tokens] * 3 + [fixed(a) for a in sums],
        out_shape=[
            jax.ShapeDtypeStruct((length, width), BF),
            jax.ShapeDtypeStruct((length, width), F32),
            jax.ShapeDtypeStruct((length, width), BF),
            *sums,
        ],
        scratch_shapes=[
            pltpu.VMEM((rows, deep), F32),
            pltpu.VMEM((GROUPS, width // GROUPS, deep // GROUPS), F32),
            pltpu.VMEM(wo.shape, F32),
            pltpu.VMEM(wr.shape, F32),
            pltpu.VMEM((len(cots), rows, width), BF),
            pltpu.SemaphoreType.DMA((len(cots),)),
        ],
        compiler_params=pltpu.CompilerParams(vmem_limit_bytes=56 << 20),
        name="middle",
    )(*halves, *mixed, *cots, wo, we, wr, bo, g1, s1, be, br, g2, s2)


def back_kernel(
    packed, x_ref, q_ref, k_ref, v_ref, mix_ref, gmix_ref, lse_ref, gres_ref, wq_ref, wk_ref, wv_ref, row_ref, col_ref,
    ghid_ref, dw_ref, dqb_ref, dvb_ref, qaug, kaug, vaug, gaug, dq_acc, dq, dk, dv,
):
    length = x_ref.shape[0]
    rows = 256
    low = lanes((length, 128)) < 64
    lane = lanes((length, 128))
    alive = row_ref[:, 6:7].astype(F32)
    scale = HEAD**-0.5
    zero = jnp.zeros((length, 128), BF)
    for pair in range(x_ref.shape[1] // 128):
        cut = slice(128 * pair, 128 * pair + 128)
        q_parts = query_parts(q_ref[:, cut], low)
        k_parts = key_parts(k_ref[:, cut], low)
        grad = gmix_ref[:, cut]
        prod = grad.astype(F32) * mix_ref[:, cut].astype(F32)
        lse = lse_ref[:, cut]
        turned = pltpu.roll(lse, 64, 1)
        vaug[:, :128] = v_ref[:, cut]
        vaug[:, 128:] = jnp.ones((length, 128), BF)
        for head in range(2):
            mine = low if head == 0 else ~low
            dot = jnp.sum(jnp.where(mine, prod, 0.0), axis=1, keepdims=True)
            d1, d2, d3 = split3(jnp.broadcast_to(-dot, (length, 128)))
            l1, l2, l3 = split3(-jnp.where(mine, lse, turned))
            qaug[head, :, :128] = q_parts[head]
            qaug[head, :, 128:] = jnp.where(
                lane == 3, l1, jnp.where(lane == 4, l2, jnp.where(lane == 5, l3, row_ref[...]))
            )
            kaug[head, :, :128] = k_parts[head]
            kaug[head, :, 128:] = col_ref[...]
            gaug[head, :, :128] = jnp.where(mine, grad, zero)
            gaug[head, :, 128:] = jnp.where(
                lane == 0, d1, jnp.where(lane == 1, d2, jnp.where(lane == 2, d3, zero))
            )
        dq_acc[...] = jnp.zeros_like(dq_acc)

        def block(step, carry):
            at = pl.ds(pl.multiple_of(step * rows, rows), rows)
            left = lanes((length, 128)) < 64
            near = lanes((rows, 128)) < 64
            d_key = jnp.zeros((rows, 128), F32)
            d_value = jnp.zeros((rows, 128), F32)
            for head in range(2):
                probs = jnp.exp2(mm(kaug[head, at, :], qaug[head], NT))
                slopes = mm(vaug[at, :], gaug[head], NT)
                grads = (probs * slopes).astype(BF)
                d_value += mm(probs.astype(BF), gaug[head, :, :128], NN)
                queries = q_ref[:, cut]
                keys = k_ref[at, cut]
                if head == 0:
                    queries = jnp.where(left, queries, jnp.zeros_like(queries))
                    keys = jnp.where(near, keys, jnp.zeros_like(keys))
                else:
                    queries = jnp.where(left, jnp.zeros_like(queries), queries)
                    keys = jnp.where(near, jnp.zeros_like(keys), keys)
                d_key += mm(grads, queries, NN)
                dq_acc[...] += mm(grads, keys, TN)
            dk[at, cut] = (d_key * scale).astype(BF)
            dv[at, cut] = d_value.astype(BF)
            return carry

        lax.fori_loop(0, length // rows, block, 0)
        dq[:, cut] = (dq_acc[...] * (alive * scale)).astype(BF)
    dqb_ref[...] = total(dq[...].astype(F32))
    dvb_ref[...] = total(dv[...].astype(F32))
    ghid_ref[...] = (
        gres_ref[...]
        + mm(dq[...], square(wq_ref), NN)
        + mm(dk[...], square(wk_ref), NN)
        + mm(dv[...], square(wv_ref), NN)
    ).astype(BF)
    part = x_ref.shape[1] // 2
    sums = []
    for grad in (dq, dk, dv):
        both = mm(grad[...], x_ref[...], TN)
        sums.append((both[:part, :part], both[part:, part:]))
    for g in range(2):
        wide = jnp.concatenate([each[g] for each in sums], axis=1)
        if not packed:
            dw_ref[part * g : part * g + part, :] = wide
            continue
        for n in range(8):
            owner = 8 * g + n
            dw_ref[owner % 2, owner // 4, owner // 2 % 2] = wide[24 * n : 24 * n + 24].astype(BF)


def attend_backward(packed, which, x, q, k, v, mixed, lse, gmix, gres, weights, row, col):
    length, half = x.shape
    wide = pl.BlockSpec((length, half), lambda i: (0, which))
    own = pl.BlockSpec((length, half), lambda i: (0, 0))
    weight = [pl.BlockSpec((half, half // 2), lambda i: (which, 0))] * 3
    info = pl.BlockSpec((length, 128), lambda i: (0, 0))
    line = pl.BlockSpec((1, half), lambda i: (0, 0))
    if packed:
        grads = jax.ShapeDtypeStruct((2, 4, 2, 24, half * 3 // 2), BF)
    else:
        grads = jax.ShapeDtypeStruct((half, half * 3 // 2), F32)
    return pl.pallas_call(
        functools.partial(back_kernel, packed),
        grid=(1,),
        in_specs=[own, own, own, own, own, wide, own, wide, *weight, info, info],
        out_specs=[own, pl.BlockSpec(grads.shape, lambda i: (0,) * len(grads.shape)), line, line],
        out_shape=[jax.ShapeDtypeStruct((length, half), BF), grads]
        + [jax.ShapeDtypeStruct((1, half), F32)] * 2,
        scratch_shapes=[
            pltpu.VMEM((2, length, 256), BF),
            pltpu.VMEM((2, length, 256), BF),
            pltpu.VMEM((length, 256), BF),
            pltpu.VMEM((2, length, 256), BF),
            pltpu.VMEM((length, 128), F32),
            pltpu.VMEM((length, half), BF),
            pltpu.VMEM((length, half), BF),
            pltpu.VMEM((length, half), BF),
        ],
        compiler_params=pltpu.CompilerParams(vmem_limit_bytes=56 << 20),
        name="attend_backward",
    )(x, q, k, v, mixed, gmix, lse, gres, *weights, row, col)


def mask_tables(segments, living):
    ids = jnp.arange(3, dtype=jnp.int32)
    same = segments[:, None] == ids[None, :]
    real = same & (living[:, None] == 1)
    lives = jnp.any(real, axis=0)
    row_hot = (same & lives[None, :]).astype(BF)
    row_alive = jnp.any(same & lives[None, :], axis=1, keepdims=True).astype(BF)
    length = segments.shape[0]
    row = jnp.concatenate(
        [row_hot, jnp.zeros((length, 3), BF), row_alive, jnp.zeros((length, 121), BF)], axis=1
    )
    col = jnp.concatenate(
        [
            jnp.where(real, 0.0, -BIG).astype(BF),
            jnp.ones((length, 3), BF),
            jnp.zeros((length, 122), BF),
        ],
        axis=1,
    )
    return row, col


def turn(v, axis, step, size):
    return lax.ppermute(v, axis, [(i, i ^ step) for i in range(size)])


def pick(v, index):
    return lax.dynamic_index_in_dim(v, index, 0, keepdims=False)


def swap_in(v, seq):
    return [pick(v, seq)] + [turn(pick(v, seq ^ m), "seq", m, 4) for m in range(1, 4)]


def swap_out(slots):
    return [slots[0]] + [turn(slots[m], "seq", m, 4) for m in range(1, 4)]


def in_order(slots, index):
    v = jnp.stack(slots)
    count, bit = len(slots), 1
    while bit < count:
        pairs = v.reshape(count // (2 * bit), 2, bit, *v.shape[1:])
        v = jnp.where((index & bit) != 0, pairs[:, ::-1], pairs).reshape(v.shape)
        bit *= 2
    return v


def gather_held(weights, fsdp, core):
    halves = [pick(w.reshape(2, w.shape[0] // 2, *w.shape[1:]), core) for w in weights]
    along_z = [jnp.stack([h] + [turn(h, "fsdp", m, 8) for m in (2, 4, 6)]) for h in halves]
    along_x = [jnp.stack([v, turn(v, "fsdp", 1, 8)]) for v in along_z]
    whole = [jnp.stack([v, turn(v, "seq", 1, 4)]) for v in along_x]
    full = []
    for v, w in zip(whole, weights):
        v = jnp.where(core == 1, v[::-1], v)
        v = jnp.where((fsdp & 1) == 1, v[:, ::-1], v)
        v = jnp.where((fsdp & 2) == 2, v.reshape(2, 2, 2, 2, *v.shape[3:])[:, :, :, ::-1].reshape(v.shape), v)
        v = jnp.where((fsdp & 4) == 4, v.reshape(2, 2, 2, 2, *v.shape[3:])[:, :, ::-1].reshape(v.shape), v)
        v = v.transpose(2, 1, 0, 3, 4)
        full.append(v.reshape(w.shape[0] * 8, w.shape[1]))
    return full


def gather_lines(lines, fsdp):
    pieces = [lines] + [turn(lines, "fsdp", m, 8) for m in range(1, 8)]
    return in_order(pieces, fsdp)


def add_up(parts):
    result = parts[0].astype(F32)
    for part in parts[1:]:
        result = result + part.astype(F32)
    return result


def sum_lines(v, axis, size):
    return add_up([v] + [turn(v, axis, m, size) for m in range(1, size)])


def local(mesh_shape, hidden, cotangent, segment_ids, pad_mask, *weights):
    micro, _, span, width = hidden.shape
    length = micro * span
    fsdp, seq = lax.axis_index("fsdp"), lax.axis_index("seq")
    core, y = seq & 1, seq >> 1
    packed = mesh_shape["fsdp"] == 8
    marks = jnp.concatenate(swap_in((segment_ids * 2 + pad_mask)[:, 0], seq))
    half = width // 2
    slots = [swap_in(hidden[:, 0, :, half * n : half * n + half], seq) for n in range(2)]
    cots = swap_in(cotangent[:, 0], seq)
    (wq, wk, wv, bq, bv, wo, bo, g1, s1, we, be, wr, br, g2, s2) = weights
    if packed:
        wq, wk, wv, wo, we, wr = gather_held((wq, wk, wv, wo, we, wr), fsdp, core)
        lines = gather_lines(jnp.concatenate([bq, bv, bo, g1, s1, br, g2, s2, be]).reshape(12, -1), fsdp)
        vecs = lines[:, :8].astype(F32).transpose(1, 0, 2).reshape(8, 1, width)
        bq, bv, bo, g1, s1, br, g2, s2 = (vecs[n] for n in range(8))
        be = lines[:, 8:].astype(F32).reshape(1, -1)
    else:
        gathered = [lax.all_gather(w, "fsdp", axis=0, tiled=True) for w in weights]
        (wq, wk, wv, bq, bv, wo, bo, g1, s1, we, be, wr, br, g2, s2) = [
            w.astype(F32)[None] if w.ndim == 1 else w for w in gathered
        ]
    row, col = mask_tables(marks >> 1, marks & 1)
    ahead = [attend_forward(n, slots[n], (wq, wk, wv), bq, bv, row, col) for n in range(2)]
    xs = [a[0] for a in ahead]
    mixed = [a[4] for a in ahead]
    (out, gres, gmix, dwo, dwe, dwr, dbo, dg1, ds1, dbe, dbr, dg2, ds2) = middle(
        packed, xs, mixed, cots, wo, we, wr, bo, g1, s1, be, br, g2, s2
    )
    out = out.reshape(micro, span, width)
    layer_out = in_order(swap_out([out[m] for m in range(4)]), seq)[:, None]
    back, halves = [], []
    for n in range(2):
        x, q, k, v, mix, lse = ahead[n]
        back.append(attend_backward(packed, n, x, q, k, v, mix, lse, gmix, gres, (wq, wk, wv), row, col))
        ghid = back[n][0].reshape(micro, span, half)
        halves.append(swap_out([ghid[m] for m in range(4)]))
    grad_hidden = in_order([jnp.concatenate(p, axis=1).astype(F32) for p in zip(*halves)], seq)[:, None]
    dbq, dbv = (jnp.concatenate([b[n] for b in back], axis=1) for n in (2, 3))
    short = [dbq, dbv, dbo, dg1, ds1, dbr, dg2, ds2]
    if packed:
        early = [dbo, dg1, ds1, dbr, dg2, ds2, *(dbe[:, width * n : width * n + width] for n in range(4))]

        def lines_of(rows):
            both = sum_lines(sum_lines(jnp.concatenate(rows), "seq", 4), "fsdp", 8)
            return both.reshape(len(rows), width)

        start = (fsdp * 4 + seq) * 24
        first = lines_of(early)
        last = lines_of([dbq, dbv])
        dbo, dg1, ds1, dbr, dg2, ds2 = (lax.dynamic_slice_in_dim(first[n], start, 24) for n in range(6))
        dbe = lax.dynamic_slice_in_dim(first[6:].reshape(-1), start * 4, 96)
        dbq, dbv = (lax.dynamic_slice_in_dim(last[n], start, 24) for n in range(2))

        def scatter(v):
            v = add_up([pick(v, core), turn(pick(v, core ^ 1), "seq", 1, 4)])
            low = v.astype(BF)
            v = add_up([pick(v, fsdp)] + [turn(pick(low, fsdp ^ m), "fsdp", m, 8) for m in range(1, 8)])
            return add_up([pick(v, y), turn(pick(v, y ^ 1).astype(BF), "seq", 2, 4)])

        dwo, dwr = scatter(dwo), scatter(dwr)
        dwe = scatter(dwe)
        dwe = jnp.concatenate([dwe[:, : width // 4], dwe[:, width // 4 :]])
        dw = scatter(jnp.concatenate([back[0][1], back[1][1]], axis=1))
        part = width // GROUPS
        dwq, dwk, dwv = (dw[:, part * n : part * n + part] for n in range(3))
    else:
        dw = jnp.concatenate([b[1] for b in back])
        part = width // GROUPS
        dwq, dwk, dwv = (dw[:, part * n : part * n + part] for n in range(3))

        def scatter(v):
            return lax.psum_scatter(v, ("fsdp", "seq"), scatter_dimension=0, tiled=True)

        dwq, dwk, dwv, dwo, dwe, dwr = (scatter(v) for v in (dwq, dwk, dwv, dwo, dwe, dwr))
        dbq, dbv, dbo, dg1, ds1, dbr, dg2, ds2 = (scatter(v[0]) for v in short)
        dbe = scatter(dbe[0])
    return (
        layer_out, grad_hidden, dwq, dwk, dwv, dbq, dbv, dwo, dbo, dg1, ds1, dwe, dbe, dwr, dbr, dg2, ds2,
    )


def solution(mesh):
    tokens = P(None, "fsdp", "seq", None)
    marks = P(None, "fsdp", "seq")
    held, line = P("fsdp", None), P("fsdp")
    both, both_line = P(("fsdp", "seq"), None), P(("fsdp", "seq"))
    ranks = (2, 2, 2, 1, 1, 2, 1, 1, 1, 2, 1, 2, 1, 1, 1)
    in_specs = (tokens, tokens, marks, marks, *(held if n == 2 else line for n in ranks))
    out_specs = (tokens, tokens, *(both if n == 2 else both_line for n in ranks))
    return jax.shard_map(functools.partial(local, dict(mesh.shape)), mesh=mesh, in_specs=in_specs, out_specs=out_specs, check_vma=False)
```

```python
import functools

import jax
import jax.numpy as jnp
from jax import lax
from jax.experimental import pallas as pl
from jax.experimental.pallas import tpu as pltpu
from jax.sharding import PartitionSpec as P

GROUPS = 4
HEAD = 64
EPS = 1e-05
LOG2E = 1.4426950408889634
BIG = float(2**30)
BF = jnp.bfloat16
F32 = jnp.float32
NT = (((1,), (1,)), ((), ()))
NN = (((1,), (0,)), ((), ()))
TN = (((0,), (0,)), ((), ()))


def mm(a, b, dims):
    return lax.dot_general(a, b, dims, preferred_element_type=F32)


def split2(v):
    hi = v.astype(BF)
    return hi, (v - hi.astype(F32)).astype(BF)


def split3(v):
    hi = v.astype(BF)
    rest = v - hi.astype(F32)
    mid = rest.astype(BF)
    return hi, mid, (rest - mid.astype(F32)).astype(BF)


def lanes(shape):
    return lax.broadcasted_iota(jnp.int32, shape, 1)


def query_parts(q, low):
    scaled = q.astype(F32) * (LOG2E * HEAD**-0.5)
    hi, lo = split2(scaled)
    hi, lo = hi.astype(F32), lo.astype(F32)
    turned = pltpu.roll(lo, 64, 1)
    return (
        jnp.where(low, hi, turned).astype(BF),
        jnp.where(low, turned, hi).astype(BF),
    )


def key_parts(k, low):
    k = k.astype(F32)
    turned = pltpu.roll(k, 64, 1)
    return (
        jnp.where(low, k, turned).astype(BF),
        jnp.where(low, turned, k).astype(BF),
    )


def square(w):
    part = w.shape[1]
    zero = jnp.zeros((part, part), w.dtype)
    return jnp.concatenate(
        [jnp.concatenate([w[:part], zero], axis=1), jnp.concatenate([zero, w[part:]], axis=1)], axis=0
    )


def squares(pack):
    part = pack.shape[0] // 2
    return [square(pack[:, part * n : part * n + part]) for n in range(3)]


def fetch(place, own, other, dest, sem, shards):
    core, fsdp = place[0], place[1]
    copies = []
    for n, f in enumerate(shards):
        at = ((f & 1) ^ (fsdp & 1), (f >> 1) ^ (fsdp >> 1))
        base = n * 2 * own.shape[2]
        for source, c in ((own, core), (other, 1 - core)):
            rows = pl.ds(pl.multiple_of(base + c * own.shape[2], 16), own.shape[2])
            copies.append(pltpu.make_async_copy(source.at[at[0], at[1]], dest.at[rows, :], sem))
    for copy in copies:
        copy.start()
    for copy in copies:
        copy.wait()


def mask_tables(marks):
    turned = jnp.concatenate([marks, jnp.zeros((4, marks.shape[1]), F32)], axis=0).T
    codes = jnp.concatenate([turned[:, n : n + 1] for n in range(4)], axis=0)
    length = codes.shape[0]
    codes = jnp.broadcast_to(codes, (length, 128))
    lane = lanes((length, 128)).astype(F32)
    real = codes == lane * 2 + 1
    mine = real | (codes == lane * 2)
    lives = jnp.max(jnp.where(real, 1.0, 0.0), axis=0, keepdims=True)
    hot = jnp.where(mine, jnp.broadcast_to(lives, (length, 128)), 0.0)
    alive = jnp.max(hot, axis=1, keepdims=True)
    row = jnp.where(lane == 6, jnp.broadcast_to(alive, (length, 128)), hot)
    col = jnp.where(real, 0.0, jnp.where(lane < 3, -BIG, jnp.where(lane < 6, 1.0, 0.0)))
    return row.astype(BF), col.astype(BF)


def attend_kernel(which, place, *refs):
    slots, refs = refs[:4], refs[4:]
    own_ref, other_ref, *refs = refs
    if which:
        *given, refs = *refs[:2], refs[2:]
    (
        x_ref, q_ref, k_ref, v_ref, mix_ref, lse_ref, pack_ref,
        *tables, qaug, kaug, vaug, sem,
    ) = refs
    tables = given if which else tables
    length = x_ref.shape[0]
    span = length // 4
    row_ref, col_ref = tables
    fetch(place, own_ref, other_ref, pack_ref, sem, range(4 * which, 4 * which + 4))
    for n, slot in enumerate(slots):
        x_ref[span * n : span * n + span, :] = slot[:span, :]
    if not which:
        marks = jnp.concatenate([slot[span : span + 8, :span].astype(F32)[:1] for slot in slots], axis=0)
        row_ref[...], col_ref[...] = mask_tables(marks)
    line = pack_ref[:, 512:640].astype(F32).T
    rows = 256
    x = x_ref[...]
    alive = row_ref[:, 6:7].astype(F32)
    wq, wk, wv = squares(pack_ref[...])
    q_ref[...] = ((mm(x, wq, NT) + line[64:65, :]) * alive).astype(BF)
    k_ref[...] = mm(x, wk, NT).astype(BF)
    v_ref[...] = (mm(x, wv, NT) + line[65:66, :]).astype(BF)
    low = lanes((length, 128)) < 64
    for pair in range(x_ref.shape[1] // 128):
        cut = slice(128 * pair, 128 * pair + 128)
        q_parts = query_parts(q_ref[:, cut], low)
        k_parts = key_parts(k_ref[:, cut], low)
        vaug[:, :128] = v_ref[:, cut]
        vaug[:, 128:] = jnp.ones((length, 128), BF)
        for head in range(2):
            qaug[head, :, :128] = q_parts[head]
            qaug[head, :, 128:] = row_ref[...]
            kaug[head, :, :128] = k_parts[head]
            kaug[head, :, 128:] = col_ref[...]

        def block(step, carry):
            at = pl.ds(pl.multiple_of(step * rows, rows), rows)
            found = []
            for head in range(2):
                scores = mm(qaug[head, at, :], kaug[head], NT)
                top = jnp.max(scores, axis=1, keepdims=True)
                powers = jnp.exp2(scores - top).astype(BF)
                both = mm(powers, vaug[...], NN)
                total = both[:, 128:]
                found.append((both[:, :128] / total, top + jnp.log2(total)))
            left = lanes((rows, 128)) < 64
            mix_ref[at, cut] = jnp.where(left, found[0][0], found[1][0]).astype(BF)
            lse_ref[at, cut] = jnp.where(left, found[0][1], found[1][1])
            return carry

        lax.fori_loop(0, length // rows, block, 0)


def attend_forward(which, place, slots, span, tables, own, other):
    half = slots[0].shape[1]
    length = span * len(slots)
    whole = pl.BlockSpec(memory_space=pltpu.VMEM)
    hbm = pl.BlockSpec(memory_space=pl.ANY)
    shapes = [((length, half), BF)] * 5 + [((length, half), F32)]
    shapes += [((half, own.shape[-1]), BF)]
    if not which:
        shapes += [((length, 128), BF)] * 2
    return pl.pallas_call(
        functools.partial(attend_kernel, which),
        in_specs=[pl.BlockSpec(memory_space=pltpu.SMEM), *[whole] * 4, hbm, hbm, *[whole] * len(tables)],
        out_specs=[whole] * len(shapes),
        out_shape=[jax.ShapeDtypeStruct(*s) for s in shapes],
        scratch_shapes=[
            pltpu.VMEM((2, length, 256), BF),
            pltpu.VMEM((2, length, 256), BF),
            pltpu.VMEM((length, 256), BF),
            pltpu.SemaphoreType.DMA,
        ],
        compiler_params=pltpu.CompilerParams(vmem_limit_bytes=56 << 20),
        cost_estimate=pl.CostEstimate(flops=20_000_000_000, transcendentals=0, bytes_accessed=8_000_000),
        name="attend_forward",
    )(place, *slots, own, other, *tables)


def mean(v):
    return jnp.sum(v, axis=1, keepdims=True) * (1.0 / v.shape[1])


def total(v):
    return jnp.sum(v, axis=0, keepdims=True)


def gelu_parts(x):
    flat = jnp.abs(x) * 0.7071067811865476
    t = 1.0 / (1.0 + 0.3275911 * flat)
    power = jnp.exp(x * x * -0.5)
    poly = t * (0.127414796 + t * (-0.142248368 + t * (0.7107068705 + t * (-0.7265760135 + t * 0.5307027145))))
    tail = poly * power
    return jnp.where(x >= 0, 1.0 - tail, tail), power * 0.3989422804014327


def middle_kernel(
    place, xa_ref, xb_ref, mixa_ref, mixb_ref, cot0, cot1, cot2, cot3, own_ref, other_ref,
    out_ref, gres_ref, gmix_ref, grad_ref,
    slope, dwe_acc, dwo_ref, dwr_ref, cots, pack, we_ref, line_ref, be_ref, dbe_ref, sums, sems, sem,
):
    step = pl.program_id(0)
    width = pack.shape[0]
    part = width // GROUPS
    deep = width
    wo_ref = pack.at[:, :width]
    wr_ref = pack.at[:, width : 2 * width]
    bo_ref, g1_ref, s1_ref, br_ref, g2_ref, s2_ref = (line_ref.at[n : n + 1, :] for n in range(1, 7))
    dbo_ref, dg1_ref, ds1_ref, dbr_ref, dg2_ref, ds2_ref = (sums.at[n : n + 1, :] for n in range(6))

    @pl.when(step == 0)
    def _():
        for n, ref in enumerate((cot0, cot1, cot2, cot3)):
            pltpu.make_async_copy(ref, cots.at[n], sems.at[n]).start()
        fetch(place, own_ref, other_ref, pack, sem, range(8))
        for ref in (dwo_ref, dwr_ref, dwe_acc, dbe_ref, sums):
            ref[...] = jnp.zeros_like(ref)
        line_ref[...] = pack[:, 2 * width + 128 : 2 * width + 256].astype(F32).T[64:72]
        for f in range(8):
            for j in range(4):
                we_ref[384 * f + 96 * j : 384 * f + 96 * j + 96, :] = pack[
                    96 * f : 96 * f + 96, 2 * width + 256 * j : 2 * width + 256 * j + 256
                ]
        for g in range(GROUPS):
            be_ref[:, deep * g : deep * g + deep] = we_ref[deep * g : deep * g + deep, 128:].astype(F32).T[64:65]

    pltpu.make_async_copy(cot0, cots.at[step], sems.at[step]).wait()
    mixed = jnp.concatenate([mixa_ref[...], mixb_ref[...]], axis=1)
    rows_in = jnp.concatenate([xa_ref[...], xb_ref[...]], axis=1)
    residual = rows_in.astype(F32) + mm(mixed, wo_ref[...], NT) + bo_ref[...]
    centred = residual - mean(residual)
    rate1 = lax.rsqrt(mean(centred * centred) + EPS)
    hat1 = centred * rate1
    normed = hat1 * g1_ref[...] + s1_ref[...]
    normed_low = normed.astype(BF)
    acts, branches = [], []
    for g in range(GROUPS):
        piece = normed_low[:, part * g : part * g + part]
        tall = slice(deep * g, deep * g + deep)
        pre = mm(piece, we_ref[tall, :part], NT) + be_ref[:, tall]
        upper, density = gelu_parts(pre)
        acts.append((pre * upper).astype(BF))
        slope[:, tall] = upper + pre * density
        branches.append(mm(acts[g], wr_ref[part * g : part * g + part, :], NT))
    second = normed + jnp.concatenate(branches, axis=1) + br_ref[...]
    centred = second - mean(second)
    rate2 = lax.rsqrt(mean(centred * centred) + EPS)
    hat2 = centred * rate2
    out_ref[...] = (hat2 * g2_ref[...] + s2_ref[...]).astype(BF)
    cot = cots[step].astype(F32)
    dg2_ref[...] += total(cot * hat2)
    ds2_ref[...] += total(cot)
    e = cot * g2_ref[...]
    grad_second = rate2 * (e - mean(e) - hat2 * mean(e * hat2))
    grad_branch = grad_second.astype(BF)
    dbr_ref[...] += total(grad_branch.astype(F32))
    backs = []
    for g in range(GROUPS):
        narrow = slice(part * g, part * g + part)
        tall = slice(deep * g, deep * g + deep)
        piece = grad_branch[:, narrow]
        dwr_ref[narrow, :] += mm(piece, acts[g], TN)
        grad_pre = mm(piece, wr_ref[narrow, :], NN) * slope[:, tall]
        grad_pre_low = grad_pre.astype(BF)
        dbe_ref[:, tall] += total(grad_pre_low.astype(F32))
        dwe_acc[g] += mm(normed_low[:, narrow], grad_pre_low, TN)
        backs.append(mm(grad_pre_low, we_ref[tall, :part], NN))
    grad_normed = grad_second + jnp.concatenate(backs, axis=1)
    dg1_ref[...] += total(grad_normed * hat1)
    ds1_ref[...] += total(grad_normed)
    e = grad_normed * g1_ref[...]
    grad_residual = rate1 * (e - mean(e) - hat1 * mean(e * hat1))
    gres_ref[...] = grad_residual
    grad_projected = grad_residual.astype(BF)
    dbo_ref[...] += total(grad_projected.astype(F32))
    dwo_ref[...] += mm(grad_projected, mixed, TN)
    gmix_ref[...] = mm(grad_projected, wo_ref[...], NN).astype(BF)

    @pl.when(step == pl.num_programs(0) - 1)
    def _():
        side = jnp.concatenate([sums[...], *(dbe_ref[:, deep * g : deep * g + deep] for g in range(GROUPS))], axis=0)
        side = jnp.concatenate([side, jnp.zeros((128 - side.shape[0], width), F32)], axis=0).T
        for g in range(GROUPS):
            tall = dwe_acc[g].T
            for n in range(8):
                owner = 8 * g + n
                few = slice(24 * owner, 24 * owner + 24)
                turns = [slice(96 * n + 24 * j, 96 * n + 24 * j + 24) for j in range(4)]
                lane = lanes((24, 128))
                extra = side[few]
                for j, cut in enumerate(turns):
                    extra = jnp.where(lane == 8 + j, jnp.broadcast_to(side[cut, 8 + g : 9 + g], (24, 128)), extra)
                piece = jnp.concatenate(
                    [dwo_ref[few, :], dwr_ref[few, :], *(tall[cut] for cut in turns), extra], axis=1
                )
                grad_ref[owner % 2, owner // 4 % 2, owner // 8, owner // 2 % 2] = piece.astype(BF)


def middle(place, halves, mixed, cots, own, other):
    rows, width = cots[0].shape
    length = rows * len(cots)
    deep = width * GROUPS
    tokens = pl.BlockSpec((rows, width), lambda i: (i, 0))
    half = pl.BlockSpec((rows, width // 2), lambda i: (i, 0))
    whole = pl.BlockSpec(memory_space=pltpu.VMEM)
    hbm = pl.BlockSpec(memory_space=pl.ANY)
    return pl.pallas_call(
        middle_kernel,
        grid=(length // rows,),
        in_specs=[pl.BlockSpec(memory_space=pltpu.SMEM), *[half] * 4, *[hbm] * 6],
        out_specs=[tokens] * 3 + [whole],
        out_shape=[
            jax.ShapeDtypeStruct((length, width), BF),
            jax.ShapeDtypeStruct((length, width), F32),
            jax.ShapeDtypeStruct((length, width), BF),
            jax.ShapeDtypeStruct((2, 2, 4, 2, 24, 3 * width + 128), BF),
        ],
        scratch_shapes=[
            pltpu.VMEM((rows, deep), F32),
            pltpu.VMEM((GROUPS, width // GROUPS, width), F32),
            pltpu.VMEM((width, width), F32),
            pltpu.VMEM((width, width), F32),
            pltpu.VMEM((len(cots), rows, width), BF),
            pltpu.VMEM((width, own.shape[-1]), BF),
            pltpu.VMEM((deep, 256), BF),
            pltpu.VMEM((8, width), F32),
            pltpu.VMEM((1, deep), F32),
            pltpu.VMEM((1, deep), F32),
            pltpu.VMEM((8, width), F32),
            pltpu.SemaphoreType.DMA((len(cots),)),
            pltpu.SemaphoreType.DMA,
        ],
        compiler_params=pltpu.CompilerParams(vmem_limit_bytes=56 << 20),
        cost_estimate=pl.CostEstimate(flops=40_000_000_000, transcendentals=0, bytes_accessed=16_000_000),
        name="middle",
    )(place, *halves, *mixed, *cots, own, other)


def back_kernel(
    pairs, first, final, q_ref, k_ref, v_ref, mix_ref, gmix_ref, lse_ref, row_ref, col_ref, *refs,
):
    if final:
        x_ref, gres_ref, pack_ref, ready_ref, ghid_ref, dw_ref, *refs = refs
        *refs, dq, dk, dv = refs
        for n, ref in enumerate((dq, dk, dv)):
            for pair in range(first):
                ref[:, 128 * pair : 128 * pair + 128] = ready_ref[n, pair]

        def keep(n, pair, at, value):
            (dq, dk, dv)[n][at, 128 * pair : 128 * pair + 128] = value
    else:
        ready_ref, *refs = refs

        def keep(n, pair, at, value):
            ready_ref[n, pair - first, at] = value

    qaug, kaug, vaug, gaug, dq_acc = refs
    length = q_ref.shape[0]
    rows = 256
    low = lanes((length, 128)) < 64
    lane = lanes((length, 128))
    alive = row_ref[:, 6:7].astype(F32)
    scale = HEAD**-0.5
    zero = jnp.zeros((length, 128), BF)
    for pair in range(first, first + pairs):
        cut = slice(128 * pair, 128 * pair + 128)
        q_parts = query_parts(q_ref[:, cut], low)
        k_parts = key_parts(k_ref[:, cut], low)
        grad = gmix_ref[:, cut]
        prod = grad.astype(F32) * mix_ref[:, cut].astype(F32)
        lse = lse_ref[:, cut]
        turned = pltpu.roll(lse, 64, 1)
        vaug[:, :128] = v_ref[:, cut]
        vaug[:, 128:] = jnp.ones((length, 128), BF)
        for head in range(2):
            mine = low if head == 0 else ~low
            dot = jnp.sum(jnp.where(mine, prod, 0.0), axis=1, keepdims=True)
            d1, d2, d3 = split3(jnp.broadcast_to(-dot, (length, 128)))
            l1, l2, l3 = split3(-jnp.where(mine, lse, turned))
            qaug[head, :, :128] = q_parts[head]
            qaug[head, :, 128:] = jnp.where(
                lane == 3, l1, jnp.where(lane == 4, l2, jnp.where(lane == 5, l3, row_ref[...]))
            )
            kaug[head, :, :128] = k_parts[head]
            kaug[head, :, 128:] = col_ref[...]
            gaug[head, :, :128] = jnp.where(mine, grad, zero)
            gaug[head, :, 128:] = jnp.where(
                lane == 0, d1, jnp.where(lane == 1, d2, jnp.where(lane == 2, d3, zero))
            )
        dq_acc[...] = jnp.zeros_like(dq_acc)

        def block(step, carry):
            at = pl.ds(pl.multiple_of(step * rows, rows), rows)
            left = lanes((length, 128)) < 64
            near = lanes((rows, 128)) < 64
            d_key = jnp.zeros((rows, 128), F32)
            d_value = jnp.zeros((rows, 128), F32)
            for head in range(2):
                probs = jnp.exp2(mm(kaug[head, at, :], qaug[head], NT))
                slopes = mm(vaug[at, :], gaug[head], NT)
                grads = (probs * slopes).astype(BF)
                d_value += mm(probs.astype(BF), gaug[head, :, :128], NN)
                queries = q_ref[:, cut]
                keys = k_ref[at, cut]
                if head == 0:
                    queries = jnp.where(left, queries, jnp.zeros_like(queries))
                    keys = jnp.where(near, keys, jnp.zeros_like(keys))
                else:
                    queries = jnp.where(left, jnp.zeros_like(queries), queries)
                    keys = jnp.where(near, jnp.zeros_like(keys), keys)
                d_key += mm(grads, queries, NN)
                dq_acc[...] += mm(grads, keys, TN)
            keep(1, pair, at, (d_key * scale).astype(BF))
            keep(2, pair, at, d_value.astype(BF))
            return carry

        lax.fori_loop(0, length // rows, block, 0)
        keep(0, pair, slice(None), (dq_acc[...] * (alive * scale)).astype(BF))
    if not final:
        return
    wq, wk, wv = squares(pack_ref[...])
    ghid_ref[...] = (
        gres_ref[...] + mm(dq[...], wq, NN) + mm(dk[...], wk, NN) + mm(dv[...], wv, NN)
    ).astype(BF)
    part = x_ref.shape[1] // 2
    ones = jnp.ones((length, 128), BF)
    sums = []
    for grad in (dq, dk, dv):
        both = mm(grad[...], x_ref[...], TN)
        sums.append((both[:part, :part], both[part:, part:]))
    d_qb, d_vb = mm(dq[...], ones, TN), mm(dv[...], ones, TN)
    extra = jnp.where(lanes(d_qb.shape) == 0, d_qb, d_vb)[:, :64]
    for g in range(2):
        wide = jnp.concatenate([*(each[g] for each in sums), extra[part * g : part * g + part]], axis=1)
        for n in range(8):
            dw_ref[n % 2, n // 4, g, n // 2 % 2] = wide[24 * n : 24 * n + 24].astype(BF)


def attend_backward(which, first, pairs, q, k, v, mixed, lse, gmix, row, col, finish=()):
    length, half = q.shape
    wide = pl.BlockSpec((length, half), lambda i: (0, which))
    whole = pl.BlockSpec(memory_space=pltpu.VMEM)
    scratch = [
        pltpu.VMEM((2, length, 256), BF),
        pltpu.VMEM((2, length, 256), BF),
        pltpu.VMEM((length, 256), BF),
        pltpu.VMEM((2, length, 256), BF),
        pltpu.VMEM((length, 128), F32),
    ]
    if finish:
        specs = [whole, wide, whole, whole]
        shapes = [((length, half), BF), ((2, 2, 2, 2, 24, finish[2].shape[1]), BF)]
        scratch += [pltpu.VMEM((length, half), BF)] * 3
    else:
        specs = []
        shapes = [((3, pairs, length, 128), BF)]
    return pl.pallas_call(
        functools.partial(back_kernel, pairs, first, bool(finish)),
        grid=(1,),
        in_specs=[*[whole] * 4, wide, *[whole] * 3, *specs],
        out_specs=[whole] * len(shapes),
        out_shape=[jax.ShapeDtypeStruct(*s) for s in shapes],
        scratch_shapes=scratch,
        compiler_params=pltpu.CompilerParams(vmem_limit_bytes=56 << 20),
        cost_estimate=pl.CostEstimate(flops=12_000_000_000 * pairs, transcendentals=0, bytes_accessed=4_000_000),
        name="attend_backward",
    )(q, k, v, mixed, gmix, lse, row, col, *finish)


def turn(v, axis, step, size):
    return lax.ppermute(v, axis, [(i, i ^ step) for i in range(size)])


def pick(v, index):
    return lax.dynamic_index_in_dim(v, index, 0, keepdims=False)


def swap_out(slots):
    return [slots[0]] + [turn(slots[m], "seq", m, 4) for m in range(1, 4)]


def placed(slots, seq):
    result = jnp.zeros((len(slots), *slots[0].shape), slots[0].dtype)
    for m, slot in enumerate(slots):
        result = lax.dynamic_update_index_in_dim(result, slot, seq ^ m, 0)
    return result


def pack_heads(wq, wk, wv, bq, bv):
    gap = jnp.zeros((wq.shape[0], 62), BF)
    return jnp.concatenate([wq, wk, wv, bq[:, None], bv[:, None], gap], axis=1)


def pack_deep(wo, wr, we, be, lines):
    rows, part = wo.shape[0], we.shape[1]
    tall = we.reshape(rows // 96, 4, 96, part)
    side = be.reshape(rows // 96, 4, 96)
    pieces = [wo, wr]
    for j in range(4):
        pieces += [tall[:, j].reshape(rows, part), side[:, j].reshape(rows, 1)]
        extra = lines if j == 0 else []
        pieces += [v[:, None] for v in extra] + [jnp.zeros((rows, 63 - len(extra)), BF)]
    return jnp.concatenate(pieces, axis=1)


def after(value, *others):
    return lax.optimization_barrier((value, others))[0]


def along_z(pack, core):
    piece = pick(pack.reshape(2, pack.shape[0] // 2, pack.shape[1]), core)
    return [piece] + [turn(piece, "fsdp", m, 8) for m in (2, 4, 6)]


def along_x(pieces):
    v = jnp.stack(pieces)
    return jnp.stack([v, turn(v, "fsdp", 1, 8)])


def split_whole(full):
    v = full.reshape(4, 2, 2, 48, full.shape[1]).transpose(2, 1, 0, 3, 4)
    return v[0], v[1]


def add_up(parts):
    result = parts[0].astype(F32)
    for part in parts[1:]:
        result = result + part.astype(F32)
    return result


def scatter_steps(x, z, y, core):
    return (
        ("seq", core, ((1, 1),), 4),
        ("fsdp", x, ((1, 1),), 8),
        ("fsdp", z, ((1, 2), (2, 4), (3, 6)), 8),
        ("seq", y, ((1, 2),), 4),
    )


def scatter_step(parts, step):
    axis, at, hops, size = step
    came = [turn(add_up([pick(p, at ^ m) for p in parts]).astype(BF), axis, hop, size) for m, hop in hops]
    return [pick(p, at) for p in parts] + came


def open_deep(v, width):
    owners = v.shape[0] // 24
    tall = v[:, 2 * width : 3 * width].reshape(owners, 24, 4, width // 4).transpose(0, 2, 1, 3)
    d_be = v[:, 3 * width + 8 : 3 * width + 12].reshape(owners, 24, 4).transpose(0, 2, 1).reshape(-1)
    lines = [v[:, 3 * width + n] for n in range(6)]
    return v[:, :width], v[:, width : 2 * width], tall.reshape(-1, width // 4), d_be, lines


def open_heads(v, width):
    part = width // GROUPS
    return [v[:, part * n : part * n + part] for n in range(3)] + [v[:, 3 * part], v[:, 3 * part + 1]]


def local(mesh_shape, hidden, cotangent, segment_ids, pad_mask, *weights):
    micro, _, span, width = hidden.shape
    half = width // 2
    fsdp, seq = lax.axis_index("fsdp"), lax.axis_index("seq")
    core, y, x, z = seq & 1, seq >> 1, fsdp & 1, fsdp >> 1
    near = mesh_shape["fsdp"] == 8
    (wq, wk, wv, bq, bv, wo, bo, g1, s1, we, be, wr, br, g2, s2) = weights
    lines = [bo, g1, s1, br, g2, s2]

    marks = (segment_ids * 2 + pad_mask)[:, 0].astype(BF)
    marks = jnp.pad(marks[:, None, :], ((0, 0), (0, 7), (0, half - span)))
    first = jnp.concatenate([hidden[:, 0, :, :half], marks], axis=1)
    second = hidden[:, 0, :, half:]

    def swap_in(v):
        return [pick(v, seq)] + [turn(pick(v, seq ^ m), "seq", m, 4) for m in range(1, 4)]

    first = swap_in(first)
    if near:
        place = jnp.stack([core, fsdp])
        heads_z = along_z(pack_heads(wq, wk, wv, bq, bv), core)
        heads_own = along_x(heads_z)
        heads = heads_own, turn(heads_own, "seq", 1, 4)
        deep_z = along_z(after(pack_deep(wo, wr, we, be, lines), *heads_z), core)
    else:
        place = jnp.zeros((2,), jnp.int32)
        (wq, wk, wv, bq, bv, wo, bo, g1, s1, we, be, wr, br, g2, s2) = [
            lax.all_gather(w, "fsdp", axis=0, tiled=True) for w in weights
        ]
        heads = split_whole(pack_heads(wq, wk, wv, bq, bv))
        deep = split_whole(pack_deep(wo, wr, we, be, [bo, g1, s1, br, g2, s2]))
    second = swap_in(after(second, first))
    ahead = [attend_forward(0, place, after(first, second[1]), span, (), *heads)]
    tables = ahead[0][7:]
    cots = swap_in(after(cotangent[:, 0], second, tables))
    if near:
        deep_own = along_x(after(deep_z, second, tables))
    ahead.append(attend_forward(1, place, second, span, tables, *heads))
    if near:
        deep_own = after(deep_own, ahead[1][6], cots)
        deep = deep_own, turn(deep_own, "seq", 1, 4)
    xs, mixed = ([a[n] for a in ahead] for n in (0, 4))
    out, gres, gmix, d_deep = middle(place, xs, mixed, cots, *deep)
    out = out.reshape(micro, span, width)
    out_slots = swap_out([out[m] for m in range(4)])
    steps = scatter_steps(x, z, y, core)
    d_deep = [d_deep]

    def backward(n, first, pairs, gmix, *finish):
        xn, q, k, v, mix, lse, pack = ahead[n][:7]
        finish = (xn, gres, pack, *finish) if finish else ()
        return attend_backward(n, first, pairs, q, k, v, mix, lse, gmix, *tables, finish)

    def leave(ghid):
        ghid = ghid.reshape(micro, span, half)
        return swap_out([ghid[m] for m in range(4)])

    (ready,) = backward(0, 0, 1, gmix)
    if near:
        d_deep = scatter_step(d_deep, steps[0])
    gmix = after(gmix, ready, d_deep)
    ghid, dw_first = backward(0, 1, 2, gmix, ready)
    if near:
        d_deep = scatter_step(d_deep, steps[1])
    gmix = after(gmix, ghid, d_deep, out_slots)
    halves = [leave(ghid)]
    (ready,) = backward(1, 0, 2, gmix)
    if near:
        d_deep = scatter_step(d_deep, steps[2])
    gmix = after(gmix, ready, halves[0])
    ghid, dw_second = backward(1, 2, 1, gmix, ready)
    halves.append(leave(ghid))
    layer_out = placed(after(out_slots, ghid), seq)[:, None]
    grad_hidden = placed([jnp.concatenate(p, axis=1).astype(F32) for p in zip(*halves)], seq)[:, None]
    d_heads = jnp.concatenate([dw_first, dw_second], axis=2)
    if near:
        d_heads = [d_heads]
        for step in steps[:2]:
            d_heads = scatter_step(d_heads, step)
        d_deep = scatter_step(after(d_deep, d_heads), steps[3])
        for step in steps[2:]:
            d_heads = scatter_step(d_heads, step)
        dwo, dwr, dwe, dbe, d_lines = open_deep(add_up(d_deep), width)
        dwq, dwk, dwv, dbq, dbv = open_heads(add_up(d_heads), width)
    else:

        def natural(v):
            return v.transpose(2, 1, 3, 0, 4, 5).reshape(width, -1).astype(F32)

        dwo, dwr, dwe, dbe, d_lines = open_deep(natural(d_deep[0]), width)
        dwq, dwk, dwv, dbq, dbv = open_heads(natural(d_heads), width)

        def scatter(v):
            return lax.psum_scatter(v, ("fsdp", "seq"), scatter_dimension=0, tiled=True)

        dwq, dwk, dwv, dbq, dbv, dwo, dwr, dwe, dbe = (scatter(v) for v in (dwq, dwk, dwv, dbq, dbv, dwo, dwr, dwe, dbe))
        d_lines = [scatter(v) for v in d_lines]
    dbo, dg1, ds1, dbr, dg2, ds2 = d_lines
    return (
        layer_out, grad_hidden, dwq, dwk, dwv, dbq, dbv, dwo, dbo, dg1, ds1, dwe, dbe, dwr, dbr, dg2, ds2,
    )


def solution(mesh):
    tokens = P(None, "fsdp", "seq", None)
    marks = P(None, "fsdp", "seq")
    held, line = P("fsdp", None), P("fsdp")
    both, both_line = P(("fsdp", "seq"), None), P(("fsdp", "seq"))
    ranks = (2, 2, 2, 1, 1, 2, 1, 1, 1, 2, 1, 2, 1, 1, 1)
    in_specs = (tokens, tokens, marks, marks, *(held if n == 2 else line for n in ranks))
    out_specs = (tokens, tokens, *(both if n == 2 else both_line for n in ranks))
    return jax.shard_map(functools.partial(local, dict(mesh.shape)), mesh=mesh, in_specs=in_specs, out_specs=out_specs, check_vma=False)
```

```python
import functools

import jax
import jax.numpy as jnp
from jax import lax
from jax.experimental import pallas as pl
from jax.experimental.pallas import tpu as pltpu
from jax.sharding import PartitionSpec as P

GROUPS = 4
MIDDLE_ROWS = 256
HEAD = 64
EPS = 1e-05
LOG2E = 1.4426950408889634
BIG = float(2**30)
BF = jnp.bfloat16
F32 = jnp.float32
NT = (((1,), (1,)), ((), ()))
NN = (((1,), (0,)), ((), ()))
TN = (((0,), (0,)), ((), ()))


def mm(a, b, dims):
    return lax.dot_general(a, b, dims, preferred_element_type=F32)


def split2(v):
    hi = v.astype(BF)
    return hi, (v - hi.astype(F32)).astype(BF)


def split3(v):
    hi = v.astype(BF)
    rest = v - hi.astype(F32)
    mid = rest.astype(BF)
    return hi, mid, (rest - mid.astype(F32)).astype(BF)


def lanes(shape):
    return lax.broadcasted_iota(jnp.int32, shape, 1)


def query_parts(q, low):
    scaled = q.astype(F32) * (LOG2E * HEAD**-0.5)
    hi, lo = split2(scaled)
    hi, lo = hi.astype(F32), lo.astype(F32)
    turned = pltpu.roll(lo, 64, 1)
    return (
        jnp.where(low, hi, turned).astype(BF),
        jnp.where(low, turned, hi).astype(BF),
    )


def key_parts(k, low):
    k = k.astype(F32)
    turned = pltpu.roll(k, 64, 1)
    return (
        jnp.where(low, k, turned).astype(BF),
        jnp.where(low, turned, k).astype(BF),
    )


def square(w):
    part = w.shape[1]
    zero = jnp.zeros((part, part), w.dtype)
    return jnp.concatenate(
        [jnp.concatenate([w[:part], zero], axis=1), jnp.concatenate([zero, w[part:]], axis=1)], axis=0
    )


def squares(pack):
    part = pack.shape[0] // 2
    return [square(pack[:, part * n : part * n + part]) for n in range(3)]


def fetch(place, own, other, dest, sem, shards):
    core, fsdp = place[0], place[1]
    copies = []
    for n, f in enumerate(shards):
        at = ((f & 1) ^ (fsdp & 1), (f >> 1) ^ (fsdp >> 1))
        base = n * 2 * own.shape[2]
        for source, c in ((own, core), (other, 1 - core)):
            rows = pl.ds(pl.multiple_of(base + c * own.shape[2], 16), own.shape[2])
            copies.append(pltpu.make_async_copy(source.at[at[0], at[1]], dest.at[rows, :], sem))
    for copy in copies:
        copy.start()
    for copy in copies:
        copy.wait()


def mask_tables(marks):
    turned = jnp.concatenate([marks, jnp.zeros((4, marks.shape[1]), F32)], axis=0).T
    codes = jnp.concatenate([turned[:, n : n + 1] for n in range(4)], axis=0)
    length = codes.shape[0]
    codes = jnp.broadcast_to(codes, (length, 128))
    lane = lanes((length, 128)).astype(F32)
    real = codes == lane * 2 + 1
    mine = real | (codes == lane * 2)
    lives = jnp.max(jnp.where(real, 1.0, 0.0), axis=0, keepdims=True)
    hot = jnp.where(mine, jnp.broadcast_to(lives, (length, 128)), 0.0)
    alive = jnp.max(hot, axis=1, keepdims=True)
    row = jnp.where(lane == 6, jnp.broadcast_to(alive, (length, 128)), hot)
    col = jnp.where(real, 0.0, jnp.where(lane < 3, -BIG, jnp.where(lane < 6, 1.0, 0.0)))
    return row.astype(BF), col.astype(BF)


def wide_at(pair):
    return pl.ds(pl.multiple_of(128 * pair, 128), 128)


def attend_kernel(which, place, *refs):
    slots, refs = refs[:4], refs[4:]
    own_ref, other_ref, *refs = refs
    if which:
        *given, refs = *refs[:2], refs[2:]
    (
        x_ref, q_ref, k_ref, v_ref, mix_ref, low_ref, lse_ref, pack_ref,
        *tables, queries, keys, values, qaug, kaug, vaug, peak, wide, sem,
    ) = refs
    row_ref, col_ref = given if which else tables
    length = x_ref.shape[0]
    span = length // 4
    pair = pl.program_id(0)

    @pl.when(pair == 0)
    def _():
        fetch(place, own_ref, other_ref, pack_ref, sem, range(4 * which, 4 * which + 4))
        for n, slot in enumerate(slots):
            x_ref[span * n : span * n + span, :] = slot[:span, :]
        if not which:
            marks = jnp.concatenate([slot[span : span + 8, :span].astype(F32)[:1] for slot in slots], axis=0)
            row_ref[...], col_ref[...] = mask_tables(marks)
        line = pack_ref[:, 512:640].astype(F32).T
        x = x_ref[...]
        alive = row_ref[:, 6:7].astype(F32)
        wq, wk, wv = squares(pack_ref[...])
        queries[...] = ((mm(x, wq, NT) + line[64:65, :]) * alive).astype(BF)
        keys[...] = mm(x, wk, NT).astype(BF)
        values[...] = (mm(x, wv, NT) + line[65:66, :]).astype(BF)
        vaug[:, 128:] = jnp.ones((length, 128), BF)
        for head in range(2):
            kaug[head, :, 128:] = col_ref[...]
        peak[...] = jnp.zeros_like(peak)
        half = x_ref.shape[1]
        head_of = lax.broadcasted_iota(jnp.int32, (half, 128), 0) // HEAD == lanes((half, 128))
        sizes = []
        for ref in (queries, keys):
            v = ref[...].astype(F32)
            squared = (v * v).astype(BF)
            sizes.append(jnp.max(mm(squared, jnp.where(head_of, 1.0, 0.0).astype(BF), NN), axis=0, keepdims=True))
        limit = (90.0 * HEAD**0.5 / LOG2E) ** 2
        wide[0] = jnp.where(jnp.max(sizes[0] * sizes[1]) > limit, 1, 0)

    cut = wide_at(pair)
    q, k = queries[:, cut], keys[:, cut]
    q_ref[...], k_ref[...], v_ref[...] = q, k, values[:, cut]
    low = lanes((length, 128)) < 64
    q_parts = query_parts(q, low)
    k_parts = key_parts(k, low)
    vaug[:, :128] = values[:, cut]
    for head in range(2):
        qaug[head, :, :128] = q_parts[head]
        qaug[head, :, 128:] = row_ref[...]
        kaug[head, :, :128] = k_parts[head]

        @pl.when(wide[0] == 1)
        def _():
            rows = 128
            lane = lanes((rows, 128))

            def shift(step, carry):
                at = pl.ds(pl.multiple_of(step * rows, rows), rows)
                top = jnp.max(mm(qaug[head, at, :], kaug[head], NT), axis=1, keepdims=True)
                top = jnp.broadcast_to(top, (rows, 128))
                peak[head, at, :] = top
                t1, t2, t3 = split3(-top)
                info = qaug[head, at, 128:]
                qaug[head, at, 128:] = jnp.where(
                    lane == 3, t1, jnp.where(lane == 4, t2, jnp.where(lane == 5, t3, info))
                )
                return carry

            lax.fori_loop(0, length // rows, shift, 0)

    rows = 512
    left = lanes((rows, 128)) < 64

    def block(step, carry):
        at = pl.ds(pl.multiple_of(step * rows, rows), rows)
        found = []
        for head in range(2):
            powers = jnp.exp2(mm(qaug[head, at, :], kaug[head], NT)).astype(BF)
            both = mm(powers, vaug[...], NN)
            found.append((both[:, :128] / both[:, 128:], peak[head, at, :] + jnp.log2(both[:, 128:])))
        mixed = jnp.where(left, found[0][0], found[1][0])
        mix_ref[at, :], low_ref[at, :] = split2(mixed)
        lse_ref[at, :] = jnp.where(left, found[0][1], found[1][1])
        return carry

    lax.fori_loop(0, length // rows, block, 0)


def attend_forward(which, place, slots, span, tables, own, other):
    half = slots[0].shape[1]
    length = span * len(slots)
    whole = pl.BlockSpec(memory_space=pltpu.VMEM)
    hbm = pl.BlockSpec(memory_space=pl.ANY)
    pair = pl.BlockSpec((length, 128), lambda i: (0, i))
    shapes = [((length, half), BF)] * 6 + [((length, half), F32)]
    shapes += [((half, own.shape[-1]), BF)]
    if not which:
        shapes += [((length, 128), BF)] * 2
    return pl.pallas_call(
        functools.partial(attend_kernel, which),
        grid=(half // 128,),
        in_specs=[pl.BlockSpec(memory_space=pltpu.SMEM), *[whole] * 4, hbm, hbm, *[whole] * len(tables)],
        out_specs=[whole, *[pair] * 6, *[whole] * (len(shapes) - 7)],
        out_shape=[jax.ShapeDtypeStruct(*s) for s in shapes],
        scratch_shapes=[
            *[pltpu.VMEM((length, half), BF)] * 3,
            pltpu.VMEM((2, length, 256), BF),
            pltpu.VMEM((2, length, 256), BF),
            pltpu.VMEM((length, 256), BF),
            pltpu.VMEM((2, length, 128), F32),
            pltpu.SMEM((1,), jnp.int32),
            pltpu.SemaphoreType.DMA,
        ],
        compiler_params=pltpu.CompilerParams(vmem_limit_bytes=56 << 20),
        cost_estimate=pl.CostEstimate(flops=20_000_000_000, transcendentals=0, bytes_accessed=8_000_000),
        name="attend_forward",
    )(place, *slots, own, other, *tables)


def mean(v):
    return jnp.sum(v, axis=1, keepdims=True) * (1.0 / v.shape[1])


def total(v):
    return jnp.sum(v, axis=0, keepdims=True)


def gelu_parts(x):
    flat = jnp.abs(x) * 0.7071067811865476
    t = 1.0 / (1.0 + 0.3275911 * flat)
    power = jnp.exp(x * x * -0.5)
    poly = t * (0.127414796 + t * (-0.142248368 + t * (0.7107068705 + t * (-0.7265760135 + t * 0.5307027145))))
    tail = poly * power
    return jnp.where(x >= 0, 1.0 - tail, tail), power * 0.3989422804014327


def middle_kernel(
    place, xa_ref, xb_ref, mixa_ref, mixb_ref, cot0, cot1, cot2, cot3, own_ref, other_ref,
    out_ref, gres_ref, gmix_ref, grad_ref,
    slope, dwe_acc, dwo_ref, dwr_ref, cots, pack, we_ref, line_ref, be_ref, dbe_ref, sums, sems, sem,
):
    step = pl.program_id(0)
    rows, span = xa_ref.shape[0], cot0.shape[0]
    width = pack.shape[0]
    part = width // GROUPS
    deep = width
    wo_ref = pack.at[:, :width]
    wr_ref = pack.at[:, width : 2 * width]
    bo_ref, g1_ref, s1_ref, br_ref, g2_ref, s2_ref = (line_ref.at[n : n + 1, :] for n in range(1, 7))
    dbo_ref, dg1_ref, ds1_ref, dbr_ref, dg2_ref, ds2_ref = (sums.at[n : n + 1, :] for n in range(6))

    @pl.when(step == 0)
    def _():
        for n, ref in enumerate((cot0, cot1, cot2, cot3)):
            pltpu.make_async_copy(ref, cots.at[span * n : span * n + span, :], sems.at[n]).start()
        fetch(place, own_ref, other_ref, pack, sem, range(8))
        for ref in (dwo_ref, dwr_ref, dwe_acc, dbe_ref, sums):
            ref[...] = jnp.zeros_like(ref)
        line_ref[...] = pack[:, 2 * width + 128 : 2 * width + 256].astype(F32).T[64:72]
        for f in range(8):
            for j in range(4):
                we_ref[384 * f + 96 * j : 384 * f + 96 * j + 96, :] = pack[
                    96 * f : 96 * f + 96, 2 * width + 256 * j : 2 * width + 256 * j + 256
                ]
        for g in range(GROUPS):
            be_ref[:, deep * g : deep * g + deep] = we_ref[deep * g : deep * g + deep, 128:].astype(F32).T[64:65]

    for n in range(rows // span):
        pltpu.make_async_copy(cot0, cots.at[:span, :], sems.at[step * (rows // span) + n]).wait()
    mixed = jnp.concatenate([mixa_ref[...], mixb_ref[...]], axis=1)
    rows_in = jnp.concatenate([xa_ref[...], xb_ref[...]], axis=1)
    residual = rows_in.astype(F32) + mm(mixed, wo_ref[...], NT) + bo_ref[...]
    centred = residual - mean(residual)
    rate1 = lax.rsqrt(mean(centred * centred) + EPS)
    hat1 = centred * rate1
    normed = hat1 * g1_ref[...] + s1_ref[...]
    normed_low = normed.astype(BF)
    acts, branches = [], []
    for g in range(GROUPS):
        piece = normed_low[:, part * g : part * g + part]
        tall = slice(deep * g, deep * g + deep)
        pre = mm(piece, we_ref[tall, :part], NT) + be_ref[:, tall]
        upper, density = gelu_parts(pre)
        acts.append((pre * upper).astype(BF))
        slope[:, tall] = upper + pre * density
        branches.append(mm(acts[g], wr_ref[part * g : part * g + part, :], NT))
    second = normed + jnp.concatenate(branches, axis=1) + br_ref[...]
    centred = second - mean(second)
    rate2 = lax.rsqrt(mean(centred * centred) + EPS)
    hat2 = centred * rate2
    out_ref[...] = (hat2 * g2_ref[...] + s2_ref[...]).astype(BF)
    cot = cots[pl.ds(pl.multiple_of(step * rows, rows), rows), :].astype(F32)
    dg2_ref[...] += total(cot * hat2)
    ds2_ref[...] += total(cot)
    e = cot * g2_ref[...]
    grad_second = rate2 * (e - mean(e) - hat2 * mean(e * hat2))
    grad_branch = grad_second.astype(BF)
    dbr_ref[...] += total(grad_branch.astype(F32))
    backs = []
    for g in range(GROUPS):
        narrow = slice(part * g, part * g + part)
        tall = slice(deep * g, deep * g + deep)
        piece = grad_branch[:, narrow]
        dwr_ref[narrow, :] += mm(piece, acts[g], TN)
        grad_pre = mm(piece, wr_ref[narrow, :], NN) * slope[:, tall]
        grad_pre_low = grad_pre.astype(BF)
        dbe_ref[:, tall] += total(grad_pre_low.astype(F32))
        dwe_acc[g] += mm(normed_low[:, narrow], grad_pre_low, TN)
        backs.append(mm(grad_pre_low, we_ref[tall, :part], NN))
    grad_normed = grad_second + jnp.concatenate(backs, axis=1)
    dg1_ref[...] += total(grad_normed * hat1)
    ds1_ref[...] += total(grad_normed)
    e = grad_normed * g1_ref[...]
    grad_residual = rate1 * (e - mean(e) - hat1 * mean(e * hat1))
    gres_ref[...] = grad_residual
    grad_projected = grad_residual.astype(BF)
    dbo_ref[...] += total(grad_projected.astype(F32))
    dwo_ref[...] += mm(grad_projected, mixed, TN)
    gmix_ref[...] = mm(grad_projected, wo_ref[...], NN).astype(BF)

    @pl.when(step == pl.num_programs(0) - 1)
    def _():
        side = jnp.concatenate([sums[...], *(dbe_ref[:, deep * g : deep * g + deep] for g in range(GROUPS))], axis=0)
        side = jnp.concatenate([side, jnp.zeros((128 - side.shape[0], width), F32)], axis=0).T
        for g in range(GROUPS):
            tall = dwe_acc[g].T
            for n in range(8):
                owner = 8 * g + n
                few = slice(24 * owner, 24 * owner + 24)
                turns = [slice(96 * n + 24 * j, 96 * n + 24 * j + 24) for j in range(4)]
                lane = lanes((24, 128))
                extra = side[few]
                for j, cut in enumerate(turns):
                    extra = jnp.where(lane == 8 + j, jnp.broadcast_to(side[cut, 8 + g : 9 + g], (24, 128)), extra)
                piece = jnp.concatenate(
                    [dwo_ref[few, :], dwr_ref[few, :], *(tall[cut] for cut in turns), extra], axis=1
                )
                grad_ref[owner % 2, owner // 4 % 2, owner // 8, owner // 2 % 2] = piece.astype(BF)


def middle(place, halves, mixed, cots, own, other):
    span, width = cots[0].shape
    length = span * len(cots)
    rows = MIDDLE_ROWS
    deep = width * GROUPS
    tokens = pl.BlockSpec((rows, width), lambda i: (i, 0))
    half = pl.BlockSpec((rows, width // 2), lambda i: (i, 0))
    whole = pl.BlockSpec(memory_space=pltpu.VMEM)
    hbm = pl.BlockSpec(memory_space=pl.ANY)
    return pl.pallas_call(
        middle_kernel,
        grid=(length // rows,),
        in_specs=[pl.BlockSpec(memory_space=pltpu.SMEM), *[half] * 4, *[hbm] * 6],
        out_specs=[tokens] * 3 + [whole],
        out_shape=[
            jax.ShapeDtypeStruct((length, width), BF),
            jax.ShapeDtypeStruct((length, width), F32),
            jax.ShapeDtypeStruct((length, width), BF),
            jax.ShapeDtypeStruct((2, 2, 4, 2, 24, 3 * width + 128), BF),
        ],
        scratch_shapes=[
            pltpu.VMEM((rows, deep), F32),
            pltpu.VMEM((GROUPS, width // GROUPS, width), F32),
            pltpu.VMEM((width, width), F32),
            pltpu.VMEM((width, width), F32),
            pltpu.VMEM((length, width), BF),
            pltpu.VMEM((width, own.shape[-1]), BF),
            pltpu.VMEM((deep, 256), BF),
            pltpu.VMEM((8, width), F32),
            pltpu.VMEM((1, deep), F32),
            pltpu.VMEM((1, deep), F32),
            pltpu.VMEM((8, width), F32),
            pltpu.SemaphoreType.DMA((len(cots),)),
            pltpu.SemaphoreType.DMA,
        ],
        compiler_params=pltpu.CompilerParams(vmem_limit_bytes=56 << 20),
        cost_estimate=pl.CostEstimate(flops=40_000_000_000, transcendentals=0, bytes_accessed=16_000_000),
        name="middle",
    )(place, *halves, *mixed, *cots, own, other)


def back_kernel(
    q_ref, k_ref, v_ref, mix_ref, low_ref, gmix_ref, lse_ref, row_ref, col_ref, *refs,
):
    step = pl.program_id(0)
    length = q_ref.shape[0]
    x_ref, gres_ref, pack_ref, ghid_ref, dw_ref, *refs, dq, dk, dv = refs
    outs = [ref.at[:, wide_at(step)] for ref in (dq, dk, dv)]
    qaug, kaug, vaug, gaug, dq_acc = refs

    @pl.when(step == 0)
    def _():
        vaug[:, 128:] = jnp.ones((length, 128), BF)
        for head in range(2):
            kaug[head, :, 128:] = col_ref[...]

    rows = 256
    low = lanes((length, 128)) < 64
    lane = lanes((length, 128))
    alive = row_ref[:, 6:7].astype(F32)
    scale = HEAD**-0.5
    zero = jnp.zeros((length, 128), BF)
    q_parts = query_parts(q_ref[...], low)
    k_parts = key_parts(k_ref[...], low)
    grad = gmix_ref[...]
    prod = grad.astype(F32) * (mix_ref[...].astype(F32) + low_ref[...].astype(F32))
    lse = lse_ref[...]
    turned = pltpu.roll(lse, 64, 1)
    vaug[:, :128] = v_ref[...]
    for head in range(2):
        mine = low if head == 0 else ~low
        dot = jnp.sum(jnp.where(mine, prod, 0.0), axis=1, keepdims=True)
        d1, d2, d3 = split3(jnp.broadcast_to(-dot, (length, 128)))
        l1, l2, l3 = split3(-jnp.where(mine, lse, turned))
        qaug[head, :, :128] = q_parts[head]
        qaug[head, :, 128:] = jnp.where(
            lane == 3, l1, jnp.where(lane == 4, l2, jnp.where(lane == 5, l3, row_ref[...]))
        )
        kaug[head, :, :128] = k_parts[head]
        gaug[head, :, :128] = jnp.where(mine, grad, zero)
        gaug[head, :, 128:] = jnp.where(
            lane == 0, d1, jnp.where(lane == 1, d2, jnp.where(lane == 2, d3, zero))
        )
    dq_acc[...] = jnp.zeros_like(dq_acc)
    near = lanes((rows, 128)) < 64

    def block(turn_, carry):
        at = pl.ds(pl.multiple_of(turn_ * rows, rows), rows)
        d_key = jnp.zeros((rows, 128), F32)
        d_value = jnp.zeros((rows, 128), F32)
        for head in range(2):
            probs = jnp.exp2(mm(kaug[head, at, :], qaug[head], NT))
            slopes = mm(vaug[at, :], gaug[head], NT)
            grads = (probs * slopes).astype(BF)
            d_value += mm(probs.astype(BF), gaug[head, :, :128], NN)
            queries, keys = q_ref[...], k_ref[at, :]
            if head == 0:
                queries = jnp.where(low, queries, zero)
                keys = jnp.where(near, keys, jnp.zeros_like(keys))
            else:
                queries = jnp.where(low, zero, queries)
                keys = jnp.where(near, jnp.zeros_like(keys), keys)
            d_key += mm(grads, queries, NN)
            dq_acc[...] += mm(grads, keys, TN)
        outs[1][at, :] = (d_key * scale).astype(BF)
        outs[2][at, :] = d_value.astype(BF)
        return carry

    lax.fori_loop(0, length // rows, block, 0)
    outs[0][...] = (dq_acc[...] * (alive * scale)).astype(BF)

    @pl.when(step == pl.num_programs(0) - 1)
    def _():
        finish_heads(x_ref, gres_ref, pack_ref, dq, dk, dv, ghid_ref, dw_ref)


def finish_heads(x_ref, gres_ref, pack_ref, dq, dk, dv, ghid_ref, dw_ref):
    length = x_ref.shape[0]
    wq, wk, wv = squares(pack_ref[...])
    ghid_ref[...] = (
        gres_ref[...] + mm(dq[...], wq, NN) + mm(dk[...], wk, NN) + mm(dv[...], wv, NN)
    ).astype(BF)
    part = x_ref.shape[1] // 2
    ones = jnp.ones((length, 128), BF)
    sums = []
    for grad in (dq, dk, dv):
        both = mm(grad[...], x_ref[...], TN)
        sums.append((both[:part, :part], both[part:, part:]))
    d_qb, d_vb = mm(dq[...], ones, TN), mm(dv[...], ones, TN)
    extra = jnp.where(lanes(d_qb.shape) == 0, d_qb, d_vb)[:, :64]
    for g in range(2):
        wide = jnp.concatenate([*(each[g] for each in sums), extra[part * g : part * g + part]], axis=1)
        for n in range(8):
            dw_ref[n % 2, n // 4, g, n // 2 % 2] = wide[24 * n : 24 * n + 24].astype(BF)


def attend_backward(which, q, k, v, mixed, mixed_low, lse, gmix, row, col, x, gres, pack):
    length, half = q.shape
    pairs = half // 128
    base = which * pairs
    pair = pl.BlockSpec((length, 128), lambda i: (0, i))
    shifted = pl.BlockSpec((length, 128), lambda i: (0, base + i))
    whole = pl.BlockSpec(memory_space=pltpu.VMEM)
    scratch = [
        pltpu.VMEM((2, length, 256), BF),
        pltpu.VMEM((2, length, 256), BF),
        pltpu.VMEM((length, 256), BF),
        pltpu.VMEM((2, length, 256), BF),
        pltpu.VMEM((length, 128), F32),
    ]
    scratch += [pltpu.VMEM((length, half), BF)] * 3
    half_of = pl.BlockSpec((length, half), lambda i: (0, which))
    return pl.pallas_call(
        back_kernel,
        grid=(pairs,),
        in_specs=[*[pair] * 5, shifted, pair, whole, whole, whole, half_of, whole],
        out_specs=[whole, whole],
        out_shape=[
            jax.ShapeDtypeStruct((length, half), BF),
            jax.ShapeDtypeStruct((2, 2, 2, 2, 24, pack.shape[1]), BF),
        ],
        scratch_shapes=scratch,
        compiler_params=pltpu.CompilerParams(vmem_limit_bytes=56 << 20),
        cost_estimate=pl.CostEstimate(flops=12_000_000_000 * pairs, transcendentals=0, bytes_accessed=4_000_000),
        name="attend_backward",
    )(q, k, v, mixed, mixed_low, gmix, lse, row, col, x, gres, pack)


def turn(v, axis, step, size):
    return lax.ppermute(v, axis, [(i, i ^ step) for i in range(size)])


def pick(v, index):
    return lax.dynamic_index_in_dim(v, index, 0, keepdims=False)


def swap_out(slots):
    return [slots[0]] + [turn(slots[m], "seq", m, 4) for m in range(1, 4)]


def placed(slots, seq):
    result = jnp.zeros((len(slots), *slots[0].shape), slots[0].dtype)
    for m, slot in enumerate(slots):
        result = lax.dynamic_update_index_in_dim(result, slot, seq ^ m, 0)
    return result


def pack_heads(wq, wk, wv, bq, bv):
    gap = jnp.zeros((wq.shape[0], 62), BF)
    return jnp.concatenate([wq, wk, wv, bq[:, None], bv[:, None], gap], axis=1)


def pack_deep(wo, wr, we, be, lines):
    rows, part = wo.shape[0], we.shape[1]
    tall = we.reshape(rows // 96, 4, 96, part)
    side = be.reshape(rows // 96, 4, 96)
    pieces = [wo, wr]
    for j in range(4):
        pieces += [tall[:, j].reshape(rows, part), side[:, j].reshape(rows, 1)]
        extra = lines if j == 0 else []
        pieces += [v[:, None] for v in extra] + [jnp.zeros((rows, 63 - len(extra)), BF)]
    return jnp.concatenate(pieces, axis=1)


def after(value, *others):
    return lax.optimization_barrier((value, others))[0]


def along_z(pack, core):
    piece = pick(pack.reshape(2, pack.shape[0] // 2, pack.shape[1]), core)
    return [piece] + [turn(piece, "fsdp", m, 8) for m in (2, 4, 6)]


def along_x(pieces):
    v = jnp.stack(pieces)
    return jnp.stack([v, turn(v, "fsdp", 1, 8)])


def split_whole(full):
    v = full.reshape(4, 2, 2, 48, full.shape[1]).transpose(2, 1, 0, 3, 4)
    return v[0], v[1]


def add_up(parts):
    result = parts[0].astype(F32)
    for part in parts[1:]:
        result = result + part.astype(F32)
    return result


def scatter_steps(x, z, y, core):
    return (
        ("seq", core, ((1, 1),), 4),
        ("fsdp", x, ((1, 1),), 8),
        ("fsdp", z, ((1, 2), (2, 4), (3, 6)), 8),
        ("seq", y, ((1, 2),), 4),
    )


def scatter_step(parts, step):
    axis, at, hops, size = step
    came = [turn(add_up([pick(p, at ^ m) for p in parts]).astype(BF), axis, hop, size) for m, hop in hops]
    return [pick(p, at) for p in parts] + came


def open_deep(v, width):
    owners = v.shape[0] // 24
    tall = v[:, 2 * width : 3 * width].reshape(owners, 24, 4, width // 4).transpose(0, 2, 1, 3)
    d_be = v[:, 3 * width + 8 : 3 * width + 12].reshape(owners, 24, 4).transpose(0, 2, 1).reshape(-1)
    lines = [v[:, 3 * width + n] for n in range(6)]
    return v[:, :width], v[:, width : 2 * width], tall.reshape(-1, width // 4), d_be, lines


def open_heads(v, width):
    part = width // GROUPS
    return [v[:, part * n : part * n + part] for n in range(3)] + [v[:, 3 * part], v[:, 3 * part + 1]]


def local(mesh_shape, hidden, cotangent, segment_ids, pad_mask, *weights):
    micro, _, span, width = hidden.shape
    half = width // 2
    fsdp, seq = lax.axis_index("fsdp"), lax.axis_index("seq")
    core, y, x, z = seq & 1, seq >> 1, fsdp & 1, fsdp >> 1
    near = mesh_shape["fsdp"] == 8
    (wq, wk, wv, bq, bv, wo, bo, g1, s1, we, be, wr, br, g2, s2) = weights
    lines = [bo, g1, s1, br, g2, s2]

    marks = (segment_ids * 2 + pad_mask)[:, 0].astype(BF)
    marks = jnp.pad(marks[:, None, :], ((0, 0), (0, 7), (0, half - span)))
    first = jnp.concatenate([hidden[:, 0, :, :half], marks], axis=1)
    second = hidden[:, 0, :, half:]

    def swap_in(v):
        return [pick(v, seq)] + [turn(pick(v, seq ^ m), "seq", m, 4) for m in range(1, 4)]

    first = swap_in(first)
    if near:
        place = jnp.stack([core, fsdp])
        heads_z = along_z(pack_heads(wq, wk, wv, bq, bv), core)
        heads_own = along_x(heads_z)
        heads = heads_own, turn(heads_own, "seq", 1, 4)
        deep_z = along_z(after(pack_deep(wo, wr, we, be, lines), *heads_z), core)
    else:
        place = jnp.zeros((2,), jnp.int32)
        (wq, wk, wv, bq, bv, wo, bo, g1, s1, we, be, wr, br, g2, s2) = [
            lax.all_gather(w, "fsdp", axis=0, tiled=True) for w in weights
        ]
        heads = split_whole(pack_heads(wq, wk, wv, bq, bv))
        deep = split_whole(pack_deep(wo, wr, we, be, [bo, g1, s1, br, g2, s2]))
    second = swap_in(after(second, first))
    ahead = [attend_forward(0, place, after(first, second[1]), span, (), *heads)]
    tables = ahead[0][8:]
    cots = swap_in(after(cotangent[:, 0], second, tables))
    if near:
        deep_own = along_x(after(deep_z, second, tables))
    ahead.append(attend_forward(1, place, second, span, tables, *heads))
    if near:
        deep_own = after(deep_own, ahead[1][7], cots)
        deep = deep_own, turn(deep_own, "seq", 1, 4)
    xs, mixed = ([a[n] for a in ahead] for n in (0, 4))
    out, gres, gmix, d_deep = middle(place, xs, mixed, cots, *deep)
    out = out.reshape(micro, span, width)
    out_slots = swap_out([out[m] for m in range(4)])
    steps = scatter_steps(x, z, y, core)
    d_deep = [d_deep]

    def backward(n, gmix):
        xn, q, k, v, mix, mix_low, lse, pack = ahead[n][:8]
        return attend_backward(n, q, k, v, mix, mix_low, lse, gmix, *tables, xn, gres, pack)

    def leave(ghid):
        ghid = ghid.reshape(micro, span, half)
        return swap_out([ghid[m] for m in range(4)])

    if near:
        d_deep = scatter_step(d_deep, steps[0])
        d_deep, gmix = lax.optimization_barrier((d_deep, gmix))
        d_deep = scatter_step(d_deep, steps[1])
    ghid, dw_first = backward(0, gmix)
    gmix = after(gmix, ghid, d_deep, out_slots)
    halves = [leave(ghid)]
    if near:
        d_deep = scatter_step(d_deep, steps[2])
    ghid, dw_second = backward(1, gmix)
    halves[0], ghid = lax.optimization_barrier((halves[0], ghid))
    halves.append(leave(ghid))
    layer_out = placed(after(out_slots, ghid), seq)[:, None]
    grad_hidden = placed([jnp.concatenate(p, axis=1).astype(F32) for p in zip(*halves)], seq)[:, None]
    d_heads = jnp.concatenate([dw_first, dw_second], axis=2)
    if near:
        d_heads = [d_heads]
        for step in steps[:2]:
            d_heads = scatter_step(d_heads, step)
        d_deep = scatter_step(after(d_deep, d_heads), steps[3])
        for step in steps[2:]:
            d_heads = scatter_step(d_heads, step)
        dwo, dwr, dwe, dbe, d_lines = open_deep(add_up(d_deep), width)
        dwq, dwk, dwv, dbq, dbv = open_heads(add_up(d_heads), width)
    else:

        def natural(v):
            return v.transpose(2, 1, 3, 0, 4, 5).reshape(width, -1).astype(F32)

        dwo, dwr, dwe, dbe, d_lines = open_deep(natural(d_deep[0]), width)
        dwq, dwk, dwv, dbq, dbv = open_heads(natural(d_heads), width)

        def scatter(v):
            return lax.psum_scatter(v, ("fsdp", "seq"), scatter_dimension=0, tiled=True)

        dwq, dwk, dwv, dbq, dbv, dwo, dwr, dwe, dbe = (scatter(v) for v in (dwq, dwk, dwv, dbq, dbv, dwo, dwr, dwe, dbe))
        d_lines = [scatter(v) for v in d_lines]
    dbo, dg1, ds1, dbr, dg2, ds2 = d_lines
    return (
        layer_out, grad_hidden, dwq, dwk, dwv, dbq, dbv, dwo, dbo, dg1, ds1, dwe, dbe, dwr, dbr, dg2, ds2,
    )


def solution(mesh):
    tokens = P(None, "fsdp", "seq", None)
    marks = P(None, "fsdp", "seq")
    held, line = P("fsdp", None), P("fsdp")
    both, both_line = P(("fsdp", "seq"), None), P(("fsdp", "seq"))
    ranks = (2, 2, 2, 1, 1, 2, 1, 1, 1, 2, 1, 2, 1, 1, 1)
    in_specs = (tokens, tokens, marks, marks, *(held if n == 2 else line for n in ranks))
    out_specs = (tokens, tokens, *(both if n == 2 else both_line for n in ranks))
    return jax.shard_map(functools.partial(local, dict(mesh.shape)), mesh=mesh, in_specs=in_specs, out_specs=out_specs, check_vma=False)
```

```python
import functools

import jax
import jax.numpy as jnp
from jax import lax
from jax.experimental import pallas as pl
from jax.experimental.pallas import tpu as pltpu
from jax.sharding import PartitionSpec as P

GROUPS = 4
MIDDLE_ROWS = 256
HEAD = 64
EPS = 1e-05
LOG2E = 1.4426950408889634
BIG = float(2**30)
BF = jnp.bfloat16
F32 = jnp.float32
NT = (((1,), (1,)), ((), ()))
NN = (((1,), (0,)), ((), ()))
TN = (((0,), (0,)), ((), ()))


def mm(a, b, dims):
    return lax.dot_general(a, b, dims, preferred_element_type=F32)


def split2(v):
    hi = v.astype(BF)
    return hi, (v - hi.astype(F32)).astype(BF)


def split3(v):
    hi = v.astype(BF)
    rest = v - hi.astype(F32)
    mid = rest.astype(BF)
    return hi, mid, (rest - mid.astype(F32)).astype(BF)


def lanes(shape):
    return lax.broadcasted_iota(jnp.int32, shape, 1)


def query_parts(q, low):
    scaled = q.astype(F32) * (LOG2E * HEAD**-0.5)
    hi, lo = split2(scaled)
    hi, lo = hi.astype(F32), lo.astype(F32)
    turned = pltpu.roll(lo, 64, 1)
    return (
        jnp.where(low, hi, turned).astype(BF),
        jnp.where(low, turned, hi).astype(BF),
    )


def key_parts(k, low):
    k = k.astype(F32)
    turned = pltpu.roll(k, 64, 1)
    return (
        jnp.where(low, k, turned).astype(BF),
        jnp.where(low, turned, k).astype(BF),
    )


def square(w):
    part = w.shape[1]
    zero = jnp.zeros((part, part), w.dtype)
    return jnp.concatenate(
        [jnp.concatenate([w[:part], zero], axis=1), jnp.concatenate([zero, w[part:]], axis=1)], axis=0
    )


def squares(pack):
    part = pack.shape[0] // 2
    return [square(pack[:, part * n : part * n + part]) for n in range(3)]


def fetch(place, own, other, dest, sem, shards):
    core, fsdp = place[0], place[1]
    copies = []
    for n, f in enumerate(shards):
        at = ((f & 1) ^ (fsdp & 1), (f >> 1) ^ (fsdp >> 1))
        base = n * 2 * own.shape[2]
        for source, c in ((own, core), (other, 1 - core)):
            rows = pl.ds(pl.multiple_of(base + c * own.shape[2], 16), own.shape[2])
            copies.append(pltpu.make_async_copy(source.at[at[0], at[1]], dest.at[rows, :], sem))
    for copy in copies:
        copy.start()
    return copies


def mask_tables(marks):
    turned = jnp.concatenate([marks, jnp.zeros((4, marks.shape[1]), F32)], axis=0).T
    codes = jnp.concatenate([turned[:, n : n + 1] for n in range(4)], axis=0)
    length = codes.shape[0]
    codes = jnp.broadcast_to(codes, (length, 128))
    lane = lanes((length, 128)).astype(F32)
    real = codes == lane * 2 + 1
    mine = real | (codes == lane * 2)
    lives = jnp.max(jnp.where(real, 1.0, 0.0), axis=0, keepdims=True)
    hot = jnp.where(mine, jnp.broadcast_to(lives, (length, 128)), 0.0)
    alive = jnp.max(hot, axis=1, keepdims=True)
    row = jnp.where(lane == 6, jnp.broadcast_to(alive, (length, 128)), hot)
    col = jnp.where(real, 0.0, jnp.where(lane < 3, -BIG, jnp.where(lane < 6, 1.0, 0.0)))
    return row.astype(BF), col.astype(BF)


def wide_at(pair):
    return pl.ds(pl.multiple_of(128 * pair, 128), 128)


def attend_kernel(which, place, *refs):
    slots, refs = refs[:4], refs[4:]
    own_ref, other_ref, *refs = refs
    if which:
        *given, refs = *refs[:2], refs[2:]
    (
        x_ref, q_ref, k_ref, v_ref, mix_ref, low_ref, lse_ref, pack_ref,
        *tables, queries, keys, values, qaug, kaug, vaug, peak, wide, sem,
    ) = refs
    row_ref, col_ref = given if which else tables
    length = x_ref.shape[0]
    span = length // 4
    pair = pl.program_id(0)

    @pl.when(pair == 0)
    def _():
        copies = fetch(place, own_ref, other_ref, pack_ref, sem, range(4 * which, 4 * which + 4))
        for n, slot in enumerate(slots):
            x_ref[span * n : span * n + span, :] = slot[:span, :]
        if not which:
            marks = jnp.concatenate([slot[span : span + 8, :span].astype(F32)[:1] for slot in slots], axis=0)
            row_ref[...], col_ref[...] = mask_tables(marks)
        vaug[:, 128:] = jnp.ones((length, 128), BF)
        for head in range(2):
            kaug[head, :, 128:] = col_ref[...]
        peak[...] = jnp.zeros_like(peak)
        for copy in copies:
            copy.wait()
        line = pack_ref[:, 512:640].astype(F32).T
        x = x_ref[...]
        alive = row_ref[:, 6:7].astype(F32)
        wq, wk, wv = squares(pack_ref[...])
        queries[...] = ((mm(x, wq, NT) + line[64:65, :]) * alive).astype(BF)
        keys[...] = mm(x, wk, NT).astype(BF)
        values[...] = (mm(x, wv, NT) + line[65:66, :]).astype(BF)
        half = x_ref.shape[1]
        head_of = lax.broadcasted_iota(jnp.int32, (half, 128), 0) // HEAD == lanes((half, 128))
        sizes = []
        for ref in (queries, keys):
            v = ref[...].astype(F32)
            squared = (v * v).astype(BF)
            sizes.append(jnp.max(mm(squared, jnp.where(head_of, 1.0, 0.0).astype(BF), NN), axis=0, keepdims=True))
        limit = (90.0 * HEAD**0.5 / LOG2E) ** 2
        wide[0] = jnp.where(jnp.max(sizes[0] * sizes[1]) > limit, 1, 0)

    cut = wide_at(pair)
    q, k = queries[:, cut], keys[:, cut]
    q_ref[...], k_ref[...], v_ref[...] = q, k, values[:, cut]
    low = lanes((length, 128)) < 64
    q_parts = query_parts(q, low)
    k_parts = key_parts(k, low)
    vaug[:, :128] = values[:, cut]
    for head in range(2):
        qaug[head, :, :128] = q_parts[head]
        qaug[head, :, 128:] = row_ref[...]
        kaug[head, :, :128] = k_parts[head]

        @pl.when(wide[0] == 1)
        def _():
            rows = 128
            lane = lanes((rows, 128))

            def shift(step, carry):
                at = pl.ds(pl.multiple_of(step * rows, rows), rows)
                top = jnp.max(mm(qaug[head, at, :], kaug[head], NT), axis=1, keepdims=True)
                top = jnp.broadcast_to(top, (rows, 128))
                peak[head, at, :] = top
                t1, t2, t3 = split3(-top)
                info = qaug[head, at, 128:]
                qaug[head, at, 128:] = jnp.where(
                    lane == 3, t1, jnp.where(lane == 4, t2, jnp.where(lane == 5, t3, info))
                )
                return carry

            lax.fori_loop(0, length // rows, shift, 0)

    rows = 512
    left = lanes((rows, 128)) < 64

    def block(step, carry):
        at = pl.ds(pl.multiple_of(step * rows, rows), rows)
        found = []
        for head in range(2):
            powers = jnp.exp2(mm(qaug[head, at, :], kaug[head], NT)).astype(BF)
            both = mm(powers, vaug[...], NN)
            found.append((both[:, :128] / both[:, 128:], peak[head, at, :] + jnp.log2(both[:, 128:])))
        mixed = jnp.where(left, found[0][0], found[1][0])
        mix_ref[at, :], low_ref[at, :] = split2(mixed)
        lse_ref[at, :] = jnp.where(left, found[0][1], found[1][1])
        return carry

    lax.fori_loop(0, length // rows, block, 0)


def attend_forward(which, place, slots, span, tables, own, other):
    half = slots[0].shape[1]
    length = span * len(slots)
    whole = pl.BlockSpec(memory_space=pltpu.VMEM)
    hbm = pl.BlockSpec(memory_space=pl.ANY)
    pair = pl.BlockSpec((length, 128), lambda i: (0, i))
    shapes = [((length, half), BF)] * 6 + [((length, half), F32)]
    shapes += [((half, own.shape[-1]), BF)]
    if not which:
        shapes += [((length, 128), BF)] * 2
    return pl.pallas_call(
        functools.partial(attend_kernel, which),
        grid=(half // 128,),
        in_specs=[pl.BlockSpec(memory_space=pltpu.SMEM), *[whole] * 4, hbm, hbm, *[whole] * len(tables)],
        out_specs=[whole, *[pair] * 6, *[whole] * (len(shapes) - 7)],
        out_shape=[jax.ShapeDtypeStruct(*s) for s in shapes],
        scratch_shapes=[
            *[pltpu.VMEM((length, half), BF)] * 3,
            pltpu.VMEM((2, length, 256), BF),
            pltpu.VMEM((2, length, 256), BF),
            pltpu.VMEM((length, 256), BF),
            pltpu.VMEM((2, length, 128), F32),
            pltpu.SMEM((1,), jnp.int32),
            pltpu.SemaphoreType.DMA,
        ],
        compiler_params=pltpu.CompilerParams(vmem_limit_bytes=56 << 20),
        cost_estimate=pl.CostEstimate(flops=20_000_000_000, transcendentals=0, bytes_accessed=8_000_000),
        name="attend_forward",
    )(place, *slots, own, other, *tables)


def mean(v):
    return jnp.sum(v, axis=1, keepdims=True) * (1.0 / v.shape[1])


def total(v):
    return jnp.sum(v, axis=0, keepdims=True)


def leave_piece(place, grads, owner, piece):
    x, z = place[1] & 1, place[1] >> 1
    at = ((owner % 2) ^ place[0], (owner // 4 % 2) ^ x, (owner // 8) ^ z, (owner // 2 % 2) ^ place[2])
    grads[at] = piece.astype(BF)


def move(pairs, sem):
    copies = [pltpu.make_async_copy(source, dest, sem) for source, dest in pairs]
    for copy in copies:
        copy.start()
    for copy in copies:
        copy.wait()


def gelu_parts(x):
    flat = jnp.abs(x) * 0.7071067811865476
    t = 1.0 / (1.0 + 0.3275911 * flat)
    power = jnp.exp(x * x * -0.5)
    poly = t * (0.127414796 + t * (-0.142248368 + t * (0.7107068705 + t * (-0.7265760135 + t * 0.5307027145))))
    tail = poly * power
    return jnp.where(x >= 0, 1.0 - tail, tail), power * 0.3989422804014327


def middle_kernel(
    place, xa_ref, xb_ref, mixa_ref, mixb_ref, cot0, cot1, cot2, cot3, own_ref, other_ref,
    out0, out1, out2, out3, gres_ref, gmix_ref, keep_ref, send_ref,
    slope, dwe_acc, dwo_ref, dwr_ref, cots, pack, we_ref, line_ref, be_ref, dbe_ref, sums, grads, sems, sem,
):
    step = pl.program_id(0)
    rows, span = xa_ref.shape[0], cot0.shape[0]
    width = pack.shape[0]
    part = width // GROUPS
    deep = width
    wo_ref = pack.at[:, :width]
    wr_ref = pack.at[:, width : 2 * width]
    bo_ref, g1_ref, s1_ref, br_ref, g2_ref, s2_ref = (line_ref.at[n : n + 1, :] for n in range(1, 7))
    dbo_ref, dg1_ref, ds1_ref, dbr_ref, dg2_ref, ds2_ref = (sums.at[n : n + 1, :] for n in range(6))

    @pl.when(step == 0)
    def _():
        for n, ref in enumerate((cot0, cot1, cot2, cot3)):
            pltpu.make_async_copy(ref, cots.at[span * n : span * n + span, :], sems.at[n]).start()
        copies = fetch(place, own_ref, other_ref, pack, sem, range(8))
        for ref in (dwo_ref, dwr_ref, dwe_acc, dbe_ref, sums):
            ref[...] = jnp.zeros_like(ref)
        for copy in copies:
            copy.wait()
        line_ref[...] = pack[:, 2 * width + 128 : 2 * width + 256].astype(F32).T[64:72]
        for f in range(8):
            for j in range(4):
                we_ref[384 * f + 96 * j : 384 * f + 96 * j + 96, :] = pack[
                    96 * f : 96 * f + 96, 2 * width + 256 * j : 2 * width + 256 * j + 256
                ]
        for g in range(GROUPS):
            be_ref[:, deep * g : deep * g + deep] = we_ref[deep * g : deep * g + deep, 128:].astype(F32).T[64:65]

    for n in range(rows // span):
        pltpu.make_async_copy(cot0, cots.at[:span, :], sems.at[step * (rows // span) + n]).wait()
    mixed = jnp.concatenate([mixa_ref[...], mixb_ref[...]], axis=1)
    rows_in = jnp.concatenate([xa_ref[...], xb_ref[...]], axis=1)
    residual = rows_in.astype(F32) + mm(mixed, wo_ref[...], NT) + bo_ref[...]
    centred = residual - mean(residual)
    rate1 = lax.rsqrt(mean(centred * centred) + EPS)
    hat1 = centred * rate1
    normed = hat1 * g1_ref[...] + s1_ref[...]
    normed_low = normed.astype(BF)
    acts, branches = [], []
    for g in range(GROUPS):
        piece = normed_low[:, part * g : part * g + part]
        tall = slice(deep * g, deep * g + deep)
        pre = mm(piece, we_ref[tall, :part], NT) + be_ref[:, tall]
        upper, density = gelu_parts(pre)
        acts.append((pre * upper).astype(BF))
        slope[:, tall] = upper + pre * density
        branches.append(mm(acts[g], wr_ref[part * g : part * g + part, :], NT))
    second = normed + jnp.concatenate(branches, axis=1) + br_ref[...]
    centred = second - mean(second)
    rate2 = lax.rsqrt(mean(centred * centred) + EPS)
    hat2 = centred * rate2
    out = (hat2 * g2_ref[...] + s2_ref[...]).astype(BF)
    for n, ref in enumerate((out0, out1, out2, out3)):

        @pl.when(step == n * span // rows)
        def _():
            ref[...] = out[n * span % rows : n * span % rows + span, :]

    cot = cots[pl.ds(pl.multiple_of(step * rows, rows), rows), :].astype(F32)
    dg2_ref[...] += total(cot * hat2)
    ds2_ref[...] += total(cot)
    e = cot * g2_ref[...]
    grad_second = rate2 * (e - mean(e) - hat2 * mean(e * hat2))
    grad_branch = grad_second.astype(BF)
    dbr_ref[...] += total(grad_branch.astype(F32))
    backs = []
    for g in range(GROUPS):
        narrow = slice(part * g, part * g + part)
        tall = slice(deep * g, deep * g + deep)
        piece = grad_branch[:, narrow]
        dwr_ref[narrow, :] += mm(piece, acts[g], TN)
        grad_pre = mm(piece, wr_ref[narrow, :], NN) * slope[:, tall]
        grad_pre_low = grad_pre.astype(BF)
        dbe_ref[:, tall] += total(grad_pre_low.astype(F32))
        dwe_acc[g] += mm(normed_low[:, narrow], grad_pre_low, TN)
        backs.append(mm(grad_pre_low, we_ref[tall, :part], NN))
    grad_normed = grad_second + jnp.concatenate(backs, axis=1)
    dg1_ref[...] += total(grad_normed * hat1)
    ds1_ref[...] += total(grad_normed)
    e = grad_normed * g1_ref[...]
    grad_residual = rate1 * (e - mean(e) - hat1 * mean(e * hat1))
    gres_ref[...] = grad_residual
    grad_projected = grad_residual.astype(BF)
    dbo_ref[...] += total(grad_projected.astype(F32))
    dwo_ref[...] += mm(grad_projected, mixed, TN)
    gmix_ref[...] = mm(grad_projected, wo_ref[...], NN).astype(BF)

    @pl.when(step == pl.num_programs(0) - 1)
    def _():
        side = jnp.concatenate([sums[...], *(dbe_ref[:, deep * g : deep * g + deep] for g in range(GROUPS))], axis=0)
        side = jnp.concatenate([side, jnp.zeros((128 - side.shape[0], width), F32)], axis=0).T
        for g in range(GROUPS):
            tall = dwe_acc[g].T
            for n in range(8):
                owner = 8 * g + n
                few = slice(24 * owner, 24 * owner + 24)
                turns = [slice(96 * n + 24 * j, 96 * n + 24 * j + 24) for j in range(4)]
                lane = lanes((24, 128))
                extra = side[few]
                for j, cut in enumerate(turns):
                    extra = jnp.where(lane == 8 + j, jnp.broadcast_to(side[cut, 8 + g : 9 + g], (24, 128)), extra)
                piece = jnp.concatenate(
                    [dwo_ref[few, :], dwr_ref[few, :], *(tall[cut] for cut in turns), extra], axis=1
                )
                leave_piece(place, grads, owner, piece)
        move(((grads.at[0], keep_ref), (grads.at[1], send_ref)), sem)


def middle(place, halves, mixed, cots, own, other):
    span, width = cots[0].shape
    length = span * len(cots)
    rows = MIDDLE_ROWS
    deep = width * GROUPS
    tokens = pl.BlockSpec((rows, width), lambda i: (i, 0))
    half = pl.BlockSpec((rows, width // 2), lambda i: (i, 0))
    whole = pl.BlockSpec(memory_space=pltpu.VMEM)
    hbm = pl.BlockSpec(memory_space=pl.ANY)
    return pl.pallas_call(
        middle_kernel,
        grid=(length // rows,),
        in_specs=[pl.BlockSpec(memory_space=pltpu.SMEM), *[half] * 4, *[hbm] * 6],
        out_specs=[*[whole] * 4, tokens, tokens, hbm, hbm],
        out_shape=[
            *[jax.ShapeDtypeStruct((span, width), BF)] * 4,
            jax.ShapeDtypeStruct((length, width), F32),
            jax.ShapeDtypeStruct((length, width), BF),
            *[jax.ShapeDtypeStruct((2, 4, 2, 24, 3 * width + 128), BF)] * 2,
        ],
        scratch_shapes=[
            pltpu.VMEM((rows, deep), F32),
            pltpu.VMEM((GROUPS, width // GROUPS, width), F32),
            pltpu.VMEM((width, width), F32),
            pltpu.VMEM((width, width), F32),
            pltpu.VMEM((length, width), BF),
            pltpu.VMEM((width, own.shape[-1]), BF),
            pltpu.VMEM((deep, 256), BF),
            pltpu.VMEM((8, width), F32),
            pltpu.VMEM((1, deep), F32),
            pltpu.VMEM((1, deep), F32),
            pltpu.VMEM((8, width), F32),
            pltpu.VMEM((2, 2, 4, 2, 24, 3 * width + 128), BF),
            pltpu.SemaphoreType.DMA((len(cots),)),
            pltpu.SemaphoreType.DMA,
        ],
        compiler_params=pltpu.CompilerParams(vmem_limit_bytes=56 << 20),
        cost_estimate=pl.CostEstimate(flops=40_000_000_000, transcendentals=0, bytes_accessed=16_000_000),
        name="middle",
    )(place, *halves, *mixed, *cots, own, other)


def back_kernel(
    which, place, q_ref, k_ref, v_ref, mix_ref, low_ref, gmix_ref, lse_ref, row_ref, col_ref, *refs,
):
    step = pl.program_id(0)
    length = q_ref.shape[0]
    x_ref, gres_ref, pack_ref, *refs = refs
    before, refs = refs[: 2 * which], refs[2 * which :]
    *ghids, keep_ref, send_ref = refs[:6]
    *refs, dq, dk, dv, grads, sem = refs[6:]
    outs = [ref.at[:, wide_at(step)] for ref in (dq, dk, dv)]
    qaug, kaug, vaug, gaug, qmine, dq_acc = refs

    @pl.when(step == 0)
    def _():
        vaug[:, 128:] = jnp.ones((length, 128), BF)
        for head in range(2):
            kaug[head, :, 128:] = col_ref[...]

    rows = 256
    low = lanes((length, 128)) < 64
    lane = lanes((length, 128))
    alive = row_ref[:, 6:7].astype(F32)
    scale = HEAD**-0.5
    zero = jnp.zeros((length, 128), BF)
    q_parts = query_parts(q_ref[...], low)
    k_parts = key_parts(k_ref[...], low)
    grad = gmix_ref[...]
    prod = grad.astype(F32) * (mix_ref[...].astype(F32) + low_ref[...].astype(F32))
    lse = lse_ref[...]
    turned = pltpu.roll(lse, 64, 1)
    vaug[:, :128] = v_ref[...]
    for head in range(2):
        mine = low if head == 0 else ~low
        dot = jnp.sum(jnp.where(mine, prod, 0.0), axis=1, keepdims=True)
        d1, d2, d3 = split3(jnp.broadcast_to(-dot, (length, 128)))
        l1, l2, l3 = split3(-jnp.where(mine, lse, turned))
        qaug[head, :, :128] = q_parts[head]
        qaug[head, :, 128:] = jnp.where(
            lane == 3, l1, jnp.where(lane == 4, l2, jnp.where(lane == 5, l3, row_ref[...]))
        )
        kaug[head, :, :128] = k_parts[head]
        gaug[head, :, :128] = jnp.where(mine, grad, zero)
        gaug[head, :, 128:] = jnp.where(
            lane == 0, d1, jnp.where(lane == 1, d2, jnp.where(lane == 2, d3, zero))
        )
    dq_acc[...] = jnp.zeros_like(dq_acc)
    near = lanes((rows, 128)) < 64
    for head in range(2):
        mine = low if head == 0 else ~low
        qmine[head] = jnp.where(mine, q_ref[...], zero)

    def block(turn_, carry):
        at = pl.ds(pl.multiple_of(turn_ * rows, rows), rows)
        all_probs, all_grads, all_keys = [], [], []
        for head in range(2):
            probs = jnp.exp2(mm(kaug[head, at, :], qaug[head], NT))
            slopes = mm(vaug[at, :], gaug[head], NT)
            all_grads.append((probs * slopes).astype(BF))
            all_probs.append(probs.astype(BF))
            keys = k_ref[at, :]
            none = jnp.zeros_like(keys)
            all_keys.append(jnp.where(near, keys, none) if head == 0 else jnp.where(near, none, keys))
        d_value = mm(all_probs[0], gaug[0, :, :128], NN) + mm(all_probs[1], gaug[1, :, :128], NN)
        d_key = mm(all_grads[0], qmine[0], NN) + mm(all_grads[1], qmine[1], NN)
        dq_acc[...] += mm(jnp.concatenate(all_grads, axis=0), jnp.concatenate(all_keys, axis=0), TN)
        outs[1][at, :] = (d_key * scale).astype(BF)
        outs[2][at, :] = d_value.astype(BF)
        return carry

    lax.fori_loop(0, length // rows, block, 0)
    outs[0][...] = (dq_acc[...] * (alive * scale)).astype(BF)

    @pl.when(step == pl.num_programs(0) - 1)
    def _():
        move([(old, grads.at[n]) for n, old in enumerate(before)], sem)
        finish_heads(which, place, x_ref, gres_ref, pack_ref, dq, dk, dv, ghids, grads)
        move(((grads.at[0], keep_ref), (grads.at[1], send_ref)), sem)


def finish_heads(which, place, x_ref, gres_ref, pack_ref, dq, dk, dv, ghids, grads):
    length = x_ref.shape[0]
    span = length // 4
    wq, wk, wv = squares(pack_ref[...])
    ghid = (gres_ref[...] + mm(dq[...], wq, NN) + mm(dk[...], wk, NN) + mm(dv[...], wv, NN)).astype(BF)
    for n, ref in enumerate(ghids):
        ref[...] = ghid[span * n : span * n + span, :]
    part = x_ref.shape[1] // 2
    ones = jnp.ones((length, 128), BF)
    sums = []
    for grad in (dq, dk, dv):
        both = mm(grad[...], x_ref[...], TN)
        sums.append((both[:part, :part], both[part:, part:]))
    d_qb, d_vb = mm(dq[...], ones, TN), mm(dv[...], ones, TN)
    extra = jnp.where(lanes(d_qb.shape) == 0, d_qb, d_vb)[:, :64]
    for g in range(2):
        wide = jnp.concatenate([*(each[g] for each in sums), extra[part * g : part * g + part]], axis=1)
        for n in range(8):
            leave_piece(place, grads, 16 * which + 8 * g + n, wide[24 * n : 24 * n + 24])


def attend_backward(which, place, q, k, v, mixed, mixed_low, lse, gmix, row, col, x, gres, pack, before=()):
    length, half = q.shape
    pairs = half // 128
    base = which * pairs
    pair = pl.BlockSpec((length, 128), lambda i: (0, i))
    shifted = pl.BlockSpec((length, 128), lambda i: (0, base + i))
    whole = pl.BlockSpec(memory_space=pltpu.VMEM)
    scratch = [
        pltpu.VMEM((2, length, 256), BF),
        pltpu.VMEM((2, length, 256), BF),
        pltpu.VMEM((length, 256), BF),
        pltpu.VMEM((2, length, 256), BF),
        pltpu.VMEM((2, length, 128), BF),
        pltpu.VMEM((length, 128), F32),
    ]
    scratch += [pltpu.VMEM((length, half), BF)] * 3
    scratch += [pltpu.VMEM((2, 2, 4, 2, 24, pack.shape[1]), BF), pltpu.SemaphoreType.DMA]
    hbm = pl.BlockSpec(memory_space=pl.ANY)
    half_of = pl.BlockSpec((length, half), lambda i: (0, which))
    return pl.pallas_call(
        functools.partial(back_kernel, which),
        grid=(pairs,),
        in_specs=[pl.BlockSpec(memory_space=pltpu.SMEM), *[pair] * 5, shifted, pair, whole, whole, whole, half_of, whole, *[hbm] * len(before)],
        out_specs=[*[whole] * 4, hbm, hbm],
        out_shape=[
            *[jax.ShapeDtypeStruct((length // 4, half), BF)] * 4,
            *[jax.ShapeDtypeStruct((2, 4, 2, 24, pack.shape[1]), BF)] * 2,
        ],
        scratch_shapes=scratch,
        compiler_params=pltpu.CompilerParams(vmem_limit_bytes=56 << 20),
        cost_estimate=pl.CostEstimate(flops=12_000_000_000 * pairs, transcendentals=0, bytes_accessed=4_000_000),
        name="attend_backward",
    )(place, q, k, v, mixed, mixed_low, gmix, lse, row, col, x, gres, pack, *before)


def turn(v, axis, step, size):
    return lax.ppermute(v, axis, [(i, i ^ step) for i in range(size)])


def pick(v, index):
    return lax.dynamic_index_in_dim(v, index, 0, keepdims=False)


def swap_out(slots):
    return [slots[0]] + [turn(slots[m], "seq", m, 4) for m in range(1, 4)]


def placed(slots, seq):
    result = jnp.zeros((len(slots), *slots[0].shape), slots[0].dtype)
    for m, slot in enumerate(slots):
        result = lax.dynamic_update_index_in_dim(result, slot, seq ^ m, 0)
    return result


def pack_heads(wq, wk, wv, bq, bv):
    gap = jnp.zeros((wq.shape[0], 62), BF)
    return jnp.concatenate([wq, wk, wv, bq[:, None], bv[:, None], gap], axis=1)


def pack_deep(wo, wr, we, be, lines):
    rows, part = wo.shape[0], we.shape[1]
    tall = we.reshape(rows // 96, 4, 96, part)
    side = be.reshape(rows // 96, 4, 96)
    pieces = [wo, wr]
    for j in range(4):
        pieces += [tall[:, j].reshape(rows, part), side[:, j].reshape(rows, 1)]
        extra = lines if j == 0 else []
        pieces += [v[:, None] for v in extra] + [jnp.zeros((rows, 63 - len(extra)), BF)]
    return jnp.concatenate(pieces, axis=1)


def after(value, *others):
    return lax.optimization_barrier((value, others))[0]


def along_z(pack, core):
    piece = pick(pack.reshape(2, pack.shape[0] // 2, pack.shape[1]), core)
    return [piece] + [turn(piece, "fsdp", m, 8) for m in (2, 4, 6)]


def along_x(pieces):
    v = jnp.stack(pieces)
    return jnp.stack([v, turn(v, "fsdp", 1, 8)])


def split_whole(full):
    v = full.reshape(4, 2, 2, 48, full.shape[1]).transpose(2, 1, 0, 3, 4)
    return v[0], v[1]


def add_up(parts):
    result = parts[0].astype(F32)
    for part in parts[1:]:
        result = result + part.astype(F32)
    return result


STEPS = (
    ("seq", ((1, 1),), 4),
    ("fsdp", ((1, 1),), 8),
    ("fsdp", ((1, 2), (2, 4), (3, 6)), 8),
    ("seq", ((1, 2),), 4),
)


def scatter_step(parts, step):
    axis, hops, size = step
    came = [turn(add_up([p[m] for p in parts]).astype(BF), axis, hop, size) for m, hop in hops]
    return [p[0] for p in parts] + came


def open_deep(v, width):
    owners = v.shape[0] // 24
    tall = v[:, 2 * width : 3 * width].reshape(owners, 24, 4, width // 4).transpose(0, 2, 1, 3)
    d_be = v[:, 3 * width + 8 : 3 * width + 12].reshape(owners, 24, 4).transpose(0, 2, 1).reshape(-1)
    lines = [v[:, 3 * width + n] for n in range(6)]
    return v[:, :width], v[:, width : 2 * width], tall.reshape(-1, width // 4), d_be, lines


def open_heads(v, width):
    part = width // GROUPS
    return [v[:, part * n : part * n + part] for n in range(3)] + [v[:, 3 * part], v[:, 3 * part + 1]]


def local(mesh_shape, hidden, cotangent, segment_ids, pad_mask, *weights):
    micro, _, span, width = hidden.shape
    half = width // 2
    fsdp, seq = lax.axis_index("fsdp"), lax.axis_index("seq")
    core, y = seq & 1, seq >> 1
    near = mesh_shape["fsdp"] == 8
    (wq, wk, wv, bq, bv, wo, bo, g1, s1, we, be, wr, br, g2, s2) = weights
    lines = [bo, g1, s1, br, g2, s2]

    marks = (segment_ids * 2 + pad_mask)[:, 0].astype(BF)
    marks = jnp.pad(marks[:, None, :], ((0, 0), (0, 7), (0, half - span)))
    first = jnp.concatenate([hidden[:, 0, :, :half], marks], axis=1)
    second = hidden[:, 0, :, half:]

    def swap_in(v):
        return [pick(v, seq)] + [turn(pick(v, seq ^ m), "seq", m, 4) for m in range(1, 4)]

    first = swap_in(first)
    if near:
        place = jnp.stack([core, fsdp, y])
        heads_z = along_z(pack_heads(wq, wk, wv, bq, bv), core)
        heads_own = along_x(heads_z)
        heads = heads_own, turn(heads_own, "seq", 1, 4)
        deep_z = along_z(after(pack_deep(wo, wr, we, be, lines), *heads_z), core)
    else:
        place = jnp.zeros((3,), jnp.int32)
        (wq, wk, wv, bq, bv, wo, bo, g1, s1, we, be, wr, br, g2, s2) = [
            lax.all_gather(w, "fsdp", axis=0, tiled=True) for w in weights
        ]
        heads = split_whole(pack_heads(wq, wk, wv, bq, bv))
        deep = split_whole(pack_deep(wo, wr, we, be, [bo, g1, s1, br, g2, s2]))
    second = swap_in(after(second, first))
    ahead = [attend_forward(0, place, after(first, second[1]), span, (), *heads)]
    tables = ahead[0][8:]
    cots = swap_in(after(cotangent[:, 0], second, tables))
    if near:
        deep_own = along_x(after(deep_z, second, tables))
    ahead.append(attend_forward(1, place, second, span, tables, *heads))
    if near:
        deep_own = after(deep_own, ahead[1][7], cots)
        deep = deep_own, turn(deep_own, "seq", 1, 4)
    xs, mixed = ([a[n] for a in ahead] for n in (0, 4))
    *out, gres, gmix, d_deep, d_deep_send = middle(place, xs, mixed, cots, *deep)
    out_slots = swap_out(out)

    def backward(n, gmix, before):
        xn, q, k, v, mix, mix_low, lse, pack = ahead[n][:8]
        return attend_backward(n, place, q, k, v, mix, mix_low, lse, gmix, *tables, xn, gres, pack, before)

    if near:
        d_deep = [d_deep, turn(d_deep_send, "seq", 1, 4)]
        d_deep, gmix = lax.optimization_barrier((d_deep, gmix))
        d_deep = scatter_step(d_deep, STEPS[1])
    *ghid, keep, send = backward(0, gmix, ())
    halves = [swap_out(ghid)]
    gmix = after(gmix, halves[0][1], d_deep, out_slots)
    if near:
        d_deep = scatter_step(d_deep, STEPS[2])
    *ghid, keep, send = backward(1, gmix, (keep, send))
    halves[0], d_deep, ghid = lax.optimization_barrier((halves[0], d_deep, ghid))
    halves.append(swap_out(ghid))
    if near:
        d_heads = [keep, turn(send, "seq", 1, 4)]
        d_deep = scatter_step(d_deep, STEPS[3])
        d_heads = scatter_step(d_heads, STEPS[1])
        d_deep, out_slots = after((d_deep, out_slots), d_heads)
        d_heads = scatter_step(d_heads, STEPS[2])
        halves[1] = after(halves[1], d_heads)
        d_heads = scatter_step(d_heads, STEPS[3])
    layer_out = placed(out_slots, seq)[:, None]
    grad_hidden = placed([jnp.concatenate(p, axis=1).astype(F32) for p in zip(*halves)], seq)[:, None]
    if near:
        dwo, dwr, dwe, dbe, d_lines = open_deep(add_up(d_deep), width)
        dwq, dwk, dwv, dbq, dbv = open_heads(add_up(d_heads), width)
    else:

        def natural(keep, send):
            return jnp.stack([keep, send]).transpose(2, 1, 3, 0, 4, 5).reshape(width, -1).astype(F32)

        dwo, dwr, dwe, dbe, d_lines = open_deep(natural(d_deep, d_deep_send), width)
        dwq, dwk, dwv, dbq, dbv = open_heads(natural(keep, send), width)

        def scatter(v):
            return lax.psum_scatter(v, ("fsdp", "seq"), scatter_dimension=0, tiled=True)

        dwq, dwk, dwv, dbq, dbv, dwo, dwr, dwe, dbe = (scatter(v) for v in (dwq, dwk, dwv, dbq, dbv, dwo, dwr, dwe, dbe))
        d_lines = [scatter(v) for v in d_lines]
    dbo, dg1, ds1, dbr, dg2, ds2 = d_lines
    return (
        layer_out, grad_hidden, dwq, dwk, dwv, dbq, dbv, dwo, dbo, dg1, ds1, dwe, dbe, dwr, dbr, dg2, ds2,
    )


def solution(mesh):
    tokens = P(None, "fsdp", "seq", None)
    marks = P(None, "fsdp", "seq")
    held, line = P("fsdp", None), P("fsdp")
    both, both_line = P(("fsdp", "seq"), None), P(("fsdp", "seq"))
    ranks = (2, 2, 2, 1, 1, 2, 1, 1, 1, 2, 1, 2, 1, 1, 1)
    in_specs = (tokens, tokens, marks, marks, *(held if n == 2 else line for n in ranks))
    out_specs = (tokens, tokens, *(both if n == 2 else both_line for n in ranks))
    return jax.shard_map(functools.partial(local, dict(mesh.shape)), mesh=mesh, in_specs=in_specs, out_specs=out_specs, check_vma=False)
```

```python
import functools

import jax
import jax.numpy as jnp
from jax import lax
from jax.experimental import pallas as pl
from jax.experimental.pallas import tpu as pltpu
from jax.sharding import PartitionSpec as P

GROUPS = 4
HEAD = 64
EPS = 1e-05
LOG2E = 1.4426950408889634
BIG = float(2**30)
BF = jnp.bfloat16
F32 = jnp.float32
NT = (((1,), (1,)), ((), ()))
NN = (((1,), (0,)), ((), ()))
TN = (((0,), (0,)), ((), ()))


def mm(a, b, dims):
    return lax.dot_general(a, b, dims, preferred_element_type=F32)


def split2(v):
    hi = v.astype(BF)
    return hi, (v - hi.astype(F32)).astype(BF)


def split3(v):
    hi = v.astype(BF)
    rest = v - hi.astype(F32)
    mid = rest.astype(BF)
    return hi, mid, (rest - mid.astype(F32)).astype(BF)


def lanes(shape):
    return lax.broadcasted_iota(jnp.int32, shape, 1)


def query_parts(q, low):
    scaled = q.astype(F32) * (LOG2E * HEAD**-0.5)
    hi, lo = split2(scaled)
    hi, lo = hi.astype(F32), lo.astype(F32)
    turned = pltpu.roll(lo, 64, 1)
    return (
        jnp.where(low, hi, turned).astype(BF),
        jnp.where(low, turned, hi).astype(BF),
    )


def key_parts(k, low):
    k = k.astype(F32)
    turned = pltpu.roll(k, 64, 1)
    return (
        jnp.where(low, k, turned).astype(BF),
        jnp.where(low, turned, k).astype(BF),
    )


def square(w):
    part = w.shape[1]
    zero = jnp.zeros((part, part), w.dtype)
    return jnp.concatenate(
        [jnp.concatenate([w[:part], zero], axis=1), jnp.concatenate([zero, w[part:]], axis=1)], axis=0
    )


def squares(pack):
    part = pack.shape[0] // 2
    return [square(pack[:, part * n : part * n + part]) for n in range(3)]


def fetch(place, own, other, dest, sem, shards):
    core, fsdp = place[0], place[1]
    copies = []
    for n, f in enumerate(shards):
        at = ((f & 1) ^ (fsdp & 1), (f >> 1) ^ (fsdp >> 1))
        base = n * 2 * own.shape[2]
        for source, c in ((own, core), (other, 1 - core)):
            rows = pl.ds(pl.multiple_of(base + c * own.shape[2], 16), own.shape[2])
            copies.append(pltpu.make_async_copy(source.at[at[0], at[1]], dest.at[rows, :], sem))
    for copy in copies:
        copy.start()
    return copies


def mask_tables(marks):
    turned = jnp.concatenate([marks, jnp.zeros((4, marks.shape[1]), F32)], axis=0).T
    codes = jnp.concatenate([turned[:, n : n + 1] for n in range(4)], axis=0)
    length = codes.shape[0]
    codes = jnp.broadcast_to(codes, (length, 128))
    lane = lanes((length, 128)).astype(F32)
    real = codes == lane * 2 + 1
    mine = real | (codes == lane * 2)
    lives = jnp.max(jnp.where(real, 1.0, 0.0), axis=0, keepdims=True)
    hot = jnp.where(mine, jnp.broadcast_to(lives, (length, 128)), 0.0)
    alive = jnp.max(hot, axis=1, keepdims=True)
    row = jnp.where(lane == 6, jnp.broadcast_to(alive, (length, 128)), hot)
    col = jnp.where(real, 0.0, jnp.where(lane < 3, -BIG, jnp.where(lane < 6, 1.0, 0.0)))
    return row.astype(BF), col.astype(BF)


def wide_at(pair):
    return pl.ds(pl.multiple_of(128 * pair, 128), 128)


def attend_kernel(which, place, *refs):
    slots, refs = refs[:4], refs[4:]
    own_ref, other_ref, *refs = refs
    if which:
        *given, refs = *refs[:2], refs[2:]
    (
        x_ref, q_ref, k_ref, v_ref, mix_ref, low_ref, lse_ref, pack_ref,
        *tables, queries, keys, values, qaug, kaug, vaug, peak, wide, sem,
    ) = refs
    row_ref, col_ref = given if which else tables
    length = x_ref.shape[0]
    span = length // 4
    pair = pl.program_id(0)

    @pl.when(pair == 0)
    def _():
        copies = fetch(place, own_ref, other_ref, pack_ref, sem, range(4 * which, 4 * which + 4))
        for n, slot in enumerate(slots):
            x_ref[span * n : span * n + span, :] = slot[:span, :]
        if not which:
            marks = jnp.concatenate([slot[span : span + 8, :span].astype(F32)[:1] for slot in slots], axis=0)
            row_ref[...], col_ref[...] = mask_tables(marks)
        vaug[:, 128:] = jnp.ones((length, 128), BF)
        for head in range(2):
            kaug[head, :, 128:] = col_ref[...]
        peak[...] = jnp.zeros_like(peak)
        for copy in copies:
            copy.wait()
        line = pack_ref[:, 512:640].astype(F32).T
        x = x_ref[...]
        alive = row_ref[:, 6:7].astype(F32)
        wq, wk, wv = squares(pack_ref[...])
        queries[...] = ((mm(x, wq, NT) + line[64:65, :]) * alive).astype(BF)
        keys[...] = mm(x, wk, NT).astype(BF)
        values[...] = (mm(x, wv, NT) + line[65:66, :]).astype(BF)
        half = x_ref.shape[1]
        head_of = lax.broadcasted_iota(jnp.int32, (half, 128), 0) // HEAD == lanes((half, 128))
        sizes = []
        for ref in (queries, keys):
            v = ref[...].astype(F32)
            squared = (v * v).astype(BF)
            sizes.append(jnp.max(mm(squared, jnp.where(head_of, 1.0, 0.0).astype(BF), NN), axis=0, keepdims=True))
        limit = (90.0 * HEAD**0.5 / LOG2E) ** 2
        wide[0] = jnp.where(jnp.max(sizes[0] * sizes[1]) > limit, 1, 0)

    cut = wide_at(pair)
    q, k = queries[:, cut], keys[:, cut]
    q_ref[...], k_ref[...], v_ref[...] = q, k, values[:, cut]
    low = lanes((length, 128)) < 64
    q_parts = query_parts(q, low)
    k_parts = key_parts(k, low)
    vaug[:, :128] = values[:, cut]
    for head in range(2):
        qaug[head, :, :128] = q_parts[head]
        qaug[head, :, 128:] = row_ref[...]
        kaug[head, :, :128] = k_parts[head]

        @pl.when(wide[0] == 1)
        def _():
            rows = 128
            lane = lanes((rows, 128))

            def shift(step, carry):
                at = pl.ds(pl.multiple_of(step * rows, rows), rows)
                top = jnp.max(mm(qaug[head, at, :], kaug[head], NT), axis=1, keepdims=True)
                top = jnp.broadcast_to(top, (rows, 128))
                peak[head, at, :] = top
                t1, t2, t3 = split3(-top)
                info = qaug[head, at, 128:]
                qaug[head, at, 128:] = jnp.where(
                    lane == 3, t1, jnp.where(lane == 4, t2, jnp.where(lane == 5, t3, info))
                )
                return carry

            lax.fori_loop(0, length // rows, shift, 0)

    rows = 512
    left = lanes((rows, 128)) < 64

    def block(step, carry):
        at = pl.ds(pl.multiple_of(step * rows, rows), rows)
        found = []
        for head in range(2):
            powers = jnp.exp2(mm(qaug[head, at, :], kaug[head], NT)).astype(BF)
            both = mm(powers, vaug[...], NN)
            found.append((both[:, :128] / both[:, 128:], peak[head, at, :] + jnp.log2(both[:, 128:])))
        mixed = jnp.where(left, found[0][0], found[1][0])
        mix_ref[at, :], low_ref[at, :] = split2(mixed)
        lse_ref[at, :] = jnp.where(left, found[0][1], found[1][1])
        return carry

    lax.fori_loop(0, length // rows, block, 0)


def attend_forward(which, place, slots, span, tables, own, other):
    half = slots[0].shape[1]
    length = span * len(slots)
    whole = pl.BlockSpec(memory_space=pltpu.VMEM)
    hbm = pl.BlockSpec(memory_space=pl.ANY)
    pair = pl.BlockSpec((length, 128), lambda i: (0, i))
    shapes = [((length, half), BF)] * 6 + [((length, half), F32)]
    shapes += [((half, own.shape[-1]), BF)]
    if not which:
        shapes += [((length, 128), BF)] * 2
    return pl.pallas_call(
        functools.partial(attend_kernel, which),
        grid=(half // 128,),
        in_specs=[pl.BlockSpec(memory_space=pltpu.SMEM), *[whole] * 4, hbm, hbm, *[whole] * len(tables)],
        out_specs=[whole, *[pair] * 6, *[whole] * (len(shapes) - 7)],
        out_shape=[jax.ShapeDtypeStruct(*s) for s in shapes],
        scratch_shapes=[
            *[pltpu.VMEM((length, half), BF)] * 3,
            pltpu.VMEM((2, length, 256), BF),
            pltpu.VMEM((2, length, 256), BF),
            pltpu.VMEM((length, 256), BF),
            pltpu.VMEM((2, length, 128), F32),
            pltpu.SMEM((1,), jnp.int32),
            pltpu.SemaphoreType.DMA,
        ],
        compiler_params=pltpu.CompilerParams(vmem_limit_bytes=56 << 20),
        cost_estimate=pl.CostEstimate(flops=20_000_000_000, transcendentals=0, bytes_accessed=8_000_000),
        name="attend_forward",
    )(place, *slots, own, other, *tables)


def mean(v):
    return jnp.sum(v, axis=1, keepdims=True) * (1.0 / v.shape[1])


def total(v):
    return jnp.sum(v, axis=0, keepdims=True)


def leave_piece(place, grads, owner, piece):
    x, z = place[1] & 1, place[1] >> 1
    at = ((owner % 2) ^ place[0], (owner // 4 % 2) ^ x, (owner // 8) ^ z, (owner // 2 % 2) ^ place[2])
    grads[at] = piece.astype(BF)


def move(pairs, sem):
    copies = [pltpu.make_async_copy(source, dest, sem) for source, dest in pairs]
    for copy in copies:
        copy.start()
    for copy in copies:
        copy.wait()


def gelu_parts(x):
    return 0.5 * lax.erf(x * 0.7071067811865476) + 0.5, jnp.exp2(x * x * (-0.5 * LOG2E)) * 0.3989422804014327


def middle_kernel(
    place, xa_ref, xb_ref, mixa_ref, mixb_ref, cot0, cot1, cot2, cot3, own_ref, other_ref,
    out0, out1, out2, out3, gres_ref, gmix_ref, keep_ref, send_ref,
    slope, dwe_acc, dwo_ref, dwr_ref, cots, pack, we_ref, line_ref, be_ref, sums, grads, sems, sem,
):
    step = pl.program_id(0)
    rows, span = xa_ref.shape[0], cot0.shape[0]
    width = pack.shape[0]
    part = width // GROUPS
    deep = width
    wo_ref = pack.at[:, :width]
    wr_ref = pack.at[:, width : 2 * width]
    bo_ref, g1_ref, s1_ref, br_ref, g2_ref, s2_ref = (line_ref.at[n : n + 1, :] for n in range(1, 7))
    dbo_ref, dg1_ref, ds1_ref, dbr_ref, dg2_ref, ds2_ref = (sums.at[n : n + 1, :] for n in range(6))

    @pl.when(step == 0)
    def _():
        for n, ref in enumerate((cot0, cot1, cot2, cot3)):
            pltpu.make_async_copy(ref, cots.at[span * n : span * n + span, :], sems.at[n]).start()
        copies = fetch(place, own_ref, other_ref, pack, sem, range(8))
        for ref in (dwo_ref, dwr_ref, dwe_acc, sums):
            ref[...] = jnp.zeros_like(ref)
        for copy in copies:
            copy.wait()
        line_ref[...] = pack[:, 2 * width + 128 : 2 * width + 256].astype(F32).T[64:72]
        for f in range(8):
            for j in range(4):
                we_ref[384 * f + 96 * j : 384 * f + 96 * j + 96, :] = pack[
                    96 * f : 96 * f + 96, 2 * width + 256 * j : 2 * width + 256 * j + 256
                ]
        for g in range(GROUPS):
            be_ref[:, deep * g : deep * g + deep] = we_ref[deep * g : deep * g + deep, 128:].astype(F32).T[64:65]

    for n in range(rows // span):
        pltpu.make_async_copy(cot0, cots.at[:span, :], sems.at[step * (rows // span) + n]).wait()
    few = rows // 2
    ones = jnp.ones((few, 64), BF)
    outs = []

    def block(n):
        at = slice(few * n, few * n + few)
        mixed = jnp.concatenate([mixa_ref[at, :], mixb_ref[at, :]], axis=1)
        rows_in = jnp.concatenate([xa_ref[at, :], xb_ref[at, :]], axis=1)
        residual = rows_in.astype(F32) + mm(mixed, wo_ref[...], NT) + bo_ref[...]
        yield
        centred = residual - mean(residual)
        rate1 = lax.rsqrt(mean(centred * centred) + EPS)
        hat1 = centred * rate1
        normed = hat1 * g1_ref[...] + s1_ref[...]
        normed_low = normed.astype(BF)
        yield
        acts, branches = [], []
        for g in range(GROUPS):
            piece = normed_low[:, part * g : part * g + part]
            tall = slice(deep * g, deep * g + deep)
            pre = mm(piece, we_ref[tall, :part], NT) + be_ref[:, tall]
            upper, density = gelu_parts(pre)
            acts.append((pre * upper).astype(BF))
            slope[at, tall] = upper + pre * density
            branches.append(mm(acts[g], wr_ref[part * g : part * g + part, :], NT))
        second = normed + jnp.concatenate(branches, axis=1) + br_ref[...]
        yield
        centred = second - mean(second)
        rate2 = lax.rsqrt(mean(centred * centred) + EPS)
        hat2 = centred * rate2
        outs.append((hat2 * g2_ref[...] + s2_ref[...]).astype(BF))
        cot = cots[pl.ds(pl.multiple_of(step * rows + few * n, few), few), :].astype(F32)
        dg2_ref[...] += total(cot * hat2)
        ds2_ref[...] += total(cot)
        e = cot * g2_ref[...]
        grad_second = rate2 * (e - mean(e) - hat2 * mean(e * hat2))
        grad_branch = grad_second.astype(BF)
        dbr_ref[...] += total(grad_branch.astype(F32))
        yield
        backs = []
        for g in range(GROUPS):
            narrow = slice(part * g, part * g + part)
            tall = slice(deep * g, deep * g + deep)
            piece = grad_branch[:, narrow]
            dwr_ref[narrow, :] += mm(piece, acts[g], TN)
            grad_pre = mm(piece, wr_ref[narrow, :], NN) * slope[at, tall]
            grad_pre_low = grad_pre.astype(BF)
            dwe_acc[g] += mm(jnp.concatenate([normed_low[:, narrow], ones], axis=1), grad_pre_low, TN)
            backs.append(mm(grad_pre_low, we_ref[tall, :part], NN))
        grad_normed = grad_second + jnp.concatenate(backs, axis=1)
        yield
        dg1_ref[...] += total(grad_normed * hat1)
        ds1_ref[...] += total(grad_normed)
        e = grad_normed * g1_ref[...]
        grad_residual = rate1 * (e - mean(e) - hat1 * mean(e * hat1))
        gres_ref[at, :] = grad_residual
        grad_projected = grad_residual.astype(BF)
        dbo_ref[...] += total(grad_projected.astype(F32))
        yield
        dwo_ref[...] += mm(grad_projected, mixed, TN)
        gmix_ref[at, :] = mm(grad_projected, wo_ref[...], NN).astype(BF)

    halves = [block(0), block(1)]
    for _ in range(7):
        for half in halves:
            next(half, None)
    out = jnp.concatenate(outs, axis=0)
    for n, ref in enumerate((out0, out1, out2, out3)):

        @pl.when(step == n * span // rows)
        def _():
            ref[...] = out[n * span % rows : n * span % rows + span, :]

    @pl.when(step == pl.num_programs(0) - 1)
    def _():
        low = jnp.zeros((72, width), F32)
        side = jnp.concatenate([low, sums[...], jnp.zeros((48, width), F32)], axis=0).T
        lane = lanes((24, 128))
        for g in range(GROUPS):
            tall = dwe_acc[g].T
            for n in range(8):
                owner = 8 * g + n
                few_rows = slice(24 * owner, 24 * owner + 24)
                turns = [tall[96 * n + 24 * j : 96 * n + 24 * j + 24] for j in range(4)]
                last = jnp.where(lane < 72, turns[0][:, 128:], side[few_rows])
                piece = jnp.concatenate(
                    [dwo_ref[few_rows, :], dwr_ref[few_rows, :], turns[0][:, :128], last, *turns[1:]], axis=1
                )
                leave_piece(place, grads, owner, piece)
        move(((grads.at[0], keep_ref), (grads.at[1], send_ref)), sem)


def middle(place, halves, mixed, cots, own, other):
    span, width = cots[0].shape
    length = span * len(cots)
    rows = 2 * span
    deep = width * GROUPS
    tokens = pl.BlockSpec((rows, width), lambda i: (i, 0))
    half = pl.BlockSpec((rows, width // 2), lambda i: (i, 0))
    whole = pl.BlockSpec(memory_space=pltpu.VMEM)
    hbm = pl.BlockSpec(memory_space=pl.ANY)
    return pl.pallas_call(
        middle_kernel,
        grid=(length // rows,),
        in_specs=[pl.BlockSpec(memory_space=pltpu.SMEM), *[half] * 4, *[hbm] * 6],
        out_specs=[*[whole] * 4, tokens, tokens, hbm, hbm],
        out_shape=[
            *[jax.ShapeDtypeStruct((span, width), BF)] * 4,
            jax.ShapeDtypeStruct((length, width), F32),
            jax.ShapeDtypeStruct((length, width), BF),
            *[jax.ShapeDtypeStruct((2, 4, 2, 24, 2 * width + 1024), BF)] * 2,
        ],
        scratch_shapes=[
            pltpu.VMEM((rows, deep), F32),
            pltpu.VMEM((GROUPS, width // GROUPS + 64, width), F32),
            pltpu.VMEM((width, width), F32),
            pltpu.VMEM((width, width), F32),
            pltpu.VMEM((length, width), BF),
            pltpu.VMEM((width, own.shape[-1]), BF),
            pltpu.VMEM((deep, 256), BF),
            pltpu.VMEM((8, width), F32),
            pltpu.VMEM((1, deep), F32),
            pltpu.VMEM((8, width), F32),
            pltpu.VMEM((2, 2, 4, 2, 24, 2 * width + 1024), BF),
            pltpu.SemaphoreType.DMA((len(cots),)),
            pltpu.SemaphoreType.DMA,
        ],
        compiler_params=pltpu.CompilerParams(vmem_limit_bytes=56 << 20),
        cost_estimate=pl.CostEstimate(flops=40_000_000_000, transcendentals=0, bytes_accessed=16_000_000),
        name="middle",
    )(place, *halves, *mixed, *cots, own, other)


def back_kernel(
    which, place, q_ref, k_ref, v_ref, mix_ref, low_ref, gmix_ref, lse_ref, row_ref, col_ref, *refs,
):
    step = pl.program_id(0)
    length = q_ref.shape[0]
    x_ref, gres_ref, pack_ref, *refs = refs
    before, refs = refs[: 2 * which], refs[2 * which :]
    *ghids, keep_ref, send_ref = refs[:6]
    *refs, dq, dk, dv, grads, sem = refs[6:]
    outs = [ref.at[:, wide_at(step)] for ref in (dq, dk, dv)]
    qaug, kaug, vaug, gaug, qmine, dq_acc = refs

    @pl.when(step == 0)
    def _():
        vaug[:, 128:] = jnp.ones((length, 128), BF)
        for head in range(2):
            kaug[head, :, 128:] = col_ref[...]

    rows = 256
    low = lanes((length, 128)) < 64
    lane = lanes((length, 128))
    alive = row_ref[:, 6:7].astype(F32)
    scale = HEAD**-0.5
    zero = jnp.zeros((length, 128), BF)
    q_parts = query_parts(q_ref[...], low)
    k_parts = key_parts(k_ref[...], low)
    grad = gmix_ref[...]
    prod = grad.astype(F32) * (mix_ref[...].astype(F32) + low_ref[...].astype(F32))
    lse = lse_ref[...]
    turned = pltpu.roll(lse, 64, 1)
    vaug[:, :128] = v_ref[...]
    for head in range(2):
        mine = low if head == 0 else ~low
        dot = jnp.sum(jnp.where(mine, prod, 0.0), axis=1, keepdims=True)
        d1, d2, d3 = split3(jnp.broadcast_to(-dot, (length, 128)))
        l1, l2, l3 = split3(-jnp.where(mine, lse, turned))
        qaug[head, :, :128] = q_parts[head]
        qaug[head, :, 128:] = jnp.where(
            lane == 3, l1, jnp.where(lane == 4, l2, jnp.where(lane == 5, l3, row_ref[...]))
        )
        kaug[head, :, :128] = k_parts[head]
        gaug[head, :, :128] = jnp.where(mine, grad, zero)
        gaug[head, :, 128:] = jnp.where(
            lane == 0, d1, jnp.where(lane == 1, d2, jnp.where(lane == 2, d3, zero))
        )
    dq_acc[...] = jnp.zeros_like(dq_acc)
    near = lanes((rows, 128)) < 64
    for head in range(2):
        mine = low if head == 0 else ~low
        qmine[head] = jnp.where(mine, q_ref[...], zero)

    def block(turn_, carry):
        at = pl.ds(pl.multiple_of(turn_ * rows, rows), rows)
        all_probs, all_grads, all_keys = [], [], []
        for head in range(2):
            probs = jnp.exp2(mm(kaug[head, at, :], qaug[head], NT))
            slopes = mm(vaug[at, :], gaug[head], NT)
            all_grads.append((probs * slopes).astype(BF))
            all_probs.append(probs.astype(BF))
            keys = k_ref[at, :]
            none = jnp.zeros_like(keys)
            all_keys.append(jnp.where(near, keys, none) if head == 0 else jnp.where(near, none, keys))
        d_value = mm(all_probs[0], gaug[0, :, :128], NN) + mm(all_probs[1], gaug[1, :, :128], NN)
        d_key = mm(all_grads[0], qmine[0], NN) + mm(all_grads[1], qmine[1], NN)
        dq_acc[...] += mm(jnp.concatenate(all_grads, axis=0), jnp.concatenate(all_keys, axis=0), TN)
        outs[1][at, :] = (d_key * scale).astype(BF)
        outs[2][at, :] = d_value.astype(BF)
        return carry

    lax.fori_loop(0, length // rows, block, 0)
    outs[0][...] = (dq_acc[...] * (alive * scale)).astype(BF)

    @pl.when(step == pl.num_programs(0) - 1)
    def _():
        move([(old, grads.at[n]) for n, old in enumerate(before)], sem)
        finish_heads(which, place, x_ref, gres_ref, pack_ref, dq, dk, dv, ghids, grads)
        move(((grads.at[0], keep_ref), (grads.at[1], send_ref)), sem)


def finish_heads(which, place, x_ref, gres_ref, pack_ref, dq, dk, dv, ghids, grads):
    length = x_ref.shape[0]
    span = length // 4
    wq, wk, wv = squares(pack_ref[...])
    ghid = (gres_ref[...] + mm(dq[...], wq, NN) + mm(dk[...], wk, NN) + mm(dv[...], wv, NN)).astype(BF)
    for n, ref in enumerate(ghids):
        ref[...] = ghid[span * n : span * n + span, :]
    part = x_ref.shape[1] // 2
    ones = jnp.ones((length, 128), BF)
    sums = []
    for grad in (dq, dk, dv):
        both = mm(grad[...], x_ref[...], TN)
        sums.append((both[:part, :part], both[part:, part:]))
    d_qb, d_vb = mm(dq[...], ones, TN), mm(dv[...], ones, TN)
    extra = jnp.where(lanes(d_qb.shape) == 0, d_qb, d_vb)[:, :64]
    for g in range(2):
        wide = jnp.concatenate([*(each[g] for each in sums), extra[part * g : part * g + part]], axis=1)
        for n in range(8):
            leave_piece(place, grads, 16 * which + 8 * g + n, wide[24 * n : 24 * n + 24])


def attend_backward(which, place, q, k, v, mixed, mixed_low, lse, gmix, row, col, x, gres, pack, before=()):
    length, half = q.shape
    pairs = half // 128
    base = which * pairs
    pair = pl.BlockSpec((length, 128), lambda i: (0, i))
    shifted = pl.BlockSpec((length, 128), lambda i: (0, base + i))
    whole = pl.BlockSpec(memory_space=pltpu.VMEM)
    scratch = [
        pltpu.VMEM((2, length, 256), BF),
        pltpu.VMEM((2, length, 256), BF),
        pltpu.VMEM((length, 256), BF),
        pltpu.VMEM((2, length, 256), BF),
        pltpu.VMEM((2, length, 128), BF),
        pltpu.VMEM((length, 128), F32),
    ]
    scratch += [pltpu.VMEM((length, half), BF)] * 3
    scratch += [pltpu.VMEM((2, 2, 4, 2, 24, pack.shape[1]), BF), pltpu.SemaphoreType.DMA]
    hbm = pl.BlockSpec(memory_space=pl.ANY)
    half_of = pl.BlockSpec((length, half), lambda i: (0, which))
    return pl.pallas_call(
        functools.partial(back_kernel, which),
        grid=(pairs,),
        in_specs=[pl.BlockSpec(memory_space=pltpu.SMEM), *[pair] * 5, shifted, pair, whole, whole, whole, half_of, whole, *[hbm] * len(before)],
        out_specs=[*[whole] * 4, hbm, hbm],
        out_shape=[
            *[jax.ShapeDtypeStruct((length // 4, half), BF)] * 4,
            *[jax.ShapeDtypeStruct((2, 4, 2, 24, pack.shape[1]), BF)] * 2,
        ],
        scratch_shapes=scratch,
        compiler_params=pltpu.CompilerParams(vmem_limit_bytes=56 << 20),
        cost_estimate=pl.CostEstimate(flops=12_000_000_000 * pairs, transcendentals=0, bytes_accessed=4_000_000),
        name="attend_backward",
    )(place, q, k, v, mixed, mixed_low, gmix, lse, row, col, x, gres, pack, *before)


def turn(v, axis, step, size):
    return lax.ppermute(v, axis, [(i, i ^ step) for i in range(size)])


def pick(v, index):
    return lax.dynamic_index_in_dim(v, index, 0, keepdims=False)


def swap_out(slots):
    return [slots[0]] + [turn(slots[m], "seq", m, 4) for m in range(1, 4)]


def placed(slots, seq):
    result = jnp.zeros((len(slots), *slots[0].shape), slots[0].dtype)
    for m, slot in enumerate(slots):
        result = lax.dynamic_update_index_in_dim(result, slot, seq ^ m, 0)
    return result


def pack_heads(wq, wk, wv, bq, bv):
    gap = jnp.zeros((wq.shape[0], 62), BF)
    return jnp.concatenate([wq, wk, wv, bq[:, None], bv[:, None], gap], axis=1)


def pack_deep(wo, wr, we, be, lines):
    rows, part = wo.shape[0], we.shape[1]
    tall = we.reshape(rows // 96, 4, 96, part)
    side = be.reshape(rows // 96, 4, 96)
    pieces = [wo, wr]
    for j in range(4):
        pieces += [tall[:, j].reshape(rows, part), side[:, j].reshape(rows, 1)]
        extra = lines if j == 0 else []
        pieces += [v[:, None] for v in extra] + [jnp.zeros((rows, 63 - len(extra)), BF)]
    return jnp.concatenate(pieces, axis=1)


def after(value, *others):
    return lax.optimization_barrier((value, others))[0]


def along_z(pack, core):
    piece = pick(pack.reshape(2, pack.shape[0] // 2, pack.shape[1]), core)
    return [piece] + [turn(piece, "fsdp", m, 8) for m in (2, 4, 6)]


def along_x(pieces):
    v = jnp.stack(pieces)
    return jnp.stack([v, turn(v, "fsdp", 1, 8)])


def split_whole(full):
    v = full.reshape(4, 2, 2, 48, full.shape[1]).transpose(2, 1, 0, 3, 4)
    return v[0], v[1]


def add_up(parts):
    result = parts[0].astype(F32)
    for part in parts[1:]:
        result = result + part.astype(F32)
    return result


STEPS = (
    ("seq", ((1, 1),), 4),
    ("fsdp", ((1, 1),), 8),
    ("fsdp", ((1, 2), (2, 4), (3, 6)), 8),
    ("seq", ((1, 2),), 4),
)


def scatter_step(parts, step):
    axis, hops, size = step
    came = [turn(add_up([p[m] for p in parts]).astype(BF), axis, hop, size) for m, hop in hops]
    return [p[0] for p in parts] + came


def open_deep(v, width):
    owners, part = v.shape[0] // 24, width // GROUPS
    tall = v[:, 2 * width :].reshape(owners, 24, 4, 256).transpose(0, 2, 1, 3).reshape(-1, 256)
    lines = [v[:, 2 * width + part + 8 + n] for n in range(6)]
    return v[:, :width], v[:, width : 2 * width], tall[:, :part], tall[:, part], lines


def open_heads(v, width):
    part = width // GROUPS
    return [v[:, part * n : part * n + part] for n in range(3)] + [v[:, 3 * part], v[:, 3 * part + 1]]


def local(mesh_shape, hidden, cotangent, segment_ids, pad_mask, *weights):
    micro, _, span, width = hidden.shape
    half = width // 2
    fsdp, seq = lax.axis_index("fsdp"), lax.axis_index("seq")
    core, y = seq & 1, seq >> 1
    near = mesh_shape["fsdp"] == 8
    (wq, wk, wv, bq, bv, wo, bo, g1, s1, we, be, wr, br, g2, s2) = weights
    lines = [bo, g1, s1, br, g2, s2]

    marks = (segment_ids * 2 + pad_mask)[:, 0].astype(BF)
    marks = jnp.pad(marks[:, None, :], ((0, 0), (0, 7), (0, half - span)))
    first = jnp.concatenate([hidden[:, 0, :, :half], marks], axis=1)
    second = hidden[:, 0, :, half:]

    def swap_in(v):
        return [pick(v, seq)] + [turn(pick(v, seq ^ m), "seq", m, 4) for m in range(1, 4)]

    first = swap_in(first)
    if near:
        place = jnp.stack([core, fsdp, y])
        heads_z = along_z(pack_heads(wq, wk, wv, bq, bv), core)
        heads_own = along_x(heads_z)
        heads = heads_own, turn(heads_own, "seq", 1, 4)
        deep_z = along_z(after(pack_deep(wo, wr, we, be, lines), *heads_z), core)
    else:
        place = jnp.zeros((3,), jnp.int32)
        (wq, wk, wv, bq, bv, wo, bo, g1, s1, we, be, wr, br, g2, s2) = [
            lax.all_gather(w, "fsdp", axis=0, tiled=True) for w in weights
        ]
        heads = split_whole(pack_heads(wq, wk, wv, bq, bv))
        deep = split_whole(pack_deep(wo, wr, we, be, [bo, g1, s1, br, g2, s2]))
    second = swap_in(after(second, first))
    ahead = [attend_forward(0, place, after(first, second[1]), span, (), *heads)]
    tables = ahead[0][8:]
    cots = swap_in(after(cotangent[:, 0], second, tables))
    if near:
        deep_own = along_x(after(deep_z, second, tables))
    ahead.append(attend_forward(1, place, second, span, tables, *heads))
    if near:
        deep_own = after(deep_own, ahead[1][7], cots)
        deep = deep_own, turn(deep_own, "seq", 1, 4)
    xs, mixed = ([a[n] for a in ahead] for n in (0, 4))
    *out, gres, gmix, d_deep, d_deep_send = middle(place, xs, mixed, cots, *deep)
    out_slots = swap_out(out)

    def backward(n, gmix, before):
        xn, q, k, v, mix, mix_low, lse, pack = ahead[n][:8]
        return attend_backward(n, place, q, k, v, mix, mix_low, lse, gmix, *tables, xn, gres, pack, before)

    if near:
        d_deep = [d_deep, turn(d_deep_send, "seq", 1, 4)]
        d_deep, gmix = lax.optimization_barrier((d_deep, gmix))
        d_deep = scatter_step(d_deep, STEPS[1])
    *ghid, keep, send = backward(0, gmix, ())
    halves = [swap_out(ghid)]
    gmix = after(gmix, halves[0][1], d_deep, out_slots)
    if near:
        d_deep = scatter_step(d_deep, STEPS[2])
    *ghid, keep, send = backward(1, gmix, (keep, send))
    halves[0], d_deep, ghid = lax.optimization_barrier((halves[0], d_deep, ghid))
    halves.append(swap_out(ghid))
    if near:
        d_heads = [keep, turn(send, "seq", 1, 4)]
        d_deep = scatter_step(d_deep, STEPS[3])
        d_heads = scatter_step(d_heads, STEPS[1])
        d_deep, out_slots = after((d_deep, out_slots), d_heads)
        d_heads = scatter_step(d_heads, STEPS[2])
        halves[1] = after(halves[1], d_heads)
        d_heads = scatter_step(d_heads, STEPS[3])
    layer_out = placed(out_slots, seq)[:, None]
    grad_hidden = placed([jnp.concatenate(p, axis=1).astype(F32) for p in zip(*halves)], seq)[:, None]
    if near:
        dwo, dwr, dwe, dbe, d_lines = open_deep(add_up(d_deep), width)
        dwq, dwk, dwv, dbq, dbv = open_heads(add_up(d_heads), width)
    else:

        def natural(keep, send):
            return jnp.stack([keep, send]).transpose(2, 1, 3, 0, 4, 5).reshape(width, -1).astype(F32)

        dwo, dwr, dwe, dbe, d_lines = open_deep(natural(d_deep, d_deep_send), width)
        dwq, dwk, dwv, dbq, dbv = open_heads(natural(keep, send), width)

        def scatter(v):
            return lax.psum_scatter(v, ("fsdp", "seq"), scatter_dimension=0, tiled=True)

        dwq, dwk, dwv, dbq, dbv, dwo, dwr, dwe, dbe = (scatter(v) for v in (dwq, dwk, dwv, dbq, dbv, dwo, dwr, dwe, dbe))
        d_lines = [scatter(v) for v in d_lines]
    dbo, dg1, ds1, dbr, dg2, ds2 = d_lines
    return (
        layer_out, grad_hidden, dwq, dwk, dwv, dbq, dbv, dwo, dbo, dg1, ds1, dwe, dbe, dwr, dbr, dg2, ds2,
    )


def solution(mesh):
    tokens = P(None, "fsdp", "seq", None)
    marks = P(None, "fsdp", "seq")
    held, line = P("fsdp", None), P("fsdp")
    both, both_line = P(("fsdp", "seq"), None), P(("fsdp", "seq"))
    ranks = (2, 2, 2, 1, 1, 2, 1, 1, 1, 2, 1, 2, 1, 1, 1)
    in_specs = (tokens, tokens, marks, marks, *(held if n == 2 else line for n in ranks))
    out_specs = (tokens, tokens, *(both if n == 2 else both_line for n in ranks))
    return jax.shard_map(functools.partial(local, dict(mesh.shape)), mesh=mesh, in_specs=in_specs, out_specs=out_specs, check_vma=False)
```

```python
import functools

import jax
import jax.numpy as jnp
from jax import lax
from jax.experimental import pallas as pl
from jax.experimental.pallas import tpu as pltpu
from jax.sharding import PartitionSpec as P

GROUPS = 4
HEAD = 64
EPS = 1e-05
LOG2E = 1.4426950408889634
BIG = float(2**30)
BF = jnp.bfloat16
F32 = jnp.float32
NT = (((1,), (1,)), ((), ()))
NN = (((1,), (0,)), ((), ()))
TN = (((0,), (0,)), ((), ()))


def mm(a, b, dims):
    return lax.dot_general(a, b, dims, preferred_element_type=F32)


def split2(v):
    hi = v.astype(BF)
    return hi, (v - hi.astype(F32)).astype(BF)


def split3(v):
    hi = v.astype(BF)
    rest = v - hi.astype(F32)
    mid = rest.astype(BF)
    return hi, mid, (rest - mid.astype(F32)).astype(BF)


def lanes(shape):
    return lax.broadcasted_iota(jnp.int32, shape, 1)


def query_parts(q, low):
    scaled = q.astype(F32) * (LOG2E * HEAD**-0.5)
    hi, lo = split2(scaled)
    hi, lo = hi.astype(F32), lo.astype(F32)
    turned = pltpu.roll(lo, 64, 1)
    return (
        jnp.where(low, hi, turned).astype(BF),
        jnp.where(low, turned, hi).astype(BF),
    )


def key_parts(k, low):
    k = k.astype(F32)
    turned = pltpu.roll(k, 64, 1)
    return (
        jnp.where(low, k, turned).astype(BF),
        jnp.where(low, turned, k).astype(BF),
    )


def square(w):
    part = w.shape[1]
    zero = jnp.zeros((part, part), w.dtype)
    return jnp.concatenate(
        [jnp.concatenate([w[:part], zero], axis=1), jnp.concatenate([zero, w[part:]], axis=1)], axis=0
    )


def squares(pack):
    part = pack.shape[0] // 2
    return [square(pack[:, part * n : part * n + part]) for n in range(3)]


def fetch_parts(place, refs, dest, sem):
    core, fsdp = place[0], place[1]
    copies = []
    for z in range(4):
        for turned in range(2):
            f = (z ^ (fsdp >> 1)) * 2 + ((fsdp & 1) ^ turned)
            for n in range(2):
                source = refs[2 * n + turned].at[z]
                high = source.shape[0]
                rows = pl.ds(pl.multiple_of(f * 2 * high + (core ^ n) * high, 16), high)
                copies.append(pltpu.make_async_copy(source, dest.at[rows, :], sem))
    for copy in copies:
        copy.start()
    return copies


def fetch(place, own, other, dest, sem, shards):
    core, fsdp = place[0], place[1]
    copies = []
    for n, f in enumerate(shards):
        at = ((f & 1) ^ (fsdp & 1), (f >> 1) ^ (fsdp >> 1))
        base = n * 2 * own.shape[2]
        for source, c in ((own, core), (other, 1 - core)):
            rows = pl.ds(pl.multiple_of(base + c * own.shape[2], 16), own.shape[2])
            copies.append(pltpu.make_async_copy(source.at[at[0], at[1]], dest.at[rows, :], sem))
    for copy in copies:
        copy.start()
    return copies


def mask_tables(marks):
    turned = jnp.concatenate([marks, jnp.zeros((4, marks.shape[1]), F32)], axis=0).T
    codes = jnp.concatenate([turned[:, n : n + 1] for n in range(4)], axis=0)
    length = codes.shape[0]
    codes = jnp.broadcast_to(codes, (length, 128))
    lane = lanes((length, 128)).astype(F32)
    real = codes == lane * 2 + 1
    mine = real | (codes == lane * 2)
    lives = jnp.max(jnp.where(real, 1.0, 0.0), axis=0, keepdims=True)
    hot = jnp.where(mine, jnp.broadcast_to(lives, (length, 128)), 0.0)
    alive = jnp.max(hot, axis=1, keepdims=True)
    row = jnp.where(lane == 6, jnp.broadcast_to(alive, (length, 128)), hot)
    col = jnp.where(real, 0.0, jnp.where(lane < 3, -BIG, jnp.where(lane < 6, 1.0, 0.0)))
    return row.astype(BF), col.astype(BF)


def wide_at(pair):
    return pl.ds(pl.multiple_of(128 * pair, 128), 128)


def attend_kernel(which, place, *refs):
    slots, refs = refs[:4], refs[4:]
    own_ref, other_ref, *refs = refs
    if which:
        *given, refs = *refs[:2], refs[2:]
    (
        x_ref, q_ref, k_ref, v_ref, mix_ref, low_ref, lse_ref, pack_ref,
        *tables, queries, keys, values, qaug, kaug, vaug, peak, wide, sem,
    ) = refs
    row_ref, col_ref = given if which else tables
    length = x_ref.shape[0]
    span = length // 4
    pair = pl.program_id(0)

    @pl.when(pair == 0)
    def _():
        copies = fetch(place, own_ref, other_ref, pack_ref, sem, range(4 * which, 4 * which + 4))
        for n, slot in enumerate(slots):
            x_ref[span * n : span * n + span, :] = slot[:span, :]
        if not which:
            marks = jnp.concatenate([slot[span : span + 8, :span].astype(F32)[:1] for slot in slots], axis=0)
            row_ref[...], col_ref[...] = mask_tables(marks)
        vaug[:, 128:] = jnp.ones((length, 128), BF)
        for head in range(2):
            kaug[head, :, 128:] = col_ref[...]
        peak[...] = jnp.zeros_like(peak)
        for copy in copies:
            copy.wait()
        line = pack_ref[:, 512:640].astype(F32).T
        x = x_ref[...]
        alive = row_ref[:, 6:7].astype(F32)
        wq, wk, wv = squares(pack_ref[...])
        queries[...] = ((mm(x, wq, NT) + line[64:65, :]) * alive).astype(BF)
        keys[...] = mm(x, wk, NT).astype(BF)
        values[...] = (mm(x, wv, NT) + line[65:66, :]).astype(BF)
        half = x_ref.shape[1]
        head_of = lax.broadcasted_iota(jnp.int32, (half, 128), 0) // HEAD == lanes((half, 128))
        sizes = []
        for ref in (queries, keys):
            v = ref[...].astype(F32)
            squared = (v * v).astype(BF)
            sizes.append(jnp.max(mm(squared, jnp.where(head_of, 1.0, 0.0).astype(BF), NN), axis=0, keepdims=True))
        limit = (90.0 * HEAD**0.5 / LOG2E) ** 2
        wide[0] = jnp.where(jnp.max(sizes[0] * sizes[1]) > limit, 1, 0)

    cut = wide_at(pair)
    q, k = queries[:, cut], keys[:, cut]
    q_ref[...], k_ref[...], v_ref[...] = q, k, values[:, cut]
    low = lanes((length, 128)) < 64
    q_parts = query_parts(q, low)
    k_parts = key_parts(k, low)
    vaug[:, :128] = values[:, cut]
    for head in range(2):
        qaug[head, :, :128] = q_parts[head]
        qaug[head, :, 128:] = row_ref[...]
        kaug[head, :, :128] = k_parts[head]

        @pl.when(wide[0] == 1)
        def _():
            rows = 128
            lane = lanes((rows, 128))

            def shift(step, carry):
                at = pl.ds(pl.multiple_of(step * rows, rows), rows)
                top = jnp.max(mm(qaug[head, at, :], kaug[head], NT), axis=1, keepdims=True)
                top = jnp.broadcast_to(top, (rows, 128))
                peak[head, at, :] = top
                t1, t2, t3 = split3(-top)
                info = qaug[head, at, 128:]
                qaug[head, at, 128:] = jnp.where(
                    lane == 3, t1, jnp.where(lane == 4, t2, jnp.where(lane == 5, t3, info))
                )
                return carry

            lax.fori_loop(0, length // rows, shift, 0)

    rows = 512
    left = lanes((rows, 128)) < 64

    def block(step, carry):
        at = pl.ds(pl.multiple_of(step * rows, rows), rows)
        found = []
        for head in range(2):
            powers = jnp.exp2(mm(qaug[head, at, :], kaug[head], NT)).astype(BF)
            both = mm(powers, vaug[...], NN)
            found.append((both[:, :128] / both[:, 128:], peak[head, at, :] + jnp.log2(both[:, 128:])))
        mixed = jnp.where(left, found[0][0], found[1][0])
        mix_ref[at, :], low_ref[at, :] = split2(mixed)
        lse_ref[at, :] = jnp.where(left, found[0][1], found[1][1])
        return carry

    lax.fori_loop(0, length // rows, block, 0)


def attend_forward(which, place, slots, span, tables, own, other):
    half = slots[0].shape[1]
    length = span * len(slots)
    whole = pl.BlockSpec(memory_space=pltpu.VMEM)
    hbm = pl.BlockSpec(memory_space=pl.ANY)
    pair = pl.BlockSpec((length, 128), lambda i: (0, i))
    shapes = [((length, half), BF)] * 6 + [((length, half), F32)]
    shapes += [((half, own.shape[-1]), BF)]
    if not which:
        shapes += [((length, 128), BF)] * 2
    return pl.pallas_call(
        functools.partial(attend_kernel, which),
        grid=(half // 128,),
        in_specs=[pl.BlockSpec(memory_space=pltpu.SMEM), *[whole] * 4, hbm, hbm, *[whole] * len(tables)],
        out_specs=[whole, *[pair] * 6, *[whole] * (len(shapes) - 7)],
        out_shape=[jax.ShapeDtypeStruct(*s) for s in shapes],
        scratch_shapes=[
            *[pltpu.VMEM((length, half), BF)] * 3,
            pltpu.VMEM((2, length, 256), BF),
            pltpu.VMEM((2, length, 256), BF),
            pltpu.VMEM((length, 256), BF),
            pltpu.VMEM((2, length, 128), F32),
            pltpu.SMEM((1,), jnp.int32),
            pltpu.SemaphoreType.DMA,
        ],
        compiler_params=pltpu.CompilerParams(vmem_limit_bytes=56 << 20),
        cost_estimate=pl.CostEstimate(flops=20_000_000_000, transcendentals=0, bytes_accessed=8_000_000),
        name="attend_forward",
    )(place, *slots, own, other, *tables)


def mean(v):
    return jnp.sum(v, axis=1, keepdims=True) * (1.0 / v.shape[1])


def total(v):
    return jnp.sum(v, axis=0, keepdims=True)


def leave_piece(place, grads, owner, piece):
    x, z = place[1] & 1, place[1] >> 1
    at = ((owner % 2) ^ place[0], (owner // 4 % 2) ^ x, (owner // 8) ^ z, (owner // 2 % 2) ^ place[2])
    grads[at] = piece.astype(BF)


def move(pairs, sem):
    copies = [pltpu.make_async_copy(source, dest, sem) for source, dest in pairs]
    for copy in copies:
        copy.start()
    for copy in copies:
        copy.wait()


def gelu_parts(x):
    return 0.5 * lax.erf(x * 0.7071067811865476) + 0.5, jnp.exp2(x * x * (-0.5 * LOG2E)) * 0.3989422804014327


def middle_kernel(
    place, xa_ref, xb_ref, mixa_ref, mixb_ref, cot0, cot1, cot2, cot3, deep0, deep1, deep2, deep3,
    out0, out1, out2, out3, gres_ref, gmix_ref, keep_ref, send_ref,
    slope, dwe_acc, dwo_ref, dwr_ref, cots, pack, we_ref, line_ref, be_ref, sums, grads, sems, sem,
):
    step = pl.program_id(0)
    rows, span = xa_ref.shape[0], cot0.shape[0]
    width = pack.shape[0]
    part = width // GROUPS
    deep = width
    wo_ref = pack.at[:, :width]
    wr_ref = pack.at[:, width : 2 * width]
    bo_ref, g1_ref, s1_ref, br_ref, g2_ref, s2_ref = (line_ref.at[n : n + 1, :] for n in range(1, 7))
    dbo_ref, dg1_ref, ds1_ref, dbr_ref, dg2_ref, ds2_ref = (sums.at[n : n + 1, :] for n in range(6))

    @pl.when(step == 0)
    def _():
        for n, ref in enumerate((cot0, cot1, cot2, cot3)):
            pltpu.make_async_copy(ref, cots.at[span * n : span * n + span, :], sems.at[n]).start()
        copies = fetch_parts(place, (deep0, deep1, deep2, deep3), pack, sem)
        for ref in (dwo_ref, dwr_ref, dwe_acc, sums):
            ref[...] = jnp.zeros_like(ref)
        for copy in copies:
            copy.wait()
        line_ref[...] = pack[:, 2 * width + 128 : 2 * width + 256].astype(F32).T[64:72]
        for f in range(8):
            for j in range(4):
                we_ref[384 * f + 96 * j : 384 * f + 96 * j + 96, :] = pack[
                    96 * f : 96 * f + 96, 2 * width + 256 * j : 2 * width + 256 * j + 256
                ]
        for g in range(GROUPS):
            be_ref[:, deep * g : deep * g + deep] = we_ref[deep * g : deep * g + deep, 128:].astype(F32).T[64:65]

    for n in range(rows // span):
        pltpu.make_async_copy(cot0, cots.at[:span, :], sems.at[step * (rows // span) + n]).wait()
    few = rows // 2
    ones = jnp.ones((few, 64), BF)
    outs = []

    def block(n):
        at = slice(few * n, few * n + few)
        mixed = jnp.concatenate([mixa_ref[at, :], mixb_ref[at, :]], axis=1)
        rows_in = jnp.concatenate([xa_ref[at, :], xb_ref[at, :]], axis=1)
        residual = rows_in.astype(F32) + mm(mixed, wo_ref[...], NT) + bo_ref[...]
        yield
        centred = residual - mean(residual)
        rate1 = lax.rsqrt(mean(centred * centred) + EPS)
        hat1 = centred * rate1
        normed = hat1 * g1_ref[...] + s1_ref[...]
        normed_low = normed.astype(BF)
        yield
        acts, branches = [], []
        for g in range(GROUPS):
            piece = normed_low[:, part * g : part * g + part]
            tall = slice(deep * g, deep * g + deep)
            pre = mm(piece, we_ref[tall, :part], NT) + be_ref[:, tall]
            upper, density = gelu_parts(pre)
            acts.append((pre * upper).astype(BF))
            slope[at, tall] = upper + pre * density
            branches.append(mm(acts[g], wr_ref[part * g : part * g + part, :], NT))
        second = normed + jnp.concatenate(branches, axis=1) + br_ref[...]
        yield
        centred = second - mean(second)
        rate2 = lax.rsqrt(mean(centred * centred) + EPS)
        hat2 = centred * rate2
        outs.append((hat2 * g2_ref[...] + s2_ref[...]).astype(BF))
        cot = cots[pl.ds(pl.multiple_of(step * rows + few * n, few), few), :].astype(F32)
        dg2_ref[...] += total(cot * hat2)
        ds2_ref[...] += total(cot)
        e = cot * g2_ref[...]
        grad_second = rate2 * (e - mean(e) - hat2 * mean(e * hat2))
        grad_branch = grad_second.astype(BF)
        dbr_ref[...] += total(grad_branch.astype(F32))
        yield
        backs = []
        for g in range(GROUPS):
            narrow = slice(part * g, part * g + part)
            tall = slice(deep * g, deep * g + deep)
            piece = grad_branch[:, narrow]
            dwr_ref[narrow, :] += mm(piece, acts[g], TN)
            grad_pre = mm(piece, wr_ref[narrow, :], NN) * slope[at, tall]
            grad_pre_low = grad_pre.astype(BF)
            dwe_acc[g] += mm(jnp.concatenate([normed_low[:, narrow], ones], axis=1), grad_pre_low, TN)
            backs.append(mm(grad_pre_low, we_ref[tall, :part], NN))
        grad_normed = grad_second + jnp.concatenate(backs, axis=1)
        yield
        dg1_ref[...] += total(grad_normed * hat1)
        ds1_ref[...] += total(grad_normed)
        e = grad_normed * g1_ref[...]
        grad_residual = rate1 * (e - mean(e) - hat1 * mean(e * hat1))
        gres_ref[at, :] = grad_residual
        grad_projected = grad_residual.astype(BF)
        dbo_ref[...] += total(grad_projected.astype(F32))
        yield
        dwo_ref[...] += mm(grad_projected, mixed, TN)
        gmix_ref[at, :] = mm(grad_projected, wo_ref[...], NN).astype(BF)

    halves = [block(0), block(1)]
    for _ in range(7):
        for half in halves:
            next(half, None)
    out = jnp.concatenate(outs, axis=0)
    for n, ref in enumerate((out0, out1, out2, out3)):

        @pl.when(step == n * span // rows)
        def _():
            ref[...] = out[n * span % rows : n * span % rows + span, :]

    @pl.when(step == pl.num_programs(0) - 1)
    def _():
        low = jnp.zeros((72, width), F32)
        side = jnp.concatenate([low, sums[...], jnp.zeros((48, width), F32)], axis=0).T
        lane = lanes((24, 128))
        for g in range(GROUPS):
            tall = dwe_acc[g].T
            for n in range(8):
                owner = 8 * g + n
                few_rows = slice(24 * owner, 24 * owner + 24)
                turns = [tall[96 * n + 24 * j : 96 * n + 24 * j + 24] for j in range(4)]
                last = jnp.where(lane < 72, turns[0][:, 128:], side[few_rows])
                piece = jnp.concatenate(
                    [dwo_ref[few_rows, :], dwr_ref[few_rows, :], turns[0][:, :128], last, *turns[1:]], axis=1
                )
                leave_piece(place, grads, owner, piece)
        move(((grads.at[0], keep_ref), (grads.at[1], send_ref)), sem)


def middle(place, halves, mixed, cots, parts):
    span, width = cots[0].shape
    length = span * len(cots)
    rows = 2 * span
    deep = width * GROUPS
    tokens = pl.BlockSpec((rows, width), lambda i: (i, 0))
    half = pl.BlockSpec((rows, width // 2), lambda i: (i, 0))
    whole = pl.BlockSpec(memory_space=pltpu.VMEM)
    hbm = pl.BlockSpec(memory_space=pl.ANY)
    return pl.pallas_call(
        middle_kernel,
        grid=(length // rows,),
        in_specs=[pl.BlockSpec(memory_space=pltpu.SMEM), *[half] * 4, *[hbm] * 8],
        out_specs=[*[whole] * 4, tokens, tokens, hbm, hbm],
        out_shape=[
            *[jax.ShapeDtypeStruct((span, width), BF)] * 4,
            jax.ShapeDtypeStruct((length, width), F32),
            jax.ShapeDtypeStruct((length, width), BF),
            *[jax.ShapeDtypeStruct((2, 4, 2, 24, 2 * width + 1024), BF)] * 2,
        ],
        scratch_shapes=[
            pltpu.VMEM((rows, deep), F32),
            pltpu.VMEM((GROUPS, width // GROUPS + 64, width), F32),
            pltpu.VMEM((width, width), F32),
            pltpu.VMEM((width, width), F32),
            pltpu.VMEM((length, width), BF),
            pltpu.VMEM((width, parts[0].shape[-1]), BF),
            pltpu.VMEM((deep, 256), BF),
            pltpu.VMEM((8, width), F32),
            pltpu.VMEM((1, deep), F32),
            pltpu.VMEM((8, width), F32),
            pltpu.VMEM((2, 2, 4, 2, 24, 2 * width + 1024), BF),
            pltpu.SemaphoreType.DMA((len(cots),)),
            pltpu.SemaphoreType.DMA,
        ],
        compiler_params=pltpu.CompilerParams(vmem_limit_bytes=56 << 20),
        cost_estimate=pl.CostEstimate(flops=40_000_000_000, transcendentals=0, bytes_accessed=16_000_000),
        name="middle",
    )(place, *halves, *mixed, *cots, *parts)


def back_kernel(
    which, place, q_ref, k_ref, v_ref, mix_ref, low_ref, gmix_ref, lse_ref, row_ref, col_ref, *refs,
):
    step = pl.program_id(0)
    length = q_ref.shape[0]
    x_hbm, gres_hbm, pack_hbm, *refs = refs
    before, refs = refs[: 2 * which], refs[2 * which :]
    *ghids, keep_ref, send_ref = refs[:6]
    *refs, dq, dk, dv, x_ref, gres_ref, pack_ref, grads, late, sem = refs[6:]
    half = x_ref.shape[1]
    copies = [
        pltpu.make_async_copy(source, dest, late.at[n])
        for n, (source, dest) in enumerate((
            (x_hbm, x_ref), (gres_hbm.at[:, half * which : half * which + half], gres_ref), (pack_hbm, pack_ref),
            *((old, grads.at[n]) for n, old in enumerate(before)),
        ))
    ]
    outs = [ref.at[:, wide_at(step)] for ref in (dq, dk, dv)]
    qaug, kaug, vaug, gaug, qmine, dq_acc = refs

    @pl.when(step == 0)
    def _():
        for copy in copies:
            copy.start()
        vaug[:, 128:] = jnp.ones((length, 128), BF)
        for head in range(2):
            kaug[head, :, 128:] = col_ref[...]

    rows = 256
    low = lanes((length, 128)) < 64
    lane = lanes((length, 128))
    alive = row_ref[:, 6:7].astype(F32)
    scale = HEAD**-0.5
    zero = jnp.zeros((length, 128), BF)
    q_parts = query_parts(q_ref[...], low)
    k_parts = key_parts(k_ref[...], low)
    grad = gmix_ref[...]
    prod = grad.astype(F32) * (mix_ref[...].astype(F32) + low_ref[...].astype(F32))
    lse = lse_ref[...]
    turned = pltpu.roll(lse, 64, 1)
    vaug[:, :128] = v_ref[...]
    for head in range(2):
        mine = low if head == 0 else ~low
        dot = jnp.sum(jnp.where(mine, prod, 0.0), axis=1, keepdims=True)
        d1, d2, d3 = split3(jnp.broadcast_to(-dot, (length, 128)))
        l1, l2, l3 = split3(-jnp.where(mine, lse, turned))
        qaug[head, :, :128] = q_parts[head]
        qaug[head, :, 128:] = jnp.where(
            lane == 3, l1, jnp.where(lane == 4, l2, jnp.where(lane == 5, l3, row_ref[...]))
        )
        kaug[head, :, :128] = k_parts[head]
        gaug[head, :, :128] = jnp.where(mine, grad, zero)
        gaug[head, :, 128:] = jnp.where(
            lane == 0, d1, jnp.where(lane == 1, d2, jnp.where(lane == 2, d3, zero))
        )
    dq_acc[...] = jnp.zeros_like(dq_acc)
    near = lanes((rows, 128)) < 64
    for head in range(2):
        mine = low if head == 0 else ~low
        qmine[head] = jnp.where(mine, q_ref[...], zero)

    def block(turn_, carry):
        at = pl.ds(pl.multiple_of(turn_ * rows, rows), rows)
        all_probs, all_grads, all_keys = [], [], []
        for head in range(2):
            probs = jnp.exp2(mm(kaug[head, at, :], qaug[head], NT))
            slopes = mm(vaug[at, :], gaug[head], NT)
            all_grads.append((probs * slopes).astype(BF))
            all_probs.append(probs.astype(BF))
            keys = k_ref[at, :]
            none = jnp.zeros_like(keys)
            all_keys.append(jnp.where(near, keys, none) if head == 0 else jnp.where(near, none, keys))
        d_value = mm(all_probs[0], gaug[0, :, :128], NN) + mm(all_probs[1], gaug[1, :, :128], NN)
        d_key = mm(all_grads[0], qmine[0], NN) + mm(all_grads[1], qmine[1], NN)
        dq_acc[...] += mm(jnp.concatenate(all_grads, axis=0), jnp.concatenate(all_keys, axis=0), TN)
        outs[1][at, :] = (d_key * scale).astype(BF)
        outs[2][at, :] = d_value.astype(BF)
        return carry

    lax.fori_loop(0, length // rows, block, 0)
    outs[0][...] = (dq_acc[...] * (alive * scale)).astype(BF)

    @pl.when(step == pl.num_programs(0) - 1)
    def _():
        for copy in copies:
            copy.wait()
        finish_heads(which, place, x_ref, gres_ref, pack_ref, dq, dk, dv, ghids, grads)
        move(((grads.at[0], keep_ref), (grads.at[1], send_ref)), sem)


def finish_heads(which, place, x_ref, gres_ref, pack_ref, dq, dk, dv, ghids, grads):
    length = x_ref.shape[0]
    span = length // 4
    wq, wk, wv = squares(pack_ref[...])
    ghid = (gres_ref[...] + mm(dq[...], wq, NN) + mm(dk[...], wk, NN) + mm(dv[...], wv, NN)).astype(BF)
    for n, ref in enumerate(ghids):
        ref[...] = ghid[span * n : span * n + span, :]
    part = x_ref.shape[1] // 2
    ones = jnp.ones((length, 128), BF)
    sums = []
    for grad in (dq, dk, dv):
        both = mm(grad[...], x_ref[...], TN)
        sums.append((both[:part, :part], both[part:, part:]))
    d_qb, d_vb = mm(dq[...], ones, TN), mm(dv[...], ones, TN)
    extra = jnp.where(lanes(d_qb.shape) == 0, d_qb, d_vb)[:, :64]
    for g in range(2):
        wide = jnp.concatenate([*(each[g] for each in sums), extra[part * g : part * g + part]], axis=1)
        for n in range(8):
            leave_piece(place, grads, 16 * which + 8 * g + n, wide[24 * n : 24 * n + 24])


def attend_backward(which, place, q, k, v, mixed, mixed_low, lse, gmix, row, col, x, gres, pack, before=()):
    length, half = q.shape
    pairs = half // 128
    base = which * pairs
    pair = pl.BlockSpec((length, 128), lambda i: (0, i))
    shifted = pl.BlockSpec((length, 128), lambda i: (0, base + i))
    whole = pl.BlockSpec(memory_space=pltpu.VMEM)
    scratch = [
        pltpu.VMEM((2, length, 256), BF),
        pltpu.VMEM((2, length, 256), BF),
        pltpu.VMEM((length, 256), BF),
        pltpu.VMEM((2, length, 256), BF),
        pltpu.VMEM((2, length, 128), BF),
        pltpu.VMEM((length, 128), F32),
    ]
    scratch += [pltpu.VMEM((length, half), BF)] * 3
    scratch += [pltpu.VMEM((length, half), BF), pltpu.VMEM((length, half), F32), pltpu.VMEM(pack.shape, BF)]
    scratch += [pltpu.VMEM((2, 2, 4, 2, 24, pack.shape[1]), BF), pltpu.SemaphoreType.DMA((5,)), pltpu.SemaphoreType.DMA]
    hbm = pl.BlockSpec(memory_space=pl.ANY)
    return pl.pallas_call(
        functools.partial(back_kernel, which),
        grid=(pairs,),
        in_specs=[pl.BlockSpec(memory_space=pltpu.SMEM), *[pair] * 5, shifted, pair, whole, whole, *[hbm] * (3 + len(before))],
        out_specs=[*[whole] * 4, hbm, hbm],
        out_shape=[
            *[jax.ShapeDtypeStruct((length // 4, half), BF)] * 4,
            *[jax.ShapeDtypeStruct((2, 4, 2, 24, pack.shape[1]), BF)] * 2,
        ],
        scratch_shapes=scratch,
        compiler_params=pltpu.CompilerParams(vmem_limit_bytes=56 << 20),
        cost_estimate=pl.CostEstimate(flops=12_000_000_000 * pairs, transcendentals=0, bytes_accessed=4_000_000),
        name="attend_backward",
    )(place, q, k, v, mixed, mixed_low, gmix, lse, row, col, x, gres, pack, *before)


def turn(v, axis, step, size):
    return lax.ppermute(v, axis, [(i, i ^ step) for i in range(size)])


def pick(v, index):
    return lax.dynamic_index_in_dim(v, index, 0, keepdims=False)


def swap_out(slots):
    return [slots[0]] + [turn(slots[m], "seq", m, 4) for m in range(1, 4)]


def placed(slots, seq):
    result = jnp.zeros((len(slots), *slots[0].shape), slots[0].dtype)
    for m, slot in enumerate(slots):
        result = lax.dynamic_update_index_in_dim(result, slot, seq ^ m, 0)
    return result


def pack_heads(wq, wk, wv, bq, bv):
    gap = jnp.zeros((wq.shape[0], 62), BF)
    return jnp.concatenate([wq, wk, wv, bq[:, None], bv[:, None], gap], axis=1)


def pack_deep(wo, wr, we, be, lines):
    rows, part = wo.shape[0], we.shape[1]
    tall = we.reshape(rows // 96, 4, 96, part)
    side = be.reshape(rows // 96, 4, 96)
    pieces = [wo, wr]
    for j in range(4):
        pieces += [tall[:, j].reshape(rows, part), side[:, j].reshape(rows, 1)]
        extra = lines if j == 0 else []
        pieces += [v[:, None] for v in extra] + [jnp.zeros((rows, 63 - len(extra)), BF)]
    return jnp.concatenate(pieces, axis=1)


def after(value, *others):
    return lax.optimization_barrier((value, others))[0]


def along_z(pack, core):
    piece = pick(pack.reshape(2, pack.shape[0] // 2, pack.shape[1]), core)
    return [piece] + [turn(piece, "fsdp", m, 8) for m in (2, 4, 6)]


def along_x(pieces):
    v = jnp.stack(pieces)
    return jnp.stack([v, turn(v, "fsdp", 1, 8)])


def split_whole(full):
    v = full.reshape(4, 2, 2, 48, full.shape[1]).transpose(2, 1, 0, 3, 4)
    return v[0], v[1]


def add_up(parts):
    result = parts[0].astype(F32)
    for part in parts[1:]:
        result = result + part.astype(F32)
    return result


STEPS = (
    ("seq", ((1, 1),), 4),
    ("fsdp", ((1, 1),), 8),
    ("fsdp", ((1, 2), (2, 4), (3, 6)), 8),
    ("seq", ((1, 2),), 4),
)


def scatter_step(parts, step):
    axis, hops, size = step
    came = [turn(add_up([p[m] for p in parts]).astype(BF), axis, hop, size) for m, hop in hops]
    return [p[0] for p in parts] + came


def open_deep(v, width):
    owners, part = v.shape[0] // 24, width // GROUPS
    tall = v[:, 2 * width :].reshape(owners, 24, 4, 256).transpose(0, 2, 1, 3).reshape(-1, 256)
    lines = [v[:, 2 * width + part + 8 + n] for n in range(6)]
    return v[:, :width], v[:, width : 2 * width], tall[:, :part], tall[:, part], lines


def open_heads(v, width):
    part = width // GROUPS
    return [v[:, part * n : part * n + part] for n in range(3)] + [v[:, 3 * part], v[:, 3 * part + 1]]


def local(mesh_shape, hidden, cotangent, segment_ids, pad_mask, *weights):
    micro, _, span, width = hidden.shape
    half = width // 2
    fsdp, seq = lax.axis_index("fsdp"), lax.axis_index("seq")
    core, y = seq & 1, seq >> 1
    near = mesh_shape["fsdp"] == 8
    (wq, wk, wv, bq, bv, wo, bo, g1, s1, we, be, wr, br, g2, s2) = weights
    lines = [bo, g1, s1, br, g2, s2]

    marks = (segment_ids * 2 + pad_mask)[:, 0].astype(BF)
    marks = jnp.pad(marks[:, None, :], ((0, 0), (0, 7), (0, half - span)))
    first = jnp.concatenate([hidden[:, 0, :, :half], marks], axis=1)
    second = hidden[:, 0, :, half:]

    def swap_in(v):
        return [pick(v, seq)] + [turn(pick(v, seq ^ m), "seq", m, 4) for m in range(1, 4)]

    first = swap_in(first)
    if near:
        place = jnp.stack([core, fsdp, y])
        heads_z = along_z(pack_heads(wq, wk, wv, bq, bv), core)
        heads_own = along_x(heads_z)
        heads = heads_own, turn(heads_own, "seq", 1, 4)
        deep_z = along_z(after(pack_deep(wo, wr, we, be, lines), *heads_z), core)
    else:
        place = jnp.zeros((3,), jnp.int32)
        (wq, wk, wv, bq, bv, wo, bo, g1, s1, we, be, wr, br, g2, s2) = [
            lax.all_gather(w, "fsdp", axis=0, tiled=True) for w in weights
        ]
        heads = split_whole(pack_heads(wq, wk, wv, bq, bv))
        own, other = split_whole(pack_deep(wo, wr, we, be, [bo, g1, s1, br, g2, s2]))
        deep = (own[0], own[1], other[0], other[1])
    second = swap_in(after(second, first))
    ahead = [attend_forward(0, place, after(first, second[1]), span, (), *heads)]
    tables = ahead[0][8:]
    cots = swap_in(after(cotangent[:, 0], second, tables))
    if near:
        own_z = jnp.stack(after(deep_z, second, tables))
        own_x = turn(own_z, "fsdp", 1, 8)
        other_z = turn(own_z, "seq", 1, 4)
    ahead.append(attend_forward(1, place, second, span, tables, *heads))
    if near:
        own_x = after(own_x, ahead[1][7], cots, other_z)
        deep = (own_z, own_x, other_z, turn(own_x, "seq", 1, 4))
    xs, mixed = ([a[n] for a in ahead] for n in (0, 4))
    *out, gres, gmix, d_deep, d_deep_send = middle(place, xs, mixed, cots, deep)
    out_slots = swap_out(out)

    def backward(n, gmix, before):
        xn, q, k, v, mix, mix_low, lse, pack = ahead[n][:8]
        return attend_backward(n, place, q, k, v, mix, mix_low, lse, gmix, *tables, xn, gres, pack, before)

    if near:
        d_deep = [d_deep, turn(d_deep_send, "seq", 1, 4)]
        d_deep, gmix = lax.optimization_barrier((d_deep, gmix))
        d_deep = scatter_step(d_deep, STEPS[1])
    *ghid, keep, send = backward(0, gmix, ())
    halves = [swap_out(ghid)]
    gmix = after(gmix, halves[0][1], d_deep, out_slots)
    if near:
        d_deep = scatter_step(d_deep, STEPS[2])
    *ghid, keep, send = backward(1, gmix, (keep, send))
    halves[0], d_deep, ghid = lax.optimization_barrier((halves[0], d_deep, ghid))
    halves.append([ghid[0], None, turn(ghid[2], "seq", 2, 4), turn(ghid[3], "seq", 3, 4)])
    if near:
        d_heads = [keep, turn(send, "seq", 1, 4)]
        d_deep = scatter_step(d_deep, STEPS[3])
        d_heads = scatter_step(d_heads, STEPS[1])
        d_deep, out_slots, near_part = after((d_deep, out_slots, ghid[1]), d_heads)
        halves[1][1] = turn(near_part, "seq", 1, 4)
        d_heads = scatter_step(d_heads, STEPS[2])
        halves[1] = after(halves[1], d_heads)
        d_heads = scatter_step(d_heads, STEPS[3])
    else:
        halves[1][1] = turn(ghid[1], "seq", 1, 4)
    layer_out = placed(out_slots, seq)[:, None]
    grad_hidden = placed([jnp.concatenate(p, axis=1).astype(F32) for p in zip(*halves)], seq)[:, None]
    if near:
        d_heads, grad_hidden = lax.optimization_barrier((d_heads, grad_hidden))
        dwo, dwr, dwe, dbe, d_lines = open_deep(add_up(d_deep), width)
        dwq, dwk, dwv, dbq, dbv = open_heads(add_up(d_heads), width)
    else:

        def natural(keep, send):
            return jnp.stack([keep, send]).transpose(2, 1, 3, 0, 4, 5).reshape(width, -1).astype(F32)

        dwo, dwr, dwe, dbe, d_lines = open_deep(natural(d_deep, d_deep_send), width)
        dwq, dwk, dwv, dbq, dbv = open_heads(natural(keep, send), width)

        def scatter(v):
            return lax.psum_scatter(v, ("fsdp", "seq"), scatter_dimension=0, tiled=True)

        dwq, dwk, dwv, dbq, dbv, dwo, dwr, dwe, dbe = (scatter(v) for v in (dwq, dwk, dwv, dbq, dbv, dwo, dwr, dwe, dbe))
        d_lines = [scatter(v) for v in d_lines]
    dbo, dg1, ds1, dbr, dg2, ds2 = d_lines
    return (
        layer_out, grad_hidden, dwq, dwk, dwv, dbq, dbv, dwo, dbo, dg1, ds1, dwe, dbe, dwr, dbr, dg2, ds2,
    )


def solution(mesh):
    tokens = P(None, "fsdp", "seq", None)
    marks = P(None, "fsdp", "seq")
    held, line = P("fsdp", None), P("fsdp")
    both, both_line = P(("fsdp", "seq"), None), P(("fsdp", "seq"))
    ranks = (2, 2, 2, 1, 1, 2, 1, 1, 1, 2, 1, 2, 1, 1, 1)
    in_specs = (tokens, tokens, marks, marks, *(held if n == 2 else line for n in ranks))
    out_specs = (tokens, tokens, *(both if n == 2 else both_line for n in ranks))
    return jax.shard_map(functools.partial(local, dict(mesh.shape)), mesh=mesh, in_specs=in_specs, out_specs=out_specs, check_vma=False)
```

```python
import functools

import jax
import jax.numpy as jnp
from jax import lax
from jax.experimental import pallas as pl
from jax.experimental.pallas import tpu as pltpu
from jax.sharding import PartitionSpec as P

GROUPS = 4
HEAD = 64
EPS = 1e-05
LOG2E = 1.4426950408889634
BIG = float(2**30)
BF = jnp.bfloat16
F32 = jnp.float32
NT = (((1,), (1,)), ((), ()))
NN = (((1,), (0,)), ((), ()))
TN = (((0,), (0,)), ((), ()))


def mm(a, b, dims):
    return lax.dot_general(a, b, dims, preferred_element_type=F32)


def split2(v):
    hi = v.astype(BF)
    return hi, (v - hi.astype(F32)).astype(BF)


def split3(v):
    hi = v.astype(BF)
    rest = v - hi.astype(F32)
    mid = rest.astype(BF)
    return hi, mid, (rest - mid.astype(F32)).astype(BF)


def lanes(shape):
    return lax.broadcasted_iota(jnp.int32, shape, 1)


def query_parts(q, low):
    scaled = q.astype(F32) * (LOG2E * HEAD**-0.5)
    hi, lo = split2(scaled)
    hi, lo = hi.astype(F32), lo.astype(F32)
    turned = pltpu.roll(lo, 64, 1)
    return (
        jnp.where(low, hi, turned).astype(BF),
        jnp.where(low, turned, hi).astype(BF),
    )


def key_parts(k, low):
    k = k.astype(F32)
    turned = pltpu.roll(k, 64, 1)
    return (
        jnp.where(low, k, turned).astype(BF),
        jnp.where(low, turned, k).astype(BF),
    )


def square(w):
    part = w.shape[1]
    zero = jnp.zeros((part, part), w.dtype)
    return jnp.concatenate(
        [jnp.concatenate([w[:part], zero], axis=1), jnp.concatenate([zero, w[part:]], axis=1)], axis=0
    )


def squares(pack):
    part = pack.shape[0] // 2
    return [square(pack[:, part * n : part * n + part]) for n in range(3)]


def fetch_parts(place, refs, dest, sem):
    core, fsdp = place[0], place[1]
    copies = []
    for z in range(4):
        for turned in range(2):
            f = (z ^ (fsdp >> 1)) * 2 + ((fsdp & 1) ^ turned)
            for n in range(2):
                source = refs[2 * n + turned].at[z]
                high = source.shape[0]
                rows = pl.ds(pl.multiple_of(f * 2 * high + (core ^ n) * high, 16), high)
                copies.append(pltpu.make_async_copy(source, dest.at[rows, :], sem))
    for copy in copies:
        copy.start()
    return copies


def fetch(place, own, other, dest, sem, shards):
    core, fsdp = place[0], place[1]
    copies = []
    for n, f in enumerate(shards):
        at = ((f & 1) ^ (fsdp & 1), (f >> 1) ^ (fsdp >> 1))
        base = n * 2 * own.shape[2]
        for source, c in ((own, core), (other, 1 - core)):
            rows = pl.ds(pl.multiple_of(base + c * own.shape[2], 16), own.shape[2])
            copies.append(pltpu.make_async_copy(source.at[at[0], at[1]], dest.at[rows, :], sem))
    for copy in copies:
        copy.start()
    return copies


def mask_tables(marks):
    turned = jnp.concatenate([marks, jnp.zeros((4, marks.shape[1]), F32)], axis=0).T
    codes = jnp.concatenate([turned[:, n : n + 1] for n in range(4)], axis=0)
    length = codes.shape[0]
    codes = jnp.broadcast_to(codes, (length, 128))
    lane = lanes((length, 128)).astype(F32)
    real = codes == lane * 2 + 1
    mine = real | (codes == lane * 2)
    lives = jnp.max(jnp.where(real, 1.0, 0.0), axis=0, keepdims=True)
    hot = jnp.where(mine, jnp.broadcast_to(lives, (length, 128)), 0.0)
    alive = jnp.max(hot, axis=1, keepdims=True)
    row = jnp.where(lane == 6, jnp.broadcast_to(alive, (length, 128)), hot)
    col = jnp.where(real, 0.0, jnp.where(lane < 3, -BIG, jnp.where(lane < 6, 1.0, 0.0)))
    return row.astype(BF), col.astype(BF)


def wide_at(pair):
    return pl.ds(pl.multiple_of(128 * pair, 128), 128)


def attend_kernel(which, place, *refs):
    slots, refs = refs[:4], refs[4:]
    own_ref, other_ref, *refs = refs
    if which:
        *given, refs = *refs[:2], refs[2:]
    (
        x_ref, q_ref, k_ref, v_ref, mix_ref, low_ref, lse_ref, pack_ref,
        *tables, queries, keys, values, qaug, kaug, vaug, peak, wide, sem,
    ) = refs
    row_ref, col_ref = given if which else tables
    length = x_ref.shape[0]
    span = length // 4
    pair = pl.program_id(0)

    @pl.when(pair == 0)
    def _():
        copies = fetch(place, own_ref, other_ref, pack_ref, sem, range(4 * which, 4 * which + 4))
        for n, slot in enumerate(slots):
            x_ref[span * n : span * n + span, :] = slot[:span, :]
        if not which:
            marks = jnp.concatenate([slot[span : span + 8, :span].astype(F32)[:1] for slot in slots], axis=0)
            row_ref[...], col_ref[...] = mask_tables(marks)
        vaug[:, 128:] = jnp.ones((length, 128), BF)
        for head in range(2):
            kaug[head, :, 128:] = col_ref[...]
        peak[...] = jnp.zeros_like(peak)
        for copy in copies:
            copy.wait()
        line = pack_ref[:, 512:640].astype(F32).T
        x = x_ref[...]
        alive = row_ref[:, 6:7].astype(F32)
        wq, wk, wv = squares(pack_ref[...])
        queries[...] = ((mm(x, wq, NT) + line[64:65, :]) * alive).astype(BF)
        keys[...] = mm(x, wk, NT).astype(BF)
        values[...] = (mm(x, wv, NT) + line[65:66, :]).astype(BF)
        half = x_ref.shape[1]
        head_of = lax.broadcasted_iota(jnp.int32, (half, 128), 0) // HEAD == lanes((half, 128))
        sizes = []
        for ref in (queries, keys):
            v = ref[...].astype(F32)
            squared = (v * v).astype(BF)
            sizes.append(jnp.max(mm(squared, jnp.where(head_of, 1.0, 0.0).astype(BF), NN), axis=0, keepdims=True))
        limit = (90.0 * HEAD**0.5 / LOG2E) ** 2
        wide[0] = jnp.where(jnp.max(sizes[0] * sizes[1]) > limit, 1, 0)

    cut = wide_at(pair)
    q, k = queries[:, cut], keys[:, cut]
    q_ref[...], k_ref[...], v_ref[...] = q, k, values[:, cut]
    low = lanes((length, 128)) < 64
    q_parts = query_parts(q, low)
    k_parts = key_parts(k, low)
    vaug[:, :128] = values[:, cut]
    for head in range(2):
        qaug[head, :, :128] = q_parts[head]
        qaug[head, :, 128:] = row_ref[...]
        kaug[head, :, :128] = k_parts[head]

        @pl.when(wide[0] == 1)
        def _():
            rows = 128
            lane = lanes((rows, 128))

            def shift(step, carry):
                at = pl.ds(pl.multiple_of(step * rows, rows), rows)
                top = jnp.max(mm(qaug[head, at, :], kaug[head], NT), axis=1, keepdims=True)
                top = jnp.broadcast_to(top, (rows, 128))
                peak[head, at, :] = top
                t1, t2, t3 = split3(-top)
                info = qaug[head, at, 128:]
                qaug[head, at, 128:] = jnp.where(
                    lane == 3, t1, jnp.where(lane == 4, t2, jnp.where(lane == 5, t3, info))
                )
                return carry

            lax.fori_loop(0, length // rows, shift, 0)

    rows = 1024
    left = lanes((rows, 128)) < 64

    def block(step, carry):
        at = pl.ds(pl.multiple_of(step * rows, rows), rows)
        found = []
        for head in range(2):
            powers = jnp.exp2(mm(qaug[head, at, :], kaug[head], NT)).astype(BF)
            both = mm(powers, vaug[...], NN)
            found.append((both[:, :128] / both[:, 128:], peak[head, at, :] + jnp.log2(both[:, 128:])))
        mixed = jnp.where(left, found[0][0], found[1][0])
        mix_ref[at, :], low_ref[at, :] = split2(mixed)
        lse_ref[at, :] = jnp.where(left, found[0][1], found[1][1])
        return carry

    lax.fori_loop(0, length // rows, block, 0)


def attend_forward(which, place, slots, span, tables, own, other):
    half = slots[0].shape[1]
    length = span * len(slots)
    whole = pl.BlockSpec(memory_space=pltpu.VMEM)
    hbm = pl.BlockSpec(memory_space=pl.ANY)
    pair = pl.BlockSpec((length, 128), lambda i: (0, i))
    shapes = [((length, half), BF)] * 6 + [((length, half), F32)]
    shapes += [((half, own.shape[-1]), BF)]
    if not which:
        shapes += [((length, 128), BF)] * 2
    return pl.pallas_call(
        functools.partial(attend_kernel, which),
        grid=(half // 128,),
        in_specs=[pl.BlockSpec(memory_space=pltpu.SMEM), *[whole] * 4, hbm, hbm, *[whole] * len(tables)],
        out_specs=[whole, *[pair] * 6, *[whole] * (len(shapes) - 7)],
        out_shape=[jax.ShapeDtypeStruct(*s) for s in shapes],
        scratch_shapes=[
            *[pltpu.VMEM((length, half), BF)] * 3,
            pltpu.VMEM((2, length, 256), BF),
            pltpu.VMEM((2, length, 256), BF),
            pltpu.VMEM((length, 256), BF),
            pltpu.VMEM((2, length, 128), F32),
            pltpu.SMEM((1,), jnp.int32),
            pltpu.SemaphoreType.DMA,
        ],
        compiler_params=pltpu.CompilerParams(vmem_limit_bytes=56 << 20),
        cost_estimate=pl.CostEstimate(flops=20_000_000_000, transcendentals=0, bytes_accessed=8_000_000),
        name="attend_forward",
    )(place, *slots, own, other, *tables)


def mean(v):
    return jnp.sum(v, axis=1, keepdims=True) * (1.0 / v.shape[1])


def total(v):
    return jnp.sum(v, axis=0, keepdims=True)


def leave_piece(place, grads, owner, piece):
    x, z = place[1] & 1, place[1] >> 1
    at = ((owner % 2) ^ place[0], (owner // 4 % 2) ^ x, (owner // 8) ^ z, (owner // 2 % 2) ^ place[2])
    grads[at] = piece.astype(BF)


def move(pairs, sem):
    copies = [pltpu.make_async_copy(source, dest, sem) for source, dest in pairs]
    for copy in copies:
        copy.start()
    for copy in copies:
        copy.wait()


def gelu_parts(x):
    return 0.5 * lax.erf(x * 0.7071067811865476) + 0.5, jnp.exp2(x * x * (-0.5 * LOG2E)) * 0.3989422804014327


def middle_kernel(
    place, xa_ref, xb_ref, mixa_ref, mixb_ref, cot0, cot1, cot2, cot3, deep0, deep1, deep2, deep3,
    out0, out1, out2, out3, gres_ref, gmix_ref, keep_ref, send_ref,
    slope, dwe_acc, dwo_ref, dwr_ref, cots, pack, we_ref, line_ref, be_ref, sums, grads, sems, sem,
):
    step = pl.program_id(0)
    rows, span = xa_ref.shape[0], cot0.shape[0]
    width = pack.shape[0]
    part = width // GROUPS
    deep = width
    wo_ref = pack.at[:, :width]
    wr_ref = pack.at[:, width : 2 * width]
    bo_ref, g1_ref, s1_ref, br_ref, g2_ref, s2_ref = (line_ref.at[n : n + 1, :] for n in range(1, 7))
    dbo_ref, dg1_ref, ds1_ref, dbr_ref, dg2_ref, ds2_ref = (sums.at[n : n + 1, :] for n in range(6))

    @pl.when(step == 0)
    def _():
        for n, ref in enumerate((cot0, cot1, cot2, cot3)):
            pltpu.make_async_copy(ref, cots.at[span * n : span * n + span, :], sems.at[n]).start()
        copies = fetch_parts(place, (deep0, deep1, deep2, deep3), pack, sem)
        for ref in (dwo_ref, dwr_ref, dwe_acc, sums):
            ref[...] = jnp.zeros_like(ref)
        for copy in copies:
            copy.wait()
        line_ref[...] = pack[:, 2 * width + 128 : 2 * width + 256].astype(F32).T[64:72]
        for f in range(8):
            for j in range(4):
                we_ref[384 * f + 96 * j : 384 * f + 96 * j + 96, :] = pack[
                    96 * f : 96 * f + 96, 2 * width + 256 * j : 2 * width + 256 * j + 256
                ]
        for g in range(GROUPS):
            be_ref[:, deep * g : deep * g + deep] = we_ref[deep * g : deep * g + deep, 128:].astype(F32).T[64:65]

    for n in range(rows // span):
        pltpu.make_async_copy(cot0, cots.at[:span, :], sems.at[step * (rows // span) + n]).wait()
    few = rows // 2
    ones = jnp.ones((few, 64), BF)
    outs = []

    def block(n):
        at = slice(few * n, few * n + few)
        mixed = jnp.concatenate([mixa_ref[at, :], mixb_ref[at, :]], axis=1)
        rows_in = jnp.concatenate([xa_ref[at, :], xb_ref[at, :]], axis=1)
        residual = rows_in.astype(F32) + mm(mixed, wo_ref[...], NT) + bo_ref[...]
        yield
        centred = residual - mean(residual)
        rate1 = lax.rsqrt(mean(centred * centred) + EPS)
        hat1 = centred * rate1
        normed = hat1 * g1_ref[...] + s1_ref[...]
        normed_low = normed.astype(BF)
        yield
        acts, branches = [], []
        for g in range(GROUPS):
            piece = normed_low[:, part * g : part * g + part]
            tall = slice(deep * g, deep * g + deep)
            pre = mm(piece, we_ref[tall, :part], NT) + be_ref[:, tall]
            upper, density = gelu_parts(pre)
            acts.append((pre * upper).astype(BF))
            slope[at, tall] = upper + pre * density
            branches.append(mm(acts[g], wr_ref[part * g : part * g + part, :], NT))
        second = normed + jnp.concatenate(branches, axis=1) + br_ref[...]
        yield
        centred = second - mean(second)
        rate2 = lax.rsqrt(mean(centred * centred) + EPS)
        hat2 = centred * rate2
        outs.append((hat2 * g2_ref[...] + s2_ref[...]).astype(BF))
        cot = cots[pl.ds(pl.multiple_of(step * rows + few * n, few), few), :].astype(F32)
        dg2_ref[...] += total(cot * hat2)
        ds2_ref[...] += total(cot)
        e = cot * g2_ref[...]
        grad_second = rate2 * (e - mean(e) - hat2 * mean(e * hat2))
        grad_branch = grad_second.astype(BF)
        dbr_ref[...] += total(grad_branch.astype(F32))
        yield
        backs = []
        for g in range(GROUPS):
            narrow = slice(part * g, part * g + part)
            tall = slice(deep * g, deep * g + deep)
            piece = grad_branch[:, narrow]
            dwr_ref[narrow, :] += mm(piece, acts[g], TN)
            grad_pre = mm(piece, wr_ref[narrow, :], NN) * slope[at, tall]
            grad_pre_low = grad_pre.astype(BF)
            dwe_acc[g] += mm(jnp.concatenate([normed_low[:, narrow], ones], axis=1), grad_pre_low, TN)
            backs.append(mm(grad_pre_low, we_ref[tall, :part], NN))
        grad_normed = grad_second + jnp.concatenate(backs, axis=1)
        yield
        dg1_ref[...] += total(grad_normed * hat1)
        ds1_ref[...] += total(grad_normed)
        e = grad_normed * g1_ref[...]
        grad_residual = rate1 * (e - mean(e) - hat1 * mean(e * hat1))
        gres_ref[at, :] = grad_residual
        grad_projected = grad_residual.astype(BF)
        dbo_ref[...] += total(grad_projected.astype(F32))
        yield
        dwo_ref[...] += mm(grad_projected, mixed, TN)
        gmix_ref[at, :] = mm(grad_projected, wo_ref[...], NN).astype(BF)

    halves = [block(0), block(1)]
    for _ in range(7):
        for half in halves:
            next(half, None)
    out = jnp.concatenate(outs, axis=0)
    for n, ref in enumerate((out0, out1, out2, out3)):

        @pl.when(step == n * span // rows)
        def _():
            ref[...] = out[n * span % rows : n * span % rows + span, :]

    @pl.when(step == pl.num_programs(0) - 1)
    def _():
        low = jnp.zeros((72, width), F32)
        side = jnp.concatenate([low, sums[...], jnp.zeros((48, width), F32)], axis=0).T
        lane = lanes((24, 128))
        for g in range(GROUPS):
            tall = dwe_acc[g].T
            for n in range(8):
                owner = 8 * g + n
                few_rows = slice(24 * owner, 24 * owner + 24)
                turns = [tall[96 * n + 24 * j : 96 * n + 24 * j + 24] for j in range(4)]
                last = jnp.where(lane < 72, turns[0][:, 128:], side[few_rows])
                piece = jnp.concatenate(
                    [dwo_ref[few_rows, :], dwr_ref[few_rows, :], turns[0][:, :128], last, *turns[1:]], axis=1
                )
                leave_piece(place, grads, owner, piece)
        move(((grads.at[0], keep_ref), (grads.at[1], send_ref)), sem)


def middle(place, halves, mixed, cots, parts):
    span, width = cots[0].shape
    length = span * len(cots)
    rows = 2 * span
    deep = width * GROUPS
    tokens = pl.BlockSpec((rows, width), lambda i: (i, 0))
    half = pl.BlockSpec((rows, width // 2), lambda i: (i, 0))
    whole = pl.BlockSpec(memory_space=pltpu.VMEM)
    hbm = pl.BlockSpec(memory_space=pl.ANY)
    return pl.pallas_call(
        middle_kernel,
        grid=(length // rows,),
        in_specs=[pl.BlockSpec(memory_space=pltpu.SMEM), *[half] * 4, *[hbm] * 8],
        out_specs=[*[whole] * 4, tokens, tokens, hbm, hbm],
        out_shape=[
            *[jax.ShapeDtypeStruct((span, width), BF)] * 4,
            jax.ShapeDtypeStruct((length, width), F32),
            jax.ShapeDtypeStruct((length, width), BF),
            *[jax.ShapeDtypeStruct((2, 4, 2, 24, 2 * width + 1024), BF)] * 2,
        ],
        scratch_shapes=[
            pltpu.VMEM((rows, deep), F32),
            pltpu.VMEM((GROUPS, width // GROUPS + 64, width), F32),
            pltpu.VMEM((width, width), F32),
            pltpu.VMEM((width, width), F32),
            pltpu.VMEM((length, width), BF),
            pltpu.VMEM((width, parts[0].shape[-1]), BF),
            pltpu.VMEM((deep, 256), BF),
            pltpu.VMEM((8, width), F32),
            pltpu.VMEM((1, deep), F32),
            pltpu.VMEM((8, width), F32),
            pltpu.VMEM((2, 2, 4, 2, 24, 2 * width + 1024), BF),
            pltpu.SemaphoreType.DMA((len(cots),)),
            pltpu.SemaphoreType.DMA,
        ],
        compiler_params=pltpu.CompilerParams(vmem_limit_bytes=56 << 20),
        cost_estimate=pl.CostEstimate(flops=40_000_000_000, transcendentals=0, bytes_accessed=16_000_000),
        name="middle",
    )(place, *halves, *mixed, *cots, *parts)


def back_kernel(
    which, place, q_ref, k_ref, v_ref, mix_ref, low_ref, gmix_ref, lse_ref, row_ref, col_ref, *refs,
):
    step = pl.program_id(0)
    length = q_ref.shape[0]
    x_hbm, gres_hbm, pack_hbm, *refs = refs
    before, refs = refs[: 2 * which], refs[2 * which :]
    *ghids, keep_ref, send_ref = refs[:6]
    *refs, dq, dk, dv, x_ref, gres_ref, pack_ref, grads, late, sem = refs[6:]
    half = x_ref.shape[1]
    copies = [
        pltpu.make_async_copy(source, dest, late.at[n])
        for n, (source, dest) in enumerate((
            (x_hbm, x_ref), (gres_hbm.at[:, half * which : half * which + half], gres_ref), (pack_hbm, pack_ref),
            *((old, grads.at[n]) for n, old in enumerate(before)),
        ))
    ]
    outs = [ref.at[:, wide_at(step)] for ref in (dq, dk, dv)]
    qaug, kaug, vaug, gaug, qmine, dq_acc = refs

    @pl.when(step == 0)
    def _():
        for copy in copies:
            copy.start()
        vaug[:, 128:] = jnp.ones((length, 128), BF)
        for head in range(2):
            kaug[head, :, 128:] = col_ref[...]

    rows = 512
    low = lanes((length, 128)) < 64
    lane = lanes((length, 128))
    alive = row_ref[:, 6:7].astype(F32)
    scale = HEAD**-0.5
    zero = jnp.zeros((length, 128), BF)
    q_parts = query_parts(q_ref[...], low)
    k_parts = key_parts(k_ref[...], low)
    grad = gmix_ref[...]
    prod = grad.astype(F32) * (mix_ref[...].astype(F32) + low_ref[...].astype(F32))
    lse = lse_ref[...]
    turned = pltpu.roll(lse, 64, 1)
    vaug[:, :128] = v_ref[...]
    for head in range(2):
        mine = low if head == 0 else ~low
        dot = jnp.sum(jnp.where(mine, prod, 0.0), axis=1, keepdims=True)
        d1, d2, d3 = split3(jnp.broadcast_to(-dot, (length, 128)))
        l1, l2, l3 = split3(-jnp.where(mine, lse, turned))
        qaug[head, :, :128] = q_parts[head]
        qaug[head, :, 128:] = jnp.where(
            lane == 3, l1, jnp.where(lane == 4, l2, jnp.where(lane == 5, l3, row_ref[...]))
        )
        kaug[head, :, :128] = k_parts[head]
        gaug[head, :, :128] = jnp.where(mine, grad, zero)
        gaug[head, :, 128:] = jnp.where(
            lane == 0, d1, jnp.where(lane == 1, d2, jnp.where(lane == 2, d3, zero))
        )
    dq_acc[...] = jnp.zeros_like(dq_acc)
    near = lanes((rows, 128)) < 64
    for head in range(2):
        mine = low if head == 0 else ~low
        qmine[head] = jnp.where(mine, q_ref[...], zero)

    def block(turn_, carry):
        at = pl.ds(pl.multiple_of(turn_ * rows, rows), rows)
        all_probs, all_grads, all_keys = [], [], []
        for head in range(2):
            probs = jnp.exp2(mm(kaug[head, at, :], qaug[head], NT))
            slopes = mm(vaug[at, :], gaug[head], NT)
            all_grads.append((probs * slopes).astype(BF))
            all_probs.append(probs.astype(BF))
            keys = k_ref[at, :]
            none = jnp.zeros_like(keys)
            all_keys.append(jnp.where(near, keys, none) if head == 0 else jnp.where(near, none, keys))
        d_value = mm(all_probs[0], gaug[0, :, :128], NN) + mm(all_probs[1], gaug[1, :, :128], NN)
        d_key = mm(all_grads[0], qmine[0], NN) + mm(all_grads[1], qmine[1], NN)
        dq_acc[...] += mm(jnp.concatenate(all_grads, axis=0), jnp.concatenate(all_keys, axis=0), TN)
        outs[1][at, :] = (d_key * scale).astype(BF)
        outs[2][at, :] = d_value.astype(BF)
        return carry

    lax.fori_loop(0, length // rows, block, 0)
    outs[0][...] = (dq_acc[...] * (alive * scale)).astype(BF)

    @pl.when(step == pl.num_programs(0) - 1)
    def _():
        for copy in copies:
            copy.wait()
        finish_heads(which, place, x_ref, gres_ref, pack_ref, dq, dk, dv, ghids, grads)
        move(((grads.at[0], keep_ref), (grads.at[1], send_ref)), sem)


def finish_heads(which, place, x_ref, gres_ref, pack_ref, dq, dk, dv, ghids, grads):
    length = x_ref.shape[0]
    span = length // 4
    wq, wk, wv = squares(pack_ref[...])
    ghid = (gres_ref[...] + mm(dq[...], wq, NN) + mm(dk[...], wk, NN) + mm(dv[...], wv, NN)).astype(BF)
    for n, ref in enumerate(ghids):
        ref[...] = ghid[span * n : span * n + span, :]
    part = x_ref.shape[1] // 2
    ones = jnp.ones((length, 128), BF)
    sums = []
    for grad in (dq, dk, dv):
        both = mm(grad[...], x_ref[...], TN)
        sums.append((both[:part, :part], both[part:, part:]))
    d_qb, d_vb = mm(dq[...], ones, TN), mm(dv[...], ones, TN)
    extra = jnp.where(lanes(d_qb.shape) == 0, d_qb, d_vb)[:, :64]
    for g in range(2):
        wide = jnp.concatenate([*(each[g] for each in sums), extra[part * g : part * g + part]], axis=1)
        for n in range(8):
            leave_piece(place, grads, 16 * which + 8 * g + n, wide[24 * n : 24 * n + 24])


def attend_backward(which, place, q, k, v, mixed, mixed_low, lse, gmix, row, col, x, gres, pack, before=()):
    length, half = q.shape
    pairs = half // 128
    base = which * pairs
    pair = pl.BlockSpec((length, 128), lambda i: (0, i))
    shifted = pl.BlockSpec((length, 128), lambda i: (0, base + i))
    whole = pl.BlockSpec(memory_space=pltpu.VMEM)
    scratch = [
        pltpu.VMEM((2, length, 256), BF),
        pltpu.VMEM((2, length, 256), BF),
        pltpu.VMEM((length, 256), BF),
        pltpu.VMEM((2, length, 256), BF),
        pltpu.VMEM((2, length, 128), BF),
        pltpu.VMEM((length, 128), F32),
    ]
    scratch += [pltpu.VMEM((length, half), BF)] * 3
    scratch += [pltpu.VMEM((length, half), BF), pltpu.VMEM((length, half), F32), pltpu.VMEM(pack.shape, BF)]
    scratch += [pltpu.VMEM((2, 2, 4, 2, 24, pack.shape[1]), BF), pltpu.SemaphoreType.DMA((5,)), pltpu.SemaphoreType.DMA]
    hbm = pl.BlockSpec(memory_space=pl.ANY)
    return pl.pallas_call(
        functools.partial(back_kernel, which),
        grid=(pairs,),
        in_specs=[pl.BlockSpec(memory_space=pltpu.SMEM), *[pair] * 5, shifted, pair, whole, whole, *[hbm] * (3 + len(before))],
        out_specs=[*[whole] * 4, hbm, hbm],
        out_shape=[
            *[jax.ShapeDtypeStruct((length // 4, half), BF)] * 4,
            *[jax.ShapeDtypeStruct((2, 4, 2, 24, pack.shape[1]), BF)] * 2,
        ],
        scratch_shapes=scratch,
        compiler_params=pltpu.CompilerParams(vmem_limit_bytes=56 << 20),
        cost_estimate=pl.CostEstimate(flops=12_000_000_000 * pairs, transcendentals=0, bytes_accessed=4_000_000),
        name="attend_backward",
    )(place, q, k, v, mixed, mixed_low, gmix, lse, row, col, x, gres, pack, *before)


def turn(v, axis, step, size):
    return lax.ppermute(v, axis, [(i, i ^ step) for i in range(size)])


def pick(v, index):
    return lax.dynamic_index_in_dim(v, index, 0, keepdims=False)


def swap_out(slots):
    return [slots[0]] + [turn(slots[m], "seq", m, 4) for m in range(1, 4)]


def placed(slots, seq):
    result = jnp.zeros((len(slots), *slots[0].shape), slots[0].dtype)
    for m, slot in enumerate(slots):
        result = lax.dynamic_update_index_in_dim(result, slot, seq ^ m, 0)
    return result


def pack_heads(wq, wk, wv, bq, bv):
    gap = jnp.zeros((wq.shape[0], 62), BF)
    return jnp.concatenate([wq, wk, wv, bq[:, None], bv[:, None], gap], axis=1)


def pack_deep(wo, wr, we, be, lines):
    rows, part = wo.shape[0], we.shape[1]
    tall = we.reshape(rows // 96, 4, 96, part)
    side = be.reshape(rows // 96, 4, 96)
    pieces = [wo, wr]
    for j in range(4):
        pieces += [tall[:, j].reshape(rows, part), side[:, j].reshape(rows, 1)]
        extra = lines if j == 0 else []
        pieces += [v[:, None] for v in extra] + [jnp.zeros((rows, 63 - len(extra)), BF)]
    return jnp.concatenate(pieces, axis=1)


def after(value, *others):
    return lax.optimization_barrier((value, others))[0]


def along_z(pack, core):
    piece = pick(pack.reshape(2, pack.shape[0] // 2, pack.shape[1]), core)
    return [piece] + [turn(piece, "fsdp", m, 8) for m in (2, 4, 6)]


def along_x(pieces):
    v = jnp.stack(pieces)
    return jnp.stack([v, turn(v, "fsdp", 1, 8)])


def split_whole(full):
    v = full.reshape(4, 2, 2, 48, full.shape[1]).transpose(2, 1, 0, 3, 4)
    return v[0], v[1]


def add_up(parts):
    result = parts[0].astype(F32)
    for part in parts[1:]:
        result = result + part.astype(F32)
    return result


STEPS = (
    ("seq", ((1, 1),), 4),
    ("fsdp", ((1, 1),), 8),
    ("fsdp", ((1, 2), (2, 4), (3, 6)), 8),
    ("seq", ((1, 2),), 4),
)


def scatter_step(parts, step):
    axis, hops, size = step
    came = [turn(add_up([p[m] for p in parts]).astype(BF), axis, hop, size) for m, hop in hops]
    return [p[0] for p in parts] + came


def open_deep(v, width):
    owners, part = v.shape[0] // 24, width // GROUPS
    tall = v[:, 2 * width :].reshape(owners, 24, 4, 256).transpose(0, 2, 1, 3).reshape(-1, 256)
    lines = [v[:, 2 * width + part + 8 + n] for n in range(6)]
    return v[:, :width], v[:, width : 2 * width], tall[:, :part], tall[:, part], lines


def open_heads(v, width):
    part = width // GROUPS
    return [v[:, part * n : part * n + part] for n in range(3)] + [v[:, 3 * part], v[:, 3 * part + 1]]


def local(mesh_shape, hidden, cotangent, segment_ids, pad_mask, *weights):
    micro, _, span, width = hidden.shape
    half = width // 2
    fsdp, seq = lax.axis_index("fsdp"), lax.axis_index("seq")
    core, y = seq & 1, seq >> 1
    near = mesh_shape["fsdp"] == 8
    (wq, wk, wv, bq, bv, wo, bo, g1, s1, we, be, wr, br, g2, s2) = weights
    lines = [bo, g1, s1, br, g2, s2]

    marks = (segment_ids * 2 + pad_mask)[:, 0].astype(BF)
    marks = jnp.pad(marks[:, None, :], ((0, 0), (0, 7), (0, half - span)))
    first = jnp.concatenate([hidden[:, 0, :, :half], marks], axis=1)
    second = hidden[:, 0, :, half:]

    def swap_in(v):
        return [pick(v, seq)] + [turn(pick(v, seq ^ m), "seq", m, 4) for m in range(1, 4)]

    first = swap_in(first)
    if near:
        place = jnp.stack([core, fsdp, y])
        heads_z = along_z(pack_heads(wq, wk, wv, bq, bv), core)
        heads_own = along_x(heads_z)
        heads = heads_own, turn(heads_own, "seq", 1, 4)
        deep_z = along_z(after(pack_deep(wo, wr, we, be, lines), *heads_z), core)
    else:
        place = jnp.zeros((3,), jnp.int32)
        (wq, wk, wv, bq, bv, wo, bo, g1, s1, we, be, wr, br, g2, s2) = [
            lax.all_gather(w, "fsdp", axis=0, tiled=True) for w in weights
        ]
        heads = split_whole(pack_heads(wq, wk, wv, bq, bv))
        own, other = split_whole(pack_deep(wo, wr, we, be, [bo, g1, s1, br, g2, s2]))
        deep = (own[0], own[1], other[0], other[1])
    second = swap_in(after(second, first))
    ahead = [attend_forward(0, place, after(first, second[1]), span, (), *heads)]
    tables = ahead[0][8:]
    cots = swap_in(after(cotangent[:, 0], second, tables))
    if near:
        own_z = jnp.stack(after(deep_z, second, tables))
        own_x = turn(own_z, "fsdp", 1, 8)
        other_z = turn(own_z, "seq", 1, 4)
    ahead.append(attend_forward(1, place, second, span, tables, *heads))
    if near:
        own_x = after(own_x, ahead[1][7], cots, other_z)
        deep = (own_z, own_x, other_z, turn(own_x, "seq", 1, 4))
    xs, mixed = ([a[n] for a in ahead] for n in (0, 4))
    *out, gres, gmix, d_deep, d_deep_send = middle(place, xs, mixed, cots, deep)
    out_slots = swap_out(out)

    def backward(n, gmix, before):
        xn, q, k, v, mix, mix_low, lse, pack = ahead[n][:8]
        return attend_backward(n, place, q, k, v, mix, mix_low, lse, gmix, *tables, xn, gres, pack, before)

    if near:
        d_deep = [d_deep, turn(d_deep_send, "seq", 1, 4)]
        d_deep, gmix = lax.optimization_barrier((d_deep, gmix))
        d_deep = scatter_step(d_deep, STEPS[1])
    *ghid, keep, send = backward(0, gmix, ())
    halves = [swap_out(ghid)]
    gmix = after(gmix, halves[0][1], d_deep, out_slots)
    if near:
        d_deep = scatter_step(d_deep, STEPS[2])
    *ghid, keep, send = backward(1, gmix, (keep, send))
    halves[0], d_deep, ghid = lax.optimization_barrier((halves[0], d_deep, ghid))
    halves.append([ghid[0], None, turn(ghid[2], "seq", 2, 4), turn(ghid[3], "seq", 3, 4)])
    if near:
        d_heads = [keep, turn(send, "seq", 1, 4)]
        d_deep = scatter_step(d_deep, STEPS[3])
        d_heads = scatter_step(d_heads, STEPS[1])
        d_deep, out_slots, near_part = after((d_deep, out_slots, ghid[1]), d_heads)
        halves[1][1] = turn(near_part, "seq", 1, 4)
        d_heads = scatter_step(d_heads, STEPS[2])
        halves[1] = after(halves[1], d_heads)
        d_heads = scatter_step(d_heads, STEPS[3])
    else:
        halves[1][1] = turn(ghid[1], "seq", 1, 4)
    layer_out = placed(out_slots, seq)[:, None]
    grad_hidden = placed([jnp.concatenate(p, axis=1).astype(F32) for p in zip(*halves)], seq)[:, None]
    if near:
        d_heads, grad_hidden = lax.optimization_barrier((d_heads, grad_hidden))
        dwo, dwr, dwe, dbe, d_lines = open_deep(add_up(d_deep), width)
        dwq, dwk, dwv, dbq, dbv = open_heads(add_up(d_heads), width)
    else:

        def natural(keep, send):
            return jnp.stack([keep, send]).transpose(2, 1, 3, 0, 4, 5).reshape(width, -1).astype(F32)

        dwo, dwr, dwe, dbe, d_lines = open_deep(natural(d_deep, d_deep_send), width)
        dwq, dwk, dwv, dbq, dbv = open_heads(natural(keep, send), width)

        def scatter(v):
            return lax.psum_scatter(v, ("fsdp", "seq"), scatter_dimension=0, tiled=True)

        dwq, dwk, dwv, dbq, dbv, dwo, dwr, dwe, dbe = (scatter(v) for v in (dwq, dwk, dwv, dbq, dbv, dwo, dwr, dwe, dbe))
        d_lines = [scatter(v) for v in d_lines]
    dbo, dg1, ds1, dbr, dg2, ds2 = d_lines
    return (
        layer_out, grad_hidden, dwq, dwk, dwv, dbq, dbv, dwo, dbo, dg1, ds1, dwe, dbe, dwr, dbr, dg2, ds2,
    )


def solution(mesh):
    tokens = P(None, "fsdp", "seq", None)
    marks = P(None, "fsdp", "seq")
    held, line = P("fsdp", None), P("fsdp")
    both, both_line = P(("fsdp", "seq"), None), P(("fsdp", "seq"))
    ranks = (2, 2, 2, 1, 1, 2, 1, 1, 1, 2, 1, 2, 1, 1, 1)
    in_specs = (tokens, tokens, marks, marks, *(held if n == 2 else line for n in ranks))
    out_specs = (tokens, tokens, *(both if n == 2 else both_line for n in ranks))
    return jax.shard_map(functools.partial(local, dict(mesh.shape)), mesh=mesh, in_specs=in_specs, out_specs=out_specs, check_vma=False)
```
